32 devices in a mesh: dp: 4 (over y, x), expert: 8 (over z, core).
Axes of the slice: x: 2, y: 2, z: 4, core: 2. Of those that a mesh axis runs over, the one named last changes fastest.
Arguments:
- tokens: bfloat16 [4096, 2048], P(('dp', 'expert')), may hold values from -6 to 6
- out_grad: bfloat16 [4096, 2048], P(('dp', 'expert')), may hold values from -6 to 6
- routes: int32 [4096, 4], P(('dp', 'expert')), may hold values from 0 to 7, all different within a row; in each aligned block of 128 rows (0 to 127, 128 to 255, ...) at most 72 rows name the same one
- gate_values: float32 [4096, 4], P(('dp', 'expert')), may hold values from 0.05 to 1
- w_gate: bfloat16 [8, 2048, 768], P('expert', 'dp'), may hold values from -0.125 to 0.125
- w_up: bfloat16 [8, 2048, 768], P('expert', 'dp'), may hold values from -0.125 to 0.125
- w_down: bfloat16 [8, 768, 2048], P('expert', None, 'dp'), may hold values from -0.21875 to 0.21875
Outputs:
- input_grad: bfloat16 [4096, 2048], P(('dp', 'expert'))
- gate_grad: bfloat16 [8, 2048, 768], P('expert', 'dp')
- up_grad: bfloat16 [8, 2048, 768], P('expert', 'dp')
- down_grad: bfloat16 [8, 768, 2048], P('expert', None, 'dp')
The draws below stay inside these ranges and needn't reach their ends.
Inputs may be any that keep to these rules, and one draw needn't show every extreme that they name: `routes`: each token names 4 different experts. Among the 128 tokens of one device (aligned blocks of 128 tokens) no expert is named by more than 72 tokens, and in every draw some device names some expert exactly 72 times.
All inputs are finite; a program needn't handle non-finite values.
Results may differ from the reference program's by a relative error of at most 0.0095.
Values may be sent and summed in bfloat16 or wider, within the bound.
No kernel may reach another device: no remote copies, remote signals or barrier semaphores. Data moves between devices by JAX's collectives and lax.ppermute only.
A program may use at most 128 MiB of HBM per device.

```python
import math
import jax
import jax.numpy as jnp
import numpy as np
from jax import lax

D = 2048
FF = 768
TOP = 4
TOK_DEV = 128
EXPERTS = 8
CAP = 72
SLOTS = 576
TOKENS = 4096
N_DP = 4
N_EXPERT = 8


def block_scale(stream_key, extent, cuts, low, top_value):
    def one(position, blocks):
        draws = jax.random.uniform(jax.random.fold_in(jax.random.fold_in(stream_key, 6), position), (blocks,), jnp.float32, low / len(cuts), top_value / len(cuts))
        return jnp.repeat(jnp.exp(draws), extent[position] // blocks).reshape((-1,) + (1,) * (len(extent) - position - 1))

    factor_of = one(*cuts[0])
    for cut in cuts[1:]:
        factor_of = factor_of * one(*cut)
    return factor_of


def deal_out(key, own, number, rows, count, top, limit, slope):
    sequence = jax.random.permutation(key, count)
    heavy_load, usual = shares(count, rows * top, limit, slope, True), shares(count, rows * top, limit, slope, False)
    places = jnp.arange(count)

    def named(lengths, offset_by):
        used = int((lengths > 0).sum())
        fixed = max(1, used // 4)
        passed = fixed + (places - fixed + offset_by * (used - fixed)) % max(1, count - fixed)
        return jnp.zeros((count,), jnp.int32).at[sequence[jnp.where(places < fixed, places, passed)]].set(jnp.asarray(lengths, jnp.int32))

    lengths = jnp.where(number % 4 == 0, named(heavy_load, number // 4), named(usual, number - number // 4 - 1))
    mixed = jax.random.permutation(jax.random.fold_in(own, 3), count)
    donor, receiver = mixed[0:count // 2 * 2:2], mixed[1:count // 2 * 2:2]
    slack = jnp.minimum(lengths[donor] - 1, limit - lengths[receiver]) // 2
    slack = jnp.where((donor == sequence[0]) | (receiver == sequence[0]) | (lengths[receiver] == 0), 0, jnp.maximum(slack, 0))
    passed = jax.random.randint(jax.random.fold_in(own, 4), (count // 2,), 0, 1 << 20) % (slack + 1)
    lengths = lengths.at[donor].add(-passed).at[receiver].add(passed)
    members = jnp.searchsorted(jnp.cumsum(lengths), jnp.arange(rows * top), side="right").astype(jnp.int32)
    listing = members.reshape(top, rows).T
    listing = listing[jax.random.permutation(jax.random.fold_in(own, 1), rows)]
    offset_by = jax.random.randint(jax.random.fold_in(own, 2), (rows, 1), 0, top)
    return jnp.take_along_axis(listing, (jnp.arange(top)[None, :] + offset_by) % top, axis=1)


def shares(amount, total, most, lean, full):
    loads = [(1 << 20) // math.isqrt(standing ** lean) + 1 for standing in range(1, amount + 1)]
    largest = most if full else min(most, max(-(-total // amount), total * loads[0] // sum(loads)))
    least = 1 if total - largest >= amount - 1 else 0
    holding, spare = [largest] + [least] * (amount - 1), total - largest - least * (amount - 1)
    while spare > 0:
        candidates = [i for i in range(1, amount) if holding[i] < largest] or [i for i in range(1, amount) if holding[i] < most]
        whole, left = sum([loads[i] for i in candidates]), spare
        for i in candidates:
            more = min(most - holding[i], max(1, left * loads[i] // whole), spare)
            holding[i] = holding[i] + more
            spare = spare - more
    return np.array(holding)


def noise(own_key, dims, scale, bound, cuts=(), kind=jnp.bfloat16):
    result = jax.random.normal(own_key, dims, jnp.float32) * scale
    if len(cuts) > 0:
        result = block_scale(own_key, dims, cuts, -0.22, 0.18) * result
    return jnp.clip(result, min=-bound, max=bound).astype(kind)


def setup_inputs(seed: int = 0) -> dict:
    key_list = jax.random.split(jax.random.key(seed), 8)
    tokens = noise(key_list[0], (TOKENS, D), 1.0, 6.0, ((0, 32),))
    out_grad = noise(key_list[1], (TOKENS, D), 1.0, 6.0, ((0, 32),))
    routes_keys = jax.random.split(jax.random.fold_in(key_list[2], 1), TOKENS // TOK_DEV)
    routes_turns = jax.random.permutation(jax.random.fold_in(key_list[2], 3), TOKENS // TOK_DEV)
    routes = jax.vmap(lambda own, number: deal_out(jax.random.fold_in(key_list[2], 2), own, number, TOK_DEV, EXPERTS, TOP, CAP, 2))(routes_keys, routes_turns).reshape((TOKENS, TOP))
    gate_values = jnp.clip(jnp.exp(math.log(1.0) - 2.9957323 * jax.random.uniform(key_list[3], (TOKENS, TOP), jnp.float32) ** block_scale(key_list[3], (TOKENS, TOP), ((0, 32),), -0.2, 0.2)), 0.05, 1.0)
    w_gate = noise(key_list[4], (EXPERTS, D, FF), D ** -0.5, 0.125, ((0, 8), (1, 4)))
    w_up = noise(key_list[5], (EXPERTS, D, FF), D ** -0.5, 0.125, ((0, 8), (1, 4)))
    w_down = noise(key_list[6], (EXPERTS, FF, D), FF ** -0.5, 0.21875, ((0, 8), (2, 4)))
    return {"tokens": tokens, "out_grad": out_grad, "routes": routes, "gate_values": gate_values, "w_gate": w_gate, "w_up": w_up, "w_down": w_down}


def reference(tokens, out_grad, routes, gate_values, w_gate, w_up, w_down):
    pair_count = tokens.shape[0] * TOP
    expert_of = routes.reshape(-1).astype(jnp.int32)
    pair_index = jnp.arange(pair_count, dtype=jnp.int32)
    group_of = (pair_index // TOP) // (N_EXPERT * TOK_DEV)
    sort_keys = expert_of * N_DP + group_of
    order = jnp.argsort(sort_keys, stable=True).astype(jnp.int32)
    counts = jax.ops.segment_sum(jnp.ones_like(sort_keys), sort_keys, num_segments=EXPERTS * N_DP).astype(jnp.int32)
    starts = (jnp.cumsum(counts) - counts).astype(jnp.int32)
    padded = jnp.concatenate([order, jnp.zeros((SLOTS,), jnp.int32)])
    flat_gates = gate_values.reshape(-1)
    slot_range = jnp.arange(SLOTS, dtype=jnp.int32)

    def rounded_sum(partial_value):
        return lax.optimization_barrier(partial_value.astype(jnp.bfloat16)).astype(jnp.float32).sum(axis=0).astype(jnp.bfloat16)

    def per_expert(grad_sum, expert):
        first = lax.dynamic_slice_in_dim(starts, expert * N_DP, N_DP)
        number = lax.dynamic_slice_in_dim(counts, expert * N_DP, N_DP)
        filled = slot_range[None, :] < number[:, None]
        source = jnp.where(filled, padded[first[:, None] + slot_range[None, :]], 0).astype(jnp.int32)
        owner_row = source // TOP
        slot_x = jnp.where(filled[..., None], tokens[owner_row], jnp.zeros((), jnp.bfloat16))
        scaled = flat_gates[source][..., None] * out_grad[owner_row].astype(jnp.float32)
        slot_dy = jnp.where(filled[..., None], scaled, 0.0).astype(jnp.bfloat16)
        x_f = slot_x.astype(jnp.float32)
        y_f = slot_dy.astype(jnp.float32)
        gate_w = w_gate[expert].astype(jnp.float32)
        up_w = w_up[expert].astype(jnp.float32)
        down_w = w_down[expert].astype(jnp.float32)
        gate_pre = jnp.einsum("gsd,df->gsf", x_f, gate_w)
        up_pre = jnp.einsum("gsd,df->gsf", x_f, up_w)
        sigma = jax.nn.sigmoid(gate_pre)
        active = gate_pre * sigma
        activated = (active * up_pre).astype(jnp.bfloat16)
        back_hidden = jnp.einsum("gsd,fd->gsf", y_f, down_w)
        up_delta = (back_hidden * active).astype(jnp.bfloat16)
        gate_delta = (back_hidden * up_pre * sigma * (1.0 + gate_pre * (1.0 - sigma))).astype(jnp.bfloat16)
        pair_grad = (jnp.einsum("gsf,df->gsd", gate_delta.astype(jnp.float32), gate_w)
                     + jnp.einsum("gsf,df->gsd", up_delta.astype(jnp.float32), up_w)).astype(jnp.bfloat16)
        added = jnp.where(filled[..., None], pair_grad.astype(jnp.float32), 0.0).reshape(-1, D)
        grad_sum = grad_sum.at[owner_row.reshape(-1)].add(added)
        gate_part = jnp.einsum("gsd,gsf->gdf", x_f, gate_delta.astype(jnp.float32))
        up_part = jnp.einsum("gsd,gsf->gdf", x_f, up_delta.astype(jnp.float32))
        down_part = jnp.einsum("gsf,gsd->gfd", activated.astype(jnp.float32), y_f)
        return grad_sum, (rounded_sum(gate_part), rounded_sum(up_part), rounded_sum(down_part))

    start_sum = jnp.zeros((tokens.shape[0], D), jnp.float32)
    grad_sum, grads = lax.scan(per_expert, start_sum, jnp.arange(EXPERTS, dtype=jnp.int32))
    return (grad_sum.astype(jnp.bfloat16), grads[0], grads[1], grads[2])
```

```python
import jax
import jax.numpy as jnp
from jax import lax
from jax.sharding import PartitionSpec as P


F32 = jnp.float32
BF16 = jnp.bfloat16


def slots_of(tok_rows, top_count, expert_count):
    return min(tok_rows, max(2, 9 * tok_rows * top_count // (8 * expert_count)))


def line_gather(own, chips):
    right, left = [own], [own]
    for step in range(1, chips):
        right.append(
            lax.ppermute(
                right[-1], "expert", [(2 * z + c, 2 * z + 2 + c) for z in range(step - 1, chips - 1) for c in (0, 1)]
            )
        )
        left.append(
            lax.ppermute(
                left[-1], "expert", [(2 * z + c, 2 * z - 2 + c) for z in range(1, chips - step + 1) for c in (0, 1)]
            )
        )
    chip = lax.axis_index("expert") // 2
    slots = [own]
    for slot in range(1, chips):
        slots.append(jnp.where(chip >= slot, right[slot], left[chips - slot]))
    return jnp.concatenate(slots, axis=0)


def line_scatter(blocks, chips):
    right = left = None
    for step in range(1, chips):
        going_right, going_left = blocks[step], blocks[chips - step]
        if right is not None:
            going_right = (going_right.astype(F32) + right.astype(F32)).astype(BF16)
            going_left = (going_left.astype(F32) + left.astype(F32)).astype(BF16)
        right = lax.ppermute(
            going_right, "expert", [(2 * z + c, 2 * z + 2 + c) for z in range(step) if z + 1 < chips for c in (0, 1)]
        )
        left = lax.ppermute(
            going_left,
            "expert",
            [(2 * z + c, 2 * z - 2 + c) for z in range(chips - step, chips) if z > 0 for c in (0, 1)],
        )
    return blocks[0].astype(F32) + right.astype(F32) + left.astype(F32)


def dense(tokens, out_grad, routes, gate_values, w_gate, w_up, w_down):
    tok_rows, model_width = tokens.shape
    experts = lax.axis_size("expert")
    chips = experts // 2
    hidden = w_gate.shape[2]
    share = model_width // 4
    half = share // 2
    me = lax.axis_index("dp")
    expert = lax.axis_index("expert")
    chip, core = expert // 2, expert % 2
    to_x = [(i, i ^ 1) for i in range(4)]
    to_y = [(i, i ^ 2) for i in range(4)]
    partner = [(e, e ^ 1) for e in range(experts)]
    order = [(0, 0), (2, 0), (1, 0), (3, 0), (0, 1), (1, 1), (2, 1), (3, 1)]

    def reorder(rows):
        return jnp.concatenate(
            [lax.dynamic_slice_in_dim(rows, (me ^ k) * share + h * half, half, axis=1) for k, h in order], axis=1
        )

    def gather_weight(own):
        from_x = lax.ppermute(own, "dp", to_x)
        from_y = lax.ppermute(own, "dp", to_y)
        diag_a = lax.ppermute(from_y[:half], "dp", to_x)
        diag_b = lax.ppermute(from_x[half:], "dp", to_y)
        return jnp.concatenate(
            [own[:half], from_y[:half], from_x[:half], diag_a, own[half:], from_x[half:], from_y[half:], diag_b],
            axis=0,
        )

    def scatter_grad(lhs, rhs):
        def part(block):
            cols = lhs[:, block * share : (block + 1) * share]
            return lax.dot_general(cols, rhs, (((0,), (0,)), ((), ())), preferred_element_type=F32)

        from_x = lax.ppermute(part(1).astype(BF16), "dp", to_x)
        from_y = lax.ppermute(part(3).astype(BF16), "dp", to_y)
        sum_a = part(0) + from_x.astype(F32)
        sum_b = part(2) + from_y.astype(F32)
        last_a = lax.ppermute(sum_a[half:].astype(BF16), "dp", to_y)
        last_b = lax.ppermute(sum_b[half:].astype(BF16), "dp", to_x)
        return jnp.concatenate([sum_a[:half] + last_a.astype(F32), sum_b[:half] + last_b.astype(F32)], axis=0).astype(
            BF16
        )

    onehot = routes[:, :, None] == jnp.arange(experts, dtype=routes.dtype)
    gates = jnp.sum(jnp.where(onehot, gate_values[:, :, None], 0.0), axis=1)
    gates = lax.all_to_all(gates.T.reshape(experts, 1, tok_rows), "expert", split_axis=0, concat_axis=0, tiled=True)
    source = (chip - jnp.arange(chips)) % chips * 2
    source = jnp.concatenate([source + core, source + 1 - core])
    gate = gates.reshape(experts, tok_rows)[source].reshape(experts * tok_rows, 1)

    w_in = gather_weight(jnp.concatenate([w_gate[0], w_up[0]], axis=1))
    w_out = gather_weight(w_down[0].T)
    own_x = line_gather(reorder(tokens), chips)
    own_y = line_gather(reorder(out_grad), chips)
    x = jnp.concatenate([own_x, lax.ppermute(own_x, "expert", partner)], axis=0)
    y = jnp.concatenate([own_y, lax.ppermute(own_y, "expert", partner)], axis=0)

    pre = jnp.dot(x, w_in, preferred_element_type=F32)
    gate_pre, up_pre = pre[:, :hidden], pre[:, hidden:]
    sigma = jax.nn.sigmoid(gate_pre)
    active = gate_pre * sigma
    activated = (gate * active * up_pre).astype(BF16)
    back = gate * jnp.dot(y, w_out, preferred_element_type=F32)
    up_delta = (back * active).astype(BF16)
    gate_delta = (back * up_pre * sigma * (1.0 + gate_pre * (1.0 - sigma))).astype(BF16)
    delta = jnp.concatenate([gate_delta, up_delta], axis=1)
    down_share = scatter_grad(y, activated)
    in_share = scatter_grad(x, delta)
    pair = lax.dot_general(delta, w_in, (((1,), (1,)), ((), ())), preferred_element_type=F32).astype(BF16)
    split = chips * tok_rows
    other = lax.ppermute(pair[split:], "expert", partner)
    total = (pair[:split].astype(F32) + other.astype(F32)).astype(BF16)
    total = line_scatter([total[s * tok_rows : (s + 1) * tok_rows] for s in range(chips)], chips)
    total = total.astype(BF16)
    place = {pos: i for i, pos in enumerate(order)}
    pieces = []
    for block in range(4):
        for h in (0, 1):
            at = jnp.array([place[(k, h)] for k in range(4)], jnp.int32)[me ^ block]
            pieces.append(lax.dynamic_slice_in_dim(total, at * half, half, axis=1))
    input_grad = jnp.concatenate(pieces, axis=1)
    return (
        input_grad,
        in_share[None, :, :hidden],
        in_share[None, :, hidden:],
        down_share.T[None],
    )


def routed(tokens, out_grad, routes, gate_values, w_gate, w_up, w_down):
    tok_rows, model_width = tokens.shape
    top_count = routes.shape[1]
    group_count = lax.axis_size("expert")
    local_count = w_gate.shape[0]
    expert_count = group_count * local_count
    hidden_units = w_gate.shape[2]
    capacity = slots_of(tok_rows, top_count, expert_count)
    pair_count = tok_rows * top_count
    slot_count = group_count * capacity
    expert_of = routes.reshape(-1)
    onehot = (expert_of[:, None] == jnp.arange(expert_count, dtype=jnp.int32)[None, :]).astype(
        jnp.int32
    )
    before = jnp.cumsum(onehot, axis=0) - onehot
    placed = jnp.sum(before * onehot, axis=1)
    slot_of = expert_of * capacity + placed
    slot_table = jnp.full((expert_count * capacity,), pair_count, jnp.int32)
    slot_table = slot_table.at[slot_of].set(jnp.arange(pair_count, dtype=jnp.int32))
    filled = slot_table < pair_count
    source = jnp.where(filled, slot_table, 0)
    owner_row = source // top_count
    send_x = jnp.where(filled[:, None], tokens[owner_row], jnp.zeros((), jnp.bfloat16))
    scaled = gate_values.reshape(-1)[source][:, None] * out_grad[owner_row].astype(jnp.float32)
    send_dy = jnp.where(filled[:, None], scaled, 0.0).astype(jnp.bfloat16)
    send_x = send_x.reshape(expert_count, capacity, model_width)
    send_dy = send_dy.reshape(expert_count, capacity, model_width)
    recv_x, recv_dy = (
        lax.all_to_all(send_x, "expert", split_axis=0, concat_axis=0, tiled=True),
        lax.all_to_all(send_dy, "expert", split_axis=0, concat_axis=0, tiled=True),
    )

    def to_local(stacked):
        shaped = stacked.reshape(group_count, local_count, capacity, model_width)
        return shaped.transpose(1, 0, 2, 3).reshape(local_count, slot_count, model_width)

    slot_x = to_local(recv_x)
    slot_dy = to_local(recv_dy)
    part_x = slot_x
    gate_term = jnp.einsum(
        "asd,adf->asf",
        part_x,
        lax.all_gather(w_gate, "dp", axis=1, tiled=True),
        preferred_element_type=jnp.float32,
    )
    up_term = jnp.einsum(
        "asd,adf->asf",
        part_x,
        lax.all_gather(w_up, "dp", axis=1, tiled=True),
        preferred_element_type=jnp.float32,
    )
    full_gate, full_up, full_down = (
        lax.all_gather(w_gate, "dp", axis=1, tiled=True),
        lax.all_gather(w_up, "dp", axis=1, tiled=True),
        lax.all_gather(w_down, "dp", axis=2, tiled=True),
    )
    sigma = jax.nn.sigmoid(gate_term)
    active = gate_term * sigma
    activated = (active * up_term).astype(jnp.bfloat16)
    back_hidden = jnp.einsum("asd,afd->asf", slot_dy, full_down, preferred_element_type=jnp.float32)
    up_delta = (back_hidden * active).astype(jnp.bfloat16)
    gate_delta = (back_hidden * up_term * sigma * (1.0 + gate_term * (1.0 - sigma))).astype(
        jnp.bfloat16
    )
    pair_grad = (
        jnp.einsum("asf,adf->asd", gate_delta, full_gate, preferred_element_type=jnp.float32)
        + jnp.einsum("asf,adf->asd", up_delta, full_up, preferred_element_type=jnp.float32)
    ).astype(jnp.bfloat16)
    send_back = pair_grad.reshape(local_count, group_count, capacity, model_width).transpose(
        1, 0, 2, 3
    )
    send_back = send_back.reshape(expert_count, capacity, model_width)
    returned = lax.all_to_all(send_back, "expert", split_axis=0, concat_axis=0, tiled=True)
    per_pair = returned.reshape(expert_count * capacity, model_width)[slot_of].astype(jnp.float32)
    input_grad = jnp.sum(per_pair.reshape(tok_rows, top_count, model_width), axis=1).astype(
        jnp.bfloat16
    )
    block_width = local_count * hidden_units
    share_width = model_width // lax.axis_size("dp")
    part_x = slot_x
    term_gate = jnp.einsum("asd,asf->daf", part_x, gate_delta, preferred_element_type=jnp.float32)
    term_up = jnp.einsum("asd,asf->daf", part_x, up_delta, preferred_element_type=jnp.float32)
    term_down = jnp.einsum("asd,asf->daf", slot_dy, activated, preferred_element_type=jnp.float32)
    shares = lax.psum_scatter(
        jnp.concatenate(
            [
                term_gate.reshape(lax.axis_size("dp") * share_width, block_width),
                term_up.reshape(lax.axis_size("dp") * share_width, block_width),
                term_down.reshape(lax.axis_size("dp") * share_width, block_width),
            ],
            axis=1,
        ).astype(jnp.bfloat16),
        "dp",
        scatter_dimension=0,
        tiled=True,
    ).astype(jnp.float32)
    share_rows = shares.shape[0]

    def unpack(which):
        return shares[:, which * block_width : (which + 1) * block_width].reshape(
            share_rows, local_count, hidden_units
        )

    gate_grad = unpack(0).transpose(1, 0, 2).astype(jnp.bfloat16)
    up_grad = unpack(1).transpose(1, 0, 2).astype(jnp.bfloat16)
    down_grad = unpack(2).transpose(1, 2, 0).astype(jnp.bfloat16)
    return (input_grad, gate_grad, up_grad, down_grad)


def local(tokens, out_grad, routes, gate_values, w_gate, w_up, w_down):
    experts = lax.axis_size("expert") * w_gate.shape[0]
    capacity = slots_of(tokens.shape[0], routes.shape[1], experts)
    whole = lax.axis_size("dp") == 4 and lax.axis_size("expert") % 2 == 0 and w_gate.shape[0] == 1
    plan = dense if whole and tokens.shape[0] <= 2 * capacity else routed
    return plan(tokens, out_grad, routes, gate_values, w_gate, w_up, w_down)


def solution(mesh):
    return jax.shard_map(
        local,
        mesh=mesh,
        in_specs=(
            P(("dp", "expert"), None),
            P(("dp", "expert"), None),
            P(("dp", "expert"), None),
            P(("dp", "expert"), None),
            P("expert", "dp", None),
            P("expert", "dp", None),
            P("expert", None, "dp"),
        ),
        out_specs=(
            P(("dp", "expert"), None),
            P("expert", "dp", None),
            P("expert", "dp", None),
            P("expert", None, "dp"),
        ),
        check_vma=False,
    )
```

```python
import functools

import jax
import jax.numpy as jnp
from jax import lax
from jax.experimental import pallas as pl
from jax.experimental.pallas import tpu as pltpu
from jax.sharding import PartitionSpec as P


F32 = jnp.float32
BF16 = jnp.bfloat16
ANY = pl.BlockSpec(memory_space=pl.ANY)
VMEM = pl.BlockSpec(memory_space=pltpu.VMEM)
SMEM = pl.BlockSpec(memory_space=pltpu.SMEM)
LIMIT = 60 * 1024 * 1024
LANES = 128
NN = (((1,), (0,)), ((), ()))
NT = (((1,), (1,)), ((), ()))
TN = (((0,), (0,)), ((), ()))


def mm(a, b, dims):
    return lax.dot_general(a, b, dims, preferred_element_type=F32)


def slots_of(tok_rows, top_count, expert_count):
    return min(tok_rows, max(2, 9 * tok_rows * top_count // (8 * expert_count)))


def call(body, outs, ins, scratch, flops, moved):
    return pl.pallas_call(
        body,
        out_shape=[jax.ShapeDtypeStruct(s, d) for s, d, _ in outs],
        in_specs=[s for _, s in ins],
        out_specs=[s for _, _, s in outs],
        scratch_shapes=scratch,
        compiler_params=pltpu.CompilerParams(vmem_limit_bytes=LIMIT),
        cost_estimate=pl.CostEstimate(flops=flops, bytes_accessed=moved, transcendentals=0),
    )(*[a for a, _ in ins])


def prep_body(experts, routes, gates, rows, out):
    tok, width = rows.shape
    line = lax.broadcasted_iota(jnp.int32, (LANES, tok), 0)
    term, named = line // experts, line % experts
    value = jnp.zeros((LANES, tok), F32)
    for k in range(routes.shape[0]):
        value += jnp.where(routes[k : k + 1, :] == named, gates[k : k + 1, :], 0.0)
    high = value.astype(BF16).astype(F32)
    mid = (value - high).astype(BF16).astype(F32)
    low = value - high - mid
    value = jnp.where(term == 0, high, jnp.where(term == 1, mid, jnp.where(term == 2, low, 0.0)))
    out[:, :width] = rows[...]
    out[:, width:] = jnp.transpose(value).astype(BF16)


class Copies:
    def __init__(self, sems):
        self.sems, self.used = sems, 0

    def start(self, src, dst):
        copy = pltpu.make_async_copy(src, dst, self.sems.at[self.used])
        self.used += 1
        copy.start()
        return copy

    def pick(self, first, src, other, dst):
        sem = self.sems.at[self.used]
        self.used += 1

        @pl.when(first)
        def _():
            pltpu.make_async_copy(src, dst, sem).start()

        @pl.when(jnp.logical_not(first))
        def _():
            pltpu.make_async_copy(other, dst, sem).start()

        return pltpu.make_async_copy(other, dst, sem)


def load_rows(copies, chip, pieces, dst):
    tok = pieces[0].shape[0]
    started = []
    for core in (0, 1):
        own, two, right, left, far = pieces[5 * core : 5 * core + 5]
        at = [dst.at[pl.ds((4 * core + s) * tok, tok)] for s in range(4)]
        started.append(copies.start(own, at[0]))
        started.append(copies.pick(chip == 0, far, right, at[1]))
        started.append(copies.start(two, at[2]))
        started.append(copies.pick(chip == 3, far, left, at[3]))
    return started


def pre_body(place, *refs):
    pieces, w_gate, w_up = refs[:10], refs[10:14], refs[14:18]
    act, active_out, slope_out, x_out, x, wg, wu, sems = refs[18:]
    me, chip = place[0], place[1]
    copies = Copies(sems)
    rows = load_rows(copies, chip, pieces, x)
    share, hidden = w_gate[0].shape
    weights = []
    for k in range(4):
        at = pl.ds((me ^ k) * share, share)
        weights += [copies.start(w_gate[k], wg.at[at]), copies.start(w_up[k], wu.at[at])]
    for c in rows:
        c.wait()
    out = copies.start(x, x_out)
    for c in weights:
        c.wait()
    tm, tn = x.shape[0] // 2, 256

    def step(i, _):
        r = pl.ds(pl.multiple_of(i // (hidden // tn) * tm, tm), tm)
        c = pl.ds(pl.multiple_of(i % (hidden // tn) * tn, tn), tn)
        lhs = x[r, :]
        gate = mm(lhs, wg[:, c], NN)
        up = mm(lhs, wu[:, c], NN)
        sigma = jax.nn.sigmoid(gate)
        active = gate * sigma
        act[r, c] = (active * up).astype(BF16)
        active_out[r, c] = active
        slope_out[r, c] = up * sigma * (1.0 + gate * (1.0 - sigma))
        return 0

    lax.fori_loop(0, 2 * (hidden // tn), step, 0)
    out.wait()


def down_body(experts, place, *refs):
    pieces, act = refs[:10], refs[10]
    send_a, keep_a, send_b, keep_b, y_out, raw, y, sems = refs[11:]
    me, chip, expert = place[0], place[1], place[2]
    copies = Copies(sems)
    for c in load_rows(copies, chip, pieces, raw):
        c.wait()
    rows, width = y.shape
    tok = rows // 8
    lane = lax.broadcasted_iota(jnp.int32, (tok, LANES), 1)
    mine = jnp.logical_and(lane % experts == expert, lane < 3 * experts)

    def scale(i, _):
        r = pl.ds(pl.multiple_of(i * tok, tok), tok)
        gate = jnp.sum(jnp.where(mine, raw[r, width:].astype(F32), 0.0), axis=1, keepdims=True)
        y[r, :] = (raw[r, :width].astype(F32) * gate).astype(BF16)
        return 0

    lax.fori_loop(0, 8, scale, 0)
    out = copies.start(y, y_out)
    share = width // 4
    half = act.shape[1] // 2
    for dst, h, pair in ((send_a, 0, (1, 3)), (send_b, 1, (2, 3)), (keep_a, 0, (0, 2)), (keep_b, 1, (0, 1))):
        for slot, k in enumerate(pair):
            cols = pl.ds(pl.multiple_of((me ^ k) * share, share), share)
            dst[slot] = mm(act[:, h * half : (h + 1) * half], y[:, cols], TN).astype(BF16)
    out.wait()


def back_body(place, y, active, slope, own, from_x, from_y, diag_a, diag_b, gate_delta, up_delta, w, sems):
    me = place[0]
    copies = Copies(sems)
    hidden, share = own.shape
    half = hidden // 2
    started = []
    for k, src in ((0, own), (1, from_x), (2, from_y)):
        started.append(copies.start(src, w.at[me ^ k]))
    started.append(copies.start(diag_a, w.at[me ^ 3, pl.ds(0, half)]))
    started.append(copies.start(diag_b, w.at[me ^ 3, pl.ds(half, half)]))
    for c in started:
        c.wait()
    rows = y.shape[0]
    tm, tn = rows // 2, 256

    def step(i, _):
        r = pl.ds(pl.multiple_of(i // (hidden // tn) * tm, tm), tm)
        c = pl.ds(pl.multiple_of(i % (hidden // tn) * tn, tn), tn)
        back = mm(y[r, 0:share], w[0, c, :], NT)
        for j in range(1, 4):
            back += mm(y[r, j * share : (j + 1) * share], w[j, c, :], NT)
        up_delta[r, c] = (back * active[r, c]).astype(BF16)
        gate_delta[r, c] = (back * slope[r, c]).astype(BF16)
        return 0

    lax.fori_loop(0, 2 * (hidden // tn), step, 0)


def grad_body(send_pair, keep_pair, place, x, delta, send, keep):
    me = place[0]
    share = x.shape[1] // 4
    tm = share // 2
    for dst, pair in ((send, send_pair), (keep, keep_pair)):
        for slot, k in enumerate(pair):

            def step(i, _, dst=dst, slot=slot, k=k):
                cols = pl.ds(pl.multiple_of((me ^ k) * share + i * tm, tm), tm)
                dst[slot, pl.ds(pl.multiple_of(i * tm, tm), tm), :] = mm(x[:, cols], delta[...], TN).astype(BF16)
                return 0

            lax.fori_loop(0, 2, step, 0)


def pair_body(place, gate_delta, up_delta, *refs):
    w_gate, w_up = refs[:4], refs[4:8]
    send, keep, wg, wu, sems = refs[8:]
    me = place[0]
    copies = Copies(sems)
    started = []
    for k in range(4):
        started.append((copies.start(w_gate[k], wg.at[k]), copies.start(w_up[k], wu.at[k])))
    share = wg.shape[1]
    tn = share // 2
    rows = keep.shape[0]
    for k in range(4):
        for c in started[k]:
            c.wait()
    for dst, first in ((send, rows), (keep, 0)):

        def step(i, _, dst=dst, first=first):
            k, part = i // 2, pl.ds(pl.multiple_of(i % 2 * tn, tn), tn)
            total = mm(gate_delta[first : first + rows, :], wg[k, part, :], NT)
            total += mm(up_delta[first : first + rows, :], wu[k, part, :], NT)
            cols = pl.ds(pl.multiple_of((me ^ k) * share + i % 2 * tn, tn), tn)
            dst[:, cols] = total.astype(BF16)
            return 0

        lax.fori_loop(0, 8, step, 0)


def add(*terms):
    total = terms[0].astype(F32)
    for term in terms[1:]:
        total = total + term.astype(F32)
    return total.astype(BF16)


def dense(tokens, out_grad, routes, gate_values, w_gate, w_up, w_down):
    tok, width = tokens.shape
    experts = lax.axis_size("expert")
    chips = experts // 2
    hidden = w_gate.shape[2]
    share = width // 4
    half = hidden // 2
    rows = experts * tok
    expert = lax.axis_index("expert")
    chip = expert // 2
    place = jnp.stack([lax.axis_index("dp"), chip, expert]).astype(jnp.int32)

    def to_x(block):
        return lax.ppermute(block, "dp", [(i, i ^ 1) for i in range(4)])

    def to_y(block):
        return lax.ppermute(block, "dp", [(i, i ^ 2) for i in range(4)])

    def hop(block, moves):
        return lax.ppermute(block, "expert", [(2 * a + c, 2 * b + c) for a, b in moves for c in (0, 1)])

    def swap(block, at=range(chips)):
        return lax.ppermute(block, "expert", [(2 * z + c, 2 * z + 1 - c) for z in at for c in (0, 1)])

    def line(own):
        two = hop(own, [(z, (z + 2) % 4) for z in range(4)])
        right = hop(own, [(0, 1), (1, 2), (2, 3)])
        left = hop(own, [(1, 0), (2, 1), (3, 2)])
        far = hop(two, [(2, 3), (1, 0)])
        return [own, two, right, left, far] + [
            swap(own),
            swap(two),
            swap(right, (1, 2, 3)),
            swap(left, (0, 1, 2)),
            swap(far, (0, 3)),
        ]

    x_pieces = line(tokens)
    (y_own,) = call(
        functools.partial(prep_body, experts),
        [((tok, width + LANES), BF16, VMEM)],
        [(routes.T, VMEM), (gate_values.T, VMEM), (out_grad, VMEM)],
        [],
        1000,
        4 * tok * width,
    )
    y_pieces = line(y_own)

    wg0, wu0, wd0 = w_gate[0], w_up[0], w_down[0]
    wg1, wu1 = to_x(wg0), to_y(wu0)
    wg2, wu2 = to_y(wg0), to_x(wu0)
    wg3, wu3 = to_y(wg1), to_x(wu1)
    w_g, w_u = (wg0, wg1, wg2, wg3), (wu0, wu2, wu1, wu3)
    wd1, wd2 = to_x(wd0), to_y(wd0)
    wd3a, wd3b = to_x(wd2[:half]), to_y(wd1[half:])

    def dma(n):
        return pltpu.SemaphoreType.DMA((n,))

    weight = pltpu.VMEM((width, hidden), BF16)
    act, active, slope, x = call(
        pre_body,
        [
            ((rows, hidden), BF16, VMEM),
            ((rows, hidden), F32, VMEM),
            ((rows, hidden), F32, VMEM),
            ((rows, width), BF16, ANY),
        ],
        [(place, SMEM)] + [(a, ANY) for a in x_pieces] + [(a, ANY) for a in w_g + w_u],
        [pltpu.VMEM((rows, width), BF16), weight, weight, dma(17)],
        4 * rows * width * hidden,
        2 * (2 * rows * width + 2 * width * hidden) + 10 * rows * hidden,
    )
    piece = (2, half, share)
    send_a, keep_a, send_b, keep_b, y = call(
        functools.partial(down_body, experts),
        [(piece, BF16, VMEM)] * 4 + [((rows, width), BF16, ANY)],
        [(place, SMEM)] + [(a, ANY) for a in y_pieces] + [(act, VMEM)],
        [pltpu.VMEM((rows, width + LANES), BF16), pltpu.VMEM((rows, width), BF16), dma(9)],
        2 * rows * width * hidden,
        2 * (2 * rows * width + rows * hidden + width * hidden),
    )
    got_a, got_b = to_x(send_a), to_y(send_b)
    gate_delta, up_delta = call(
        back_body,
        [((rows, hidden), BF16, VMEM)] * 2,
        [(place, SMEM), (y, VMEM), (active, VMEM), (slope, VMEM)] + [(a, ANY) for a in (wd0, wd1, wd2, wd3a, wd3b)],
        [pltpu.VMEM((4, hidden, share), BF16), dma(5)],
        2 * rows * width * hidden,
        2 * (rows * width + width * hidden) + 12 * rows * hidden,
    )
    piece = (2, share, hidden)

    def grad(delta, send_pair, keep_pair):
        return call(
            functools.partial(grad_body, send_pair, keep_pair),
            [(piece, BF16, VMEM)] * 2,
            [(place, SMEM), (x, VMEM), (delta, VMEM)],
            [],
            2 * rows * width * hidden,
            2 * (rows * width + rows * hidden + width * hidden),
        )

    gate_send, gate_keep = grad(gate_delta, (1, 3), (0, 2))
    gate_got = to_x(gate_send)
    up_send, up_keep = grad(up_delta, (2, 3), (0, 1))
    up_got = to_y(up_send)
    weight = pltpu.VMEM((4, share, hidden), BF16)
    pair_send, pair_keep = call(
        pair_body,
        [((rows // 2, width), BF16, VMEM)] * 2,
        [(place, SMEM), (gate_delta, VMEM), (up_delta, VMEM)] + [(a, ANY) for a in w_g + w_u],
        [weight, weight, dma(8)],
        4 * rows * width * hidden,
        2 * (rows * width + 2 * rows * hidden + 2 * width * hidden),
    )
    down_a = add(keep_a[0], got_a[0]), to_y(add(keep_a[1], got_a[1]))
    down_b = add(keep_b[0], got_b[0]), to_x(add(keep_b[1], got_b[1]))
    down_grad = jnp.concatenate([add(*down_a), add(*down_b)], axis=0)
    gate_grad = add(add(gate_keep[0], gate_got[0]), to_y(add(gate_keep[1], gate_got[1])))
    up_grad = add(add(up_keep[0], up_got[0]), to_x(add(up_keep[1], up_got[1])))

    total = add(pair_keep, swap(pair_send)).reshape(chips, tok, width)
    far = hop(jnp.where(chip == 0, total[1], total[3]), [(3, 2), (0, 1)])
    right = hop(total[3], [(0, 1), (1, 2), (2, 3)])
    left = hop(total[1], [(1, 0), (2, 1), (3, 2)])
    two = hop(add(total[2], far), [(z, (z + 2) % 4) for z in range(4)])
    input_grad = add(total[0], right, left, two)
    return input_grad, gate_grad[None], up_grad[None], down_grad[None]


def routed(tokens, out_grad, routes, gate_values, w_gate, w_up, w_down):
    tok_rows, model_width = tokens.shape
    top_count = routes.shape[1]
    group_count = lax.axis_size("expert")
    local_count = w_gate.shape[0]
    expert_count = group_count * local_count
    hidden_units = w_gate.shape[2]
    capacity = slots_of(tok_rows, top_count, expert_count)
    pair_count = tok_rows * top_count
    slot_count = group_count * capacity
    expert_of = routes.reshape(-1)
    onehot = (expert_of[:, None] == jnp.arange(expert_count, dtype=jnp.int32)[None, :]).astype(
        jnp.int32
    )
    before = jnp.cumsum(onehot, axis=0) - onehot
    placed = jnp.sum(before * onehot, axis=1)
    slot_of = expert_of * capacity + placed
    slot_table = jnp.full((expert_count * capacity,), pair_count, jnp.int32)
    slot_table = slot_table.at[slot_of].set(jnp.arange(pair_count, dtype=jnp.int32))
    filled = slot_table < pair_count
    source = jnp.where(filled, slot_table, 0)
    owner_row = source // top_count
    send_x = jnp.where(filled[:, None], tokens[owner_row], jnp.zeros((), jnp.bfloat16))
    scaled = gate_values.reshape(-1)[source][:, None] * out_grad[owner_row].astype(jnp.float32)
    send_dy = jnp.where(filled[:, None], scaled, 0.0).astype(jnp.bfloat16)
    send_x = send_x.reshape(expert_count, capacity, model_width)
    send_dy = send_dy.reshape(expert_count, capacity, model_width)
    recv_x, recv_dy = (
        lax.all_to_all(send_x, "expert", split_axis=0, concat_axis=0, tiled=True),
        lax.all_to_all(send_dy, "expert", split_axis=0, concat_axis=0, tiled=True),
    )

    def to_local(stacked):
        shaped = stacked.reshape(group_count, local_count, capacity, model_width)
        return shaped.transpose(1, 0, 2, 3).reshape(local_count, slot_count, model_width)

    slot_x = to_local(recv_x)
    slot_dy = to_local(recv_dy)
    part_x = slot_x
    gate_term = jnp.einsum(
        "asd,adf->asf",
        part_x,
        lax.all_gather(w_gate, "dp", axis=1, tiled=True),
        preferred_element_type=jnp.float32,
    )
    up_term = jnp.einsum(
        "asd,adf->asf",
        part_x,
        lax.all_gather(w_up, "dp", axis=1, tiled=True),
        preferred_element_type=jnp.float32,
    )
    full_gate, full_up, full_down = (
        lax.all_gather(w_gate, "dp", axis=1, tiled=True),
        lax.all_gather(w_up, "dp", axis=1, tiled=True),
        lax.all_gather(w_down, "dp", axis=2, tiled=True),
    )
    sigma = jax.nn.sigmoid(gate_term)
    active = gate_term * sigma
    activated = (active * up_term).astype(jnp.bfloat16)
    back_hidden = jnp.einsum("asd,afd->asf", slot_dy, full_down, preferred_element_type=jnp.float32)
    up_delta = (back_hidden * active).astype(jnp.bfloat16)
    gate_delta = (back_hidden * up_term * sigma * (1.0 + gate_term * (1.0 - sigma))).astype(
        jnp.bfloat16
    )
    pair_grad = (
        jnp.einsum("asf,adf->asd", gate_delta, full_gate, preferred_element_type=jnp.float32)
        + jnp.einsum("asf,adf->asd", up_delta, full_up, preferred_element_type=jnp.float32)
    ).astype(jnp.bfloat16)
    send_back = pair_grad.reshape(local_count, group_count, capacity, model_width).transpose(
        1, 0, 2, 3
    )
    send_back = send_back.reshape(expert_count, capacity, model_width)
    returned = lax.all_to_all(send_back, "expert", split_axis=0, concat_axis=0, tiled=True)
    per_pair = returned.reshape(expert_count * capacity, model_width)[slot_of].astype(jnp.float32)
    input_grad = jnp.sum(per_pair.reshape(tok_rows, top_count, model_width), axis=1).astype(
        jnp.bfloat16
    )
    block_width = local_count * hidden_units
    share_width = model_width // lax.axis_size("dp")
    part_x = slot_x
    term_gate = jnp.einsum("asd,asf->daf", part_x, gate_delta, preferred_element_type=jnp.float32)
    term_up = jnp.einsum("asd,asf->daf", part_x, up_delta, preferred_element_type=jnp.float32)
    term_down = jnp.einsum("asd,asf->daf", slot_dy, activated, preferred_element_type=jnp.float32)
    shares = lax.psum_scatter(
        jnp.concatenate(
            [
                term_gate.reshape(lax.axis_size("dp") * share_width, block_width),
                term_up.reshape(lax.axis_size("dp") * share_width, block_width),
                term_down.reshape(lax.axis_size("dp") * share_width, block_width),
            ],
            axis=1,
        ).astype(jnp.bfloat16),
        "dp",
        scatter_dimension=0,
        tiled=True,
    ).astype(jnp.float32)
    share_rows = shares.shape[0]

    def unpack(which):
        return shares[:, which * block_width : (which + 1) * block_width].reshape(
            share_rows, local_count, hidden_units
        )

    gate_grad = unpack(0).transpose(1, 0, 2).astype(jnp.bfloat16)
    up_grad = unpack(1).transpose(1, 0, 2).astype(jnp.bfloat16)
    down_grad = unpack(2).transpose(1, 2, 0).astype(jnp.bfloat16)
    return (input_grad, gate_grad, up_grad, down_grad)


def local(tokens, out_grad, routes, gate_values, w_gate, w_up, w_down):
    experts = lax.axis_size("expert") * w_gate.shape[0]
    capacity = slots_of(tokens.shape[0], routes.shape[1], experts)
    whole = lax.axis_size("dp") == 4 and lax.axis_size("expert") == 8 and w_gate.shape[0] == 1
    plan = dense if whole and tokens.shape[0] <= 2 * capacity else routed
    return plan(tokens, out_grad, routes, gate_values, w_gate, w_up, w_down)


def solution(mesh):
    return jax.shard_map(
        local,
        mesh=mesh,
        in_specs=(
            P(("dp", "expert"), None),
            P(("dp", "expert"), None),
            P(("dp", "expert"), None),
            P(("dp", "expert"), None),
            P("expert", "dp", None),
            P("expert", "dp", None),
            P("expert", None, "dp"),
        ),
        out_specs=(
            P(("dp", "expert"), None),
            P("expert", "dp", None),
            P("expert", "dp", None),
            P("expert", None, "dp"),
        ),
        check_vma=False,
    )
```

```python
import functools

import jax
import jax.numpy as jnp
from jax import lax
from jax.experimental import pallas as pl
from jax.experimental.pallas import tpu as pltpu
from jax.sharding import PartitionSpec as P


F32 = jnp.float32
BF16 = jnp.bfloat16
ANY = pl.BlockSpec(memory_space=pl.ANY)
VMEM = pl.BlockSpec(memory_space=pltpu.VMEM)
SMEM = pl.BlockSpec(memory_space=pltpu.SMEM)
LIMIT = 24 * 1024 * 1024
LANES = 128
NN = (((1,), (0,)), ((), ()))
NT = (((1,), (1,)), ((), ()))
TN = (((0,), (0,)), ((), ()))


def mm(a, b, dims):
    return lax.dot_general(a, b, dims, preferred_element_type=F32)


def slots_of(tok_rows, top_count, expert_count):
    return min(tok_rows, max(2, 9 * tok_rows * top_count // (8 * expert_count)))


def call(body, outs, ins, scratch, flops, moved):
    return pl.pallas_call(
        body,
        out_shape=[jax.ShapeDtypeStruct(s, d) for s, d, _ in outs],
        in_specs=[s for _, s in ins],
        out_specs=[s for _, _, s in outs],
        scratch_shapes=scratch,
        compiler_params=pltpu.CompilerParams(vmem_limit_bytes=LIMIT),
        cost_estimate=pl.CostEstimate(flops=flops, bytes_accessed=moved, transcendentals=0),
    )(*[a for a, _ in ins])


def prep_body(experts, routes, gates, rows, out):
    tok, width = rows.shape
    line = lax.broadcasted_iota(jnp.int32, (LANES, tok), 0)
    term, named = line // experts, line % experts
    value = jnp.zeros((LANES, tok), F32)
    for k in range(routes.shape[0]):
        value += jnp.where(routes[k : k + 1, :] == named, gates[k : k + 1, :], 0.0)
    high = value.astype(BF16).astype(F32)
    mid = (value - high).astype(BF16).astype(F32)
    low = value - high - mid
    value = jnp.where(term == 0, high, jnp.where(term == 1, mid, jnp.where(term == 2, low, 0.0)))
    out[:, :width] = rows[...]
    out[:, width:] = jnp.transpose(value).astype(BF16)


class Copies:
    def __init__(self, sems):
        self.sems, self.used = sems, 0

    def start(self, src, dst):
        copy = pltpu.make_async_copy(src, dst, self.sems.at[self.used])
        self.used += 1
        copy.start()
        return copy

    def pick(self, first, src, other, dst):
        sem = self.sems.at[self.used]
        self.used += 1

        @pl.when(first)
        def _():
            pltpu.make_async_copy(src, dst, sem).start()

        @pl.when(jnp.logical_not(first))
        def _():
            pltpu.make_async_copy(other, dst, sem).start()

        return pltpu.make_async_copy(other, dst, sem)


def load_rows(copies, chip, pieces, dst):
    tok = pieces[0].shape[0]
    started = []
    for core in (0, 1):
        own, two, right, left, far = pieces[5 * core : 5 * core + 5]
        at = [dst.at[pl.ds((4 * core + s) * tok, tok)] for s in range(4)]
        started.append(copies.start(own, at[0]))
        started.append(copies.pick(chip == 0, far, right, at[1]))
        started.append(copies.start(two, at[2]))
        started.append(copies.pick(chip == 3, far, left, at[3]))
    return started


def pre_body(place, *refs):
    pieces, w_gate, w_up = refs[:10], refs[10:14], refs[14:18]
    act, active_out, slope_out, x_out, x, wg, wu, sems = refs[18:]
    me, chip = place[0], place[1]
    copies = Copies(sems)
    rows = load_rows(copies, chip, pieces, x)
    share, hidden = w_gate[0].shape
    weights = []
    for k in range(4):
        at = pl.ds((me ^ k) * share, share)
        weights += [copies.start(w_gate[k], wg.at[at]), copies.start(w_up[k], wu.at[at])]
    for c in rows:
        c.wait()
    out = copies.start(x, x_out)
    for c in weights:
        c.wait()
    tm, tn = x.shape[0] // 2, 256

    def step(i, _):
        r = pl.ds(pl.multiple_of(i // (hidden // tn) * tm, tm), tm)
        c = pl.ds(pl.multiple_of(i % (hidden // tn) * tn, tn), tn)
        lhs = x[r, :]
        gate = mm(lhs, wg[:, c], NN)
        up = mm(lhs, wu[:, c], NN)
        sigma = jax.nn.sigmoid(gate)
        active = gate * sigma
        act[r, c] = (active * up).astype(BF16)
        active_out[r, c] = active
        slope_out[r, c] = up * sigma * (1.0 + gate * (1.0 - sigma))
        return 0

    lax.fori_loop(0, 2 * (hidden // tn), step, 0)
    out.wait()


def down_body(experts, place, *refs):
    pieces, act = refs[:10], refs[10]
    send_a, keep_a, send_b, keep_b, y_out, raw, y, sems = refs[11:]
    me, chip, expert = place[0], place[1], place[2]
    copies = Copies(sems)
    for c in load_rows(copies, chip, pieces, raw):
        c.wait()
    rows, width = y.shape
    tok = rows // 8
    lane = lax.broadcasted_iota(jnp.int32, (tok, LANES), 1)
    mine = jnp.logical_and(lane % experts == expert, lane < 3 * experts)

    def scale(i, _):
        r = pl.ds(pl.multiple_of(i * tok, tok), tok)
        gate = jnp.sum(jnp.where(mine, raw[r, width:].astype(F32), 0.0), axis=1, keepdims=True)
        y[r, :] = (raw[r, :width].astype(F32) * gate).astype(BF16)
        return 0

    lax.fori_loop(0, 8, scale, 0)
    out = copies.start(y, y_out)
    share = width // 4
    half = act.shape[1] // 2
    for dst, h, pair in ((send_a, 0, (1, 3)), (send_b, 1, (2, 3)), (keep_a, 0, (0, 2)), (keep_b, 1, (0, 1))):
        for slot, k in enumerate(pair):
            cols = pl.ds(pl.multiple_of((me ^ k) * share, share), share)
            dst[slot] = mm(act[:, h * half : (h + 1) * half], y[:, cols], TN).astype(BF16)
    out.wait()


def back_body(place, y, active, slope, own, from_x, from_y, diag_a, diag_b, gate_delta, up_delta, w, sems):
    me = place[0]
    copies = Copies(sems)
    hidden, share = own.shape
    half = hidden // 2
    started = []
    for k, src in ((0, own), (1, from_x), (2, from_y)):
        started.append(copies.start(src, w.at[me ^ k]))
    started.append(copies.start(diag_a, w.at[me ^ 3, pl.ds(0, half)]))
    started.append(copies.start(diag_b, w.at[me ^ 3, pl.ds(half, half)]))
    for c in started:
        c.wait()
    rows = y.shape[0]
    tm, tn = rows // 2, 256

    def step(i, _):
        r = pl.ds(pl.multiple_of(i // (hidden // tn) * tm, tm), tm)
        c = pl.ds(pl.multiple_of(i % (hidden // tn) * tn, tn), tn)
        back = mm(y[r, 0:share], w[0, c, :], NT)
        for j in range(1, 4):
            back += mm(y[r, j * share : (j + 1) * share], w[j, c, :], NT)
        up_delta[r, c] = (back * active[r, c]).astype(BF16)
        gate_delta[r, c] = (back * slope[r, c]).astype(BF16)
        return 0

    lax.fori_loop(0, 2 * (hidden // tn), step, 0)


def grad_body(send_pair, keep_pair, place, x, delta, send, keep):
    me = place[0]
    share = x.shape[1] // 4
    tm = share // 2
    for dst, pair in ((send, send_pair), (keep, keep_pair)):
        for slot, k in enumerate(pair):

            def step(i, _, dst=dst, slot=slot, k=k):
                cols = pl.ds(pl.multiple_of((me ^ k) * share + i * tm, tm), tm)
                dst[slot, pl.ds(pl.multiple_of(i * tm, tm), tm), :] = mm(x[:, cols], delta[...], TN).astype(BF16)
                return 0

            lax.fori_loop(0, 2, step, 0)


def pair_body(place, gate_delta, up_delta, *refs):
    w_gate, w_up = refs[:4], refs[4:8]
    send, keep, wg, wu, sems = refs[8:]
    me = place[0]
    copies = Copies(sems)
    started = []
    for k in range(4):
        started.append((copies.start(w_gate[k], wg.at[k]), copies.start(w_up[k], wu.at[k])))
    share = wg.shape[1]
    tn = share // 2
    rows = keep.shape[0]
    for k in range(4):
        for c in started[k]:
            c.wait()
    for dst, first in ((send, rows), (keep, 0)):

        def step(i, _, dst=dst, first=first):
            k, part = i // 2, pl.ds(pl.multiple_of(i % 2 * tn, tn), tn)
            total = mm(gate_delta[first : first + rows, :], wg[k, part, :], NT)
            total += mm(up_delta[first : first + rows, :], wu[k, part, :], NT)
            cols = pl.ds(pl.multiple_of((me ^ k) * share + i % 2 * tn, tn), tn)
            dst[:, cols] = total.astype(BF16)
            return 0

        lax.fori_loop(0, 8, step, 0)


def add(*terms):
    total = terms[0].astype(F32)
    for term in terms[1:]:
        total = total + term.astype(F32)
    return total.astype(BF16)


def dense(tokens, out_grad, routes, gate_values, w_gate, w_up, w_down):
    tok, width = tokens.shape
    experts = lax.axis_size("expert")
    chips = experts // 2
    hidden = w_gate.shape[2]
    share = width // 4
    half = hidden // 2
    rows = experts * tok
    expert = lax.axis_index("expert")
    chip = expert // 2
    place = jnp.stack([lax.axis_index("dp"), chip, expert]).astype(jnp.int32)

    def to_x(block):
        return lax.ppermute(block, "dp", [(i, i ^ 1) for i in range(4)])

    def to_y(block):
        return lax.ppermute(block, "dp", [(i, i ^ 2) for i in range(4)])

    def hop(block, moves):
        return lax.ppermute(block, "expert", [(2 * a + c, 2 * b + c) for a, b in moves for c in (0, 1)])

    def swap(block, at=range(chips)):
        return lax.ppermute(block, "expert", [(2 * z + c, 2 * z + 1 - c) for z in at for c in (0, 1)])

    def line(own):
        two = hop(own, [(z, (z + 2) % 4) for z in range(4)])
        right = hop(own, [(0, 1), (1, 2), (2, 3)])
        left = hop(own, [(1, 0), (2, 1), (3, 2)])
        far = hop(two, [(2, 3), (1, 0)])
        return [own, two, right, left, far] + [
            swap(own), swap(two), swap(right, (1, 2, 3)), swap(left, (0, 1, 2)), swap(far, (0, 3))
        ]

    x_pieces = line(tokens)
    (y_own,) = call(
        functools.partial(prep_body, experts),
        [((tok, width + LANES), BF16, VMEM)],
        [(routes.T, VMEM), (gate_values.T, VMEM), (out_grad, VMEM)],
        [],
        1000,
        4 * tok * width,
    )
    y_pieces = line(y_own)

    wg0, wu0, wd0 = w_gate[0], w_up[0], w_down[0]
    wg1, wu1 = to_x(wg0), to_y(wu0)
    wg2, wu2 = to_y(wg0), to_x(wu0)
    wg3, wu3 = to_y(wg1), to_x(wu1)
    w_g, w_u = (wg0, wg1, wg2, wg3), (wu0, wu2, wu1, wu3)
    wd1, wd2 = to_x(wd0), to_y(wd0)
    wd3a, wd3b = to_x(wd2[:half]), to_y(wd1[half:])

    def dma(n):
        return pltpu.SemaphoreType.DMA((n,))

    weight = pltpu.VMEM((width, hidden), BF16)
    act, active, slope, x = call(
        pre_body,
        [
            ((rows, hidden), BF16, VMEM),
            ((rows, hidden), F32, VMEM),
            ((rows, hidden), F32, VMEM),
            ((rows, width), BF16, ANY),
        ],
        [(place, SMEM)] + [(a, ANY) for a in x_pieces] + [(a, ANY) for a in w_g + w_u],
        [pltpu.VMEM((rows, width), BF16), weight, weight, dma(17)],
        4 * rows * width * hidden,
        2 * (2 * rows * width + 2 * width * hidden) + 10 * rows * hidden,
    )
    piece = (2, half, share)
    send_a, keep_a, send_b, keep_b, y = call(
        functools.partial(down_body, experts),
        [(piece, BF16, VMEM)] * 4 + [((rows, width), BF16, ANY)],
        [(place, SMEM)] + [(a, ANY) for a in y_pieces] + [(act, VMEM)],
        [pltpu.VMEM((rows, width + LANES), BF16), pltpu.VMEM((rows, width), BF16), dma(9)],
        2 * rows * width * hidden,
        2 * (2 * rows * width + rows * hidden + width * hidden),
    )
    got_a, got_b = to_x(send_a), to_y(send_b)
    gate_delta, up_delta = call(
        back_body,
        [((rows, hidden), BF16, VMEM)] * 2,
        [(place, SMEM), (y, VMEM), (active, VMEM), (slope, VMEM)] + [(a, ANY) for a in (wd0, wd1, wd2, wd3a, wd3b)],
        [pltpu.VMEM((4, hidden, share), BF16), dma(5)],
        2 * rows * width * hidden,
        2 * (rows * width + width * hidden) + 12 * rows * hidden,
    )
    piece = (2, share, hidden)

    def grad(delta, send_pair, keep_pair):
        return call(
            functools.partial(grad_body, send_pair, keep_pair),
            [(piece, BF16, VMEM)] * 2,
            [(place, SMEM), (x, VMEM), (delta, VMEM)],
            [],
            2 * rows * width * hidden,
            2 * (rows * width + rows * hidden + width * hidden),
        )

    gate_send, gate_keep = grad(gate_delta, (1, 3), (0, 2))
    gate_got = to_x(gate_send)
    up_send, up_keep = grad(up_delta, (2, 3), (0, 1))
    up_got = to_y(up_send)
    weight = pltpu.VMEM((4, share, hidden), BF16)
    pair_send, pair_keep = call(
        pair_body,
        [((rows // 2, width), BF16, VMEM)] * 2,
        [(place, SMEM), (gate_delta, VMEM), (up_delta, VMEM)] + [(a, ANY) for a in w_g + w_u],
        [weight, weight, dma(8)],
        4 * rows * width * hidden,
        2 * (rows * width + 2 * rows * hidden + 2 * width * hidden),
    )
    down_a = add(keep_a[0], got_a[0]), to_y(add(keep_a[1], got_a[1]))
    down_b = add(keep_b[0], got_b[0]), to_x(add(keep_b[1], got_b[1]))
    down_grad = jnp.concatenate([add(*down_a), add(*down_b)], axis=0)
    gate_grad = add(add(gate_keep[0], gate_got[0]), to_y(add(gate_keep[1], gate_got[1])))
    up_grad = add(add(up_keep[0], up_got[0]), to_x(add(up_keep[1], up_got[1])))

    total = add(pair_keep, swap(pair_send)).reshape(chips, tok, width)
    far = hop(jnp.where(chip == 0, total[1], total[3]), [(3, 2), (0, 1)])
    right = hop(total[3], [(0, 1), (1, 2), (2, 3)])
    left = hop(total[1], [(1, 0), (2, 1), (3, 2)])
    two = hop(add(total[2], far), [(z, (z + 2) % 4) for z in range(4)])
    input_grad = add(total[0], right, left, two)
    return input_grad, gate_grad[None], up_grad[None], down_grad[None]


def routed(tokens, out_grad, routes, gate_values, w_gate, w_up, w_down):
    tok_rows, model_width = tokens.shape
    top_count = routes.shape[1]
    group_count = lax.axis_size("expert")
    local_count = w_gate.shape[0]
    expert_count = group_count * local_count
    hidden_units = w_gate.shape[2]
    capacity = slots_of(tok_rows, top_count, expert_count)
    pair_count = tok_rows * top_count
    slot_count = group_count * capacity
    expert_of = routes.reshape(-1)
    onehot = (expert_of[:, None] == jnp.arange(expert_count, dtype=jnp.int32)[None, :]).astype(
        jnp.int32
    )
    before = jnp.cumsum(onehot, axis=0) - onehot
    placed = jnp.sum(before * onehot, axis=1)
    slot_of = expert_of * capacity + placed
    slot_table = jnp.full((expert_count * capacity,), pair_count, jnp.int32)
    slot_table = slot_table.at[slot_of].set(jnp.arange(pair_count, dtype=jnp.int32))
    filled = slot_table < pair_count
    source = jnp.where(filled, slot_table, 0)
    owner_row = source // top_count
    send_x = jnp.where(filled[:, None], tokens[owner_row], jnp.zeros((), jnp.bfloat16))
    scaled = gate_values.reshape(-1)[source][:, None] * out_grad[owner_row].astype(jnp.float32)
    send_dy = jnp.where(filled[:, None], scaled, 0.0).astype(jnp.bfloat16)
    send_x = send_x.reshape(expert_count, capacity, model_width)
    send_dy = send_dy.reshape(expert_count, capacity, model_width)
    recv_x, recv_dy = (
        lax.all_to_all(send_x, "expert", split_axis=0, concat_axis=0, tiled=True),
        lax.all_to_all(send_dy, "expert", split_axis=0, concat_axis=0, tiled=True),
    )

    def to_local(stacked):
        shaped = stacked.reshape(group_count, local_count, capacity, model_width)
        return shaped.transpose(1, 0, 2, 3).reshape(local_count, slot_count, model_width)

    slot_x = to_local(recv_x)
    slot_dy = to_local(recv_dy)
    part_x = slot_x
    gate_term = jnp.einsum(
        "asd,adf->asf",
        part_x,
        lax.all_gather(w_gate, "dp", axis=1, tiled=True),
        preferred_element_type=jnp.float32,
    )
    up_term = jnp.einsum(
        "asd,adf->asf",
        part_x,
        lax.all_gather(w_up, "dp", axis=1, tiled=True),
        preferred_element_type=jnp.float32,
    )
    full_gate, full_up, full_down = (
        lax.all_gather(w_gate, "dp", axis=1, tiled=True),
        lax.all_gather(w_up, "dp", axis=1, tiled=True),
        lax.all_gather(w_down, "dp", axis=2, tiled=True),
    )
    sigma = jax.nn.sigmoid(gate_term)
    active = gate_term * sigma
    activated = (active * up_term).astype(jnp.bfloat16)
    back_hidden = jnp.einsum("asd,afd->asf", slot_dy, full_down, preferred_element_type=jnp.float32)
    up_delta = (back_hidden * active).astype(jnp.bfloat16)
    gate_delta = (back_hidden * up_term * sigma * (1.0 + gate_term * (1.0 - sigma))).astype(
        jnp.bfloat16
    )
    pair_grad = (
        jnp.einsum("asf,adf->asd", gate_delta, full_gate, preferred_element_type=jnp.float32)
        + jnp.einsum("asf,adf->asd", up_delta, full_up, preferred_element_type=jnp.float32)
    ).astype(jnp.bfloat16)
    send_back = pair_grad.reshape(local_count, group_count, capacity, model_width).transpose(
        1, 0, 2, 3
    )
    send_back = send_back.reshape(expert_count, capacity, model_width)
    returned = lax.all_to_all(send_back, "expert", split_axis=0, concat_axis=0, tiled=True)
    per_pair = returned.reshape(expert_count * capacity, model_width)[slot_of].astype(jnp.float32)
    input_grad = jnp.sum(per_pair.reshape(tok_rows, top_count, model_width), axis=1).astype(
        jnp.bfloat16
    )
    block_width = local_count * hidden_units
    share_width = model_width // lax.axis_size("dp")
    part_x = slot_x
    term_gate = jnp.einsum("asd,asf->daf", part_x, gate_delta, preferred_element_type=jnp.float32)
    term_up = jnp.einsum("asd,asf->daf", part_x, up_delta, preferred_element_type=jnp.float32)
    term_down = jnp.einsum("asd,asf->daf", slot_dy, activated, preferred_element_type=jnp.float32)
    shares = lax.psum_scatter(
        jnp.concatenate(
            [
                term_gate.reshape(lax.axis_size("dp") * share_width, block_width),
                term_up.reshape(lax.axis_size("dp") * share_width, block_width),
                term_down.reshape(lax.axis_size("dp") * share_width, block_width),
            ],
            axis=1,
        ).astype(jnp.bfloat16),
        "dp",
        scatter_dimension=0,
        tiled=True,
    ).astype(jnp.float32)
    share_rows = shares.shape[0]

    def unpack(which):
        return shares[:, which * block_width : (which + 1) * block_width].reshape(
            share_rows, local_count, hidden_units
        )

    gate_grad = unpack(0).transpose(1, 0, 2).astype(jnp.bfloat16)
    up_grad = unpack(1).transpose(1, 0, 2).astype(jnp.bfloat16)
    down_grad = unpack(2).transpose(1, 2, 0).astype(jnp.bfloat16)
    return (input_grad, gate_grad, up_grad, down_grad)


def lined(dp, expert):
    return dp == 4 and expert == 8


def local(tokens, out_grad, routes, gate_values, w_gate, w_up, w_down):
    experts = lax.axis_size("expert") * w_gate.shape[0]
    capacity = slots_of(tokens.shape[0], routes.shape[1], experts)
    fits = w_gate.shape[0] == 1 and tokens.shape[0] <= 2 * capacity
    if not (fits and lined(lax.axis_size("dp"), lax.axis_size("expert"))):
        return routed(tokens, out_grad, routes, gate_values, w_gate, w_up, w_down)
    return dense(tokens, out_grad, routes, gate_values, w_gate, w_up, w_down)


def solution(mesh):
    return jax.shard_map(
        local,
        mesh=mesh,
        in_specs=(
            P(("dp", "expert"), None),
            P(("dp", "expert"), None),
            P(("dp", "expert"), None),
            P(("dp", "expert"), None),
            P("expert", "dp", None),
            P("expert", "dp", None),
            P("expert", None, "dp"),
        ),
        out_specs=(
            P(("dp", "expert"), None),
            P("expert", "dp", None),
            P("expert", "dp", None),
            P("expert", None, "dp"),
        ),
        check_vma=False,
    )
```

```python
import functools

import jax
import jax.numpy as jnp
from jax import lax
from jax.experimental import pallas as pl
from jax.experimental.pallas import tpu as pltpu
from jax.sharding import PartitionSpec as P


F32 = jnp.float32
BF16 = jnp.bfloat16
ANY = pl.BlockSpec(memory_space=pl.ANY)
VMEM = pl.BlockSpec(memory_space=pltpu.VMEM)
SMEM = pl.BlockSpec(memory_space=pltpu.SMEM)
LIMIT = 24 * 1024 * 1024
LANES = 128
NN = (((1,), (0,)), ((), ()))
NT = (((1,), (1,)), ((), ()))


def mm(a, b, dims):
    return lax.dot_general(a, b, dims, preferred_element_type=F32)


def slots_of(tok_rows, top_count, expert_count):
    return min(tok_rows, max(2, 9 * tok_rows * top_count // (8 * expert_count)))


def call(body, outs, ins, scratch, flops, moved):
    return pl.pallas_call(
        body,
        out_shape=[jax.ShapeDtypeStruct(s, d) for s, d, _ in outs],
        in_specs=[s for _, s in ins],
        out_specs=[s for _, _, s in outs],
        scratch_shapes=scratch,
        compiler_params=pltpu.CompilerParams(vmem_limit_bytes=LIMIT),
        cost_estimate=pl.CostEstimate(flops=flops, bytes_accessed=moved, transcendentals=0),
    )(*[a for a, _ in ins])


def prep_body(experts, routes, gates, rows, out):
    tok, width = rows.shape
    line = lax.broadcasted_iota(jnp.int32, (LANES, tok), 0)
    term, named = line // experts, line % experts
    value = jnp.zeros((LANES, tok), F32)
    for k in range(routes.shape[0]):
        value += jnp.where(routes[k : k + 1, :] == named, gates[k : k + 1, :], 0.0)
    high = value.astype(BF16).astype(F32)
    mid = (value - high).astype(BF16).astype(F32)
    low = value - high - mid
    value = jnp.where(term == 0, high, jnp.where(term == 1, mid, jnp.where(term == 2, low, 0.0)))
    out[:, :width] = rows[...]
    out[:, width:] = jnp.transpose(value).astype(BF16)


class Copies:
    def __init__(self, sems):
        self.sems, self.used = sems, 0

    def start(self, src, dst):
        copy = pltpu.make_async_copy(src, dst, self.sems.at[self.used])
        self.used += 1
        copy.start()
        return copy

    def pick(self, first, src, other, dst):
        sem = self.sems.at[self.used]
        self.used += 1

        @pl.when(first)
        def _():
            pltpu.make_async_copy(src, dst, sem).start()

        @pl.when(jnp.logical_not(first))
        def _():
            pltpu.make_async_copy(other, dst, sem).start()

        return pltpu.make_async_copy(other, dst, sem)


def load_rows(copies, chip, pieces, dst):
    tok = pieces[0].shape[0]
    started = []
    for core in (0, 1):
        own, two, right, left, far = pieces[5 * core : 5 * core + 5]
        at = [dst.at[pl.ds((4 * core + s) * tok, tok)] for s in range(4)]
        started.append(copies.start(own, at[0]))
        started.append(copies.pick(chip == 0, far, right, at[1]))
        started.append(copies.start(two, at[2]))
        started.append(copies.pick(chip == 3, far, left, at[3]))
    return started


def pre_body(place, *refs):
    pieces, w_gate, w_up = refs[:10], refs[10:14], refs[14:18]
    act, active_out, slope_out, x_out, x, wg, wu, sems = refs[18:]
    me, chip = place[0], place[1]
    copies = Copies(sems)
    rows = load_rows(copies, chip, pieces, x)
    share, hidden = w_gate[0].shape
    weights = []
    for k in range(4):
        at = pl.ds((me ^ k) * share, share)
        weights += [copies.start(w_gate[k], wg.at[at]), copies.start(w_up[k], wu.at[at])]
    for c in rows:
        c.wait()
    out = copies.start(x, x_out)
    for c in weights:
        c.wait()
    tm, tn = x.shape[0] // 2, 256

    def step(i, _):
        r = pl.ds(pl.multiple_of(i // (hidden // tn) * tm, tm), tm)
        c = pl.ds(pl.multiple_of(i % (hidden // tn) * tn, tn), tn)
        lhs = x[r, :]
        gate = mm(lhs, wg[:, c], NN)
        up = mm(lhs, wu[:, c], NN)
        sigma = jax.nn.sigmoid(gate)
        active = gate * sigma
        act[r, c] = (active * up).astype(BF16)
        active_out[r, c] = active
        slope_out[r, c] = up * sigma * (1.0 + gate * (1.0 - sigma))
        return 0

    lax.fori_loop(0, 2 * (hidden // tn), step, 0)
    out.wait()


def down_send_body(experts, place, *refs):
    pieces, act = refs[:10], refs[10]
    send_a, send_b, y, raw, sems = refs[11:]
    chip, expert = place[1], place[2]
    copies = Copies(sems)
    for c in load_rows(copies, chip, pieces, raw):
        c.wait()
    rows, width = y.shape
    tok = rows // 8
    lane = lax.broadcasted_iota(jnp.int32, (tok, LANES), 1)
    mine = jnp.logical_and(lane % experts == expert, lane < 3 * experts)

    def scale(i, _):
        r = pl.ds(pl.multiple_of(i * tok, tok), tok)
        gate = jnp.sum(jnp.where(mine, raw[r, width:].astype(F32), 0.0), axis=1, keepdims=True)
        y[r, :] = (raw[r, :width].astype(F32) * gate).astype(BF16)
        return 0

    lax.fori_loop(0, 8, scale, 0)
    down_blocks(place, act, y, ((0, 1, send_a, 0), (0, 3, send_a, 1), (1, 2, send_b, 0), (1, 3, send_b, 1)))


def down_blocks(place, act, y, wanted):
    share = y.shape[1] // 4
    half = act.shape[1] // 2
    for h in (0, 1):
        turned = jnp.transpose(act[:, h * half : (h + 1) * half])
        for which, k, dst, slot in wanted:
            if which == h:
                cols = pl.ds(pl.multiple_of((place[0] ^ k) * share, share), share)
                value = mm(turned, y[:, cols], NN).astype(BF16)
                if slot is None:
                    dst[...] = value
                else:
                    dst[slot] = value


def down_keep_body(place, act, y, a0, a1, b0, b1):
    down_blocks(place, act, y, ((0, 0, a0, None), (0, 2, a1, None), (1, 0, b0, None), (1, 1, b1, None)))


def back_body(place, y, active, slope, own, from_x, from_y, diag_a, diag_b, gate_delta, up_delta, w, sems):
    me = place[0]
    copies = Copies(sems)
    hidden, share = own.shape
    half = hidden // 2
    started = []
    for k, src in ((0, own), (1, from_x), (2, from_y)):
        started.append(copies.start(src, w.at[me ^ k]))
    started.append(copies.start(diag_a, w.at[me ^ 3, pl.ds(0, half)]))
    started.append(copies.start(diag_b, w.at[me ^ 3, pl.ds(half, half)]))
    for c in started:
        c.wait()
    rows = y.shape[0]
    tm, tn = rows // 2, 256

    def step(i, _):
        r = pl.ds(pl.multiple_of(i // (hidden // tn) * tm, tm), tm)
        c = pl.ds(pl.multiple_of(i % (hidden // tn) * tn, tn), tn)
        back = mm(y[r, 0:share], w[0, c, :], NT)
        for j in range(1, 4):
            back += mm(y[r, j * share : (j + 1) * share], w[j, c, :], NT)
        up_delta[r, c] = (back * active[r, c]).astype(BF16)
        gate_delta[r, c] = (back * slope[r, c]).astype(BF16)
        return 0

    lax.fori_loop(0, 2 * (hidden // tn), step, 0)


def grad_blocks(place, x, wanted):
    share = x.shape[1] // 4
    tm = share // 2
    for k, targets in wanted:

        def step(i, _, k=k, targets=targets):
            cols = pl.ds(pl.multiple_of((place[0] ^ k) * share + i * tm, tm), tm)
            turned = jnp.transpose(x[:, cols])
            part = pl.ds(pl.multiple_of(i * tm, tm), tm)
            for delta, dst, slot in targets:
                value = mm(turned, delta[...], NN).astype(BF16)
                if slot is None:
                    dst[part, :] = value
                else:
                    dst[slot, part, :] = value
            return 0

        lax.fori_loop(0, 2, step, 0)


def grad_send_body(place, x, gd, ud, gate_send, up_send):
    grad_blocks(
        place, x, ((1, [(gd, gate_send, 0)]), (3, [(gd, gate_send, 1), (ud, up_send, 1)]), (2, [(ud, up_send, 0)]))
    )


def grad_keep_body(place, x, gd, ud, g0, g1, u0, u1):
    grad_blocks(place, x, ((2, [(gd, g1, None)]), (1, [(ud, u1, None)]), (0, [(gd, g0, None), (ud, u0, None)])))


def pair_body(place, gate_delta, up_delta, *refs):
    w_gate, w_up = refs[:4], refs[4:8]
    send, keep, wg, wu, sems = refs[8:]
    me = place[0]
    copies = Copies(sems)
    started = []
    for k in range(4):
        started.append((copies.start(w_gate[k], wg.at[k]), copies.start(w_up[k], wu.at[k])))
    share = wg.shape[1]
    tn = share // 2
    rows = keep.shape[0]
    for k in range(4):
        for c in started[k]:
            c.wait()

        def step(i, _, k=k):
            part = pl.ds(pl.multiple_of(i * tn, tn), tn)
            total = mm(gate_delta[...], wg[k, part, :], NT) + mm(up_delta[...], wu[k, part, :], NT)
            cols = pl.ds(pl.multiple_of((me ^ k) * share + i * tn, tn), tn)
            keep[:, cols] = total[:rows].astype(BF16)
            send[:, cols] = total[rows:].astype(BF16)
            return 0

        lax.fori_loop(0, 2, step, 0)


def add(*terms):
    total = terms[0].astype(F32)
    for term in terms[1:]:
        total = total + term.astype(F32)
    return total.astype(BF16)


def dense(tokens, out_grad, routes, gate_values, w_gate, w_up, w_down):
    tok, width = tokens.shape
    experts = lax.axis_size("expert")
    chips = experts // 2
    hidden = w_gate.shape[2]
    share = width // 4
    half = hidden // 2
    rows = experts * tok
    expert = lax.axis_index("expert")
    chip = expert // 2
    place = jnp.stack([lax.axis_index("dp"), chip, expert]).astype(jnp.int32)

    def to_x(block):
        return lax.ppermute(block, "dp", [(i, i ^ 1) for i in range(4)])

    def to_y(block):
        return lax.ppermute(block, "dp", [(i, i ^ 2) for i in range(4)])

    def hop(block, moves):
        return lax.ppermute(block, "expert", [(2 * a + c, 2 * b + c) for a, b in moves for c in (0, 1)])

    def swap(block, at=range(chips)):
        return lax.ppermute(block, "expert", [(2 * z + c, 2 * z + 1 - c) for z in at for c in (0, 1)])

    def line(own):
        two = hop(own, [(z, (z + 2) % 4) for z in range(4)])
        right = hop(own, [(0, 1), (1, 2), (2, 3)])
        left = hop(own, [(1, 0), (2, 1), (3, 2)])
        far = hop(two, [(2, 3), (1, 0)])
        return [own, two, right, left, far] + [
            swap(own), swap(two), swap(right, (1, 2, 3)), swap(left, (0, 1, 2)), swap(far, (0, 3))
        ]

    x_pieces = line(tokens)
    (y_own,) = call(
        functools.partial(prep_body, experts),
        [((tok, width + LANES), BF16, VMEM)],
        [(routes.T, VMEM), (gate_values.T, VMEM), (out_grad, VMEM)],
        [],
        1000,
        4 * tok * width,
    )
    y_pieces = line(y_own)

    wg0, wu0, wd0 = w_gate[0], w_up[0], w_down[0]
    wg1, wu1 = to_x(wg0), to_y(wu0)
    wg2, wu2 = to_y(wg0), to_x(wu0)
    wg3, wu3 = to_y(wg1), to_x(wu1)
    w_g, w_u = (wg0, wg1, wg2, wg3), (wu0, wu2, wu1, wu3)
    wd1, wd2 = to_x(wd0), to_y(wd0)
    wd3a, wd3b = to_x(wd2[:half]), to_y(wd1[half:])

    def dma(n):
        return pltpu.SemaphoreType.DMA((n,))

    weight = pltpu.VMEM((width, hidden), BF16)
    act, active, slope, x = call(
        pre_body,
        [
            ((rows, hidden), BF16, VMEM),
            ((rows, hidden), F32, VMEM),
            ((rows, hidden), F32, VMEM),
            ((rows, width), BF16, ANY),
        ],
        [(place, SMEM)] + [(a, ANY) for a in x_pieces] + [(a, ANY) for a in w_g + w_u],
        [pltpu.VMEM((rows, width), BF16), weight, weight, dma(17)],
        4 * rows * width * hidden,
        2 * (2 * rows * width + 2 * width * hidden) + 10 * rows * hidden,
    )
    piece = (2, half, share)
    send_a, send_b, y = call(
        functools.partial(down_send_body, experts),
        [(piece, BF16, VMEM)] * 2 + [((rows, width), BF16, VMEM)],
        [(place, SMEM)] + [(a, ANY) for a in y_pieces] + [(act, VMEM)],
        [pltpu.VMEM((rows, width + LANES), BF16), dma(8)],
        rows * width * hidden,
        2 * (2 * rows * width + rows * hidden + width * hidden // 2),
    )
    got_a, got_b = to_x(send_a), to_y(send_b)
    gate_delta, up_delta = call(
        back_body,
        [((rows, hidden), BF16, VMEM)] * 2,
        [(place, SMEM), (y, VMEM), (active, VMEM), (slope, VMEM)] + [(a, ANY) for a in (wd0, wd1, wd2, wd3a, wd3b)],
        [pltpu.VMEM((4, hidden, share), BF16), dma(5)],
        2 * rows * width * hidden,
        2 * (rows * width + width * hidden) + 12 * rows * hidden,
    )
    gate_send, up_send = call(
        grad_send_body,
        [((2, share, hidden), BF16, VMEM)] * 2,
        [(place, SMEM), (x, VMEM), (gate_delta, VMEM), (up_delta, VMEM)],
        [],
        2 * rows * width * hidden,
        2 * (rows * width + 2 * rows * hidden + width * hidden),
    )
    gate_got, up_got = to_x(gate_send), to_y(up_send)
    weight = pltpu.VMEM((4, share, hidden), BF16)
    pair_send, pair_keep = call(
        pair_body,
        [((rows // 2, width), BF16, VMEM)] * 2,
        [(place, SMEM), (gate_delta, VMEM), (up_delta, VMEM)] + [(a, ANY) for a in w_g + w_u],
        [weight, weight, dma(8)],
        4 * rows * width * hidden,
        2 * (rows * width + 2 * rows * hidden + 2 * width * hidden),
    )
    total = add(pair_keep, swap(pair_send)).reshape(chips, tok, width)
    keep_a0, keep_a1, keep_b0, keep_b1 = call(
        down_keep_body,
        [((half, share), BF16, VMEM)] * 4,
        [(place, SMEM), (act, VMEM), (y, VMEM)],
        [],
        rows * width * hidden,
        2 * (rows * width + rows * hidden + width * hidden // 2),
    )
    gate0, gate1, up0, up1 = call(
        grad_keep_body,
        [((share, hidden), BF16, VMEM)] * 4,
        [(place, SMEM), (x, VMEM), (gate_delta, VMEM), (up_delta, VMEM)],
        [],
        2 * rows * width * hidden,
        2 * (rows * width + 2 * rows * hidden + width * hidden),
    )
    down_a, down_b = to_y(add(keep_a1, got_a[1])), to_x(add(keep_b1, got_b[1]))
    gate_last = to_y(add(gate1, gate_got[1]))
    up_last = to_x(add(up1, up_got[1]))
    gate_sum, up_sum = lax.optimization_barrier((add(gate0, gate_got[0]), add(up0, up_got[0])))
    down_grad = jnp.concatenate([add(keep_a0, got_a[0], down_a), add(keep_b0, got_b[0], down_b)], axis=0)
    gate_grad, up_grad = add(gate_sum, gate_last), add(up_sum, up_last)

    far = hop(jnp.where(chip == 0, total[1], total[3]), [(3, 2), (0, 1)])
    right = hop(total[3], [(0, 1), (1, 2), (2, 3)])
    left = hop(total[1], [(1, 0), (2, 1), (3, 2)])
    two = hop(add(total[2], far), [(z, (z + 2) % 4) for z in range(4)])
    input_grad = add(total[0], right, left, two)
    return input_grad, gate_grad[None], up_grad[None], down_grad[None]


def routed(tokens, out_grad, routes, gate_values, w_gate, w_up, w_down):
    tok_rows, model_width = tokens.shape
    top_count = routes.shape[1]
    group_count = lax.axis_size("expert")
    local_count = w_gate.shape[0]
    expert_count = group_count * local_count
    hidden_units = w_gate.shape[2]
    capacity = slots_of(tok_rows, top_count, expert_count)
    pair_count = tok_rows * top_count
    slot_count = group_count * capacity
    expert_of = routes.reshape(-1)
    onehot = (expert_of[:, None] == jnp.arange(expert_count, dtype=jnp.int32)[None, :]).astype(
        jnp.int32
    )
    before = jnp.cumsum(onehot, axis=0) - onehot
    placed = jnp.sum(before * onehot, axis=1)
    slot_of = expert_of * capacity + placed
    slot_table = jnp.full((expert_count * capacity,), pair_count, jnp.int32)
    slot_table = slot_table.at[slot_of].set(jnp.arange(pair_count, dtype=jnp.int32))
    filled = slot_table < pair_count
    source = jnp.where(filled, slot_table, 0)
    owner_row = source // top_count
    send_x = jnp.where(filled[:, None], tokens[owner_row], jnp.zeros((), jnp.bfloat16))
    scaled = gate_values.reshape(-1)[source][:, None] * out_grad[owner_row].astype(jnp.float32)
    send_dy = jnp.where(filled[:, None], scaled, 0.0).astype(jnp.bfloat16)
    send_x = send_x.reshape(expert_count, capacity, model_width)
    send_dy = send_dy.reshape(expert_count, capacity, model_width)
    recv_x, recv_dy = (
        lax.all_to_all(send_x, "expert", split_axis=0, concat_axis=0, tiled=True),
        lax.all_to_all(send_dy, "expert", split_axis=0, concat_axis=0, tiled=True),
    )

    def to_local(stacked):
        shaped = stacked.reshape(group_count, local_count, capacity, model_width)
        return shaped.transpose(1, 0, 2, 3).reshape(local_count, slot_count, model_width)

    slot_x = to_local(recv_x)
    slot_dy = to_local(recv_dy)
    part_x = slot_x
    gate_term = jnp.einsum(
        "asd,adf->asf",
        part_x,
        lax.all_gather(w_gate, "dp", axis=1, tiled=True),
        preferred_element_type=jnp.float32,
    )
    up_term = jnp.einsum(
        "asd,adf->asf",
        part_x,
        lax.all_gather(w_up, "dp", axis=1, tiled=True),
        preferred_element_type=jnp.float32,
    )
    full_gate, full_up, full_down = (
        lax.all_gather(w_gate, "dp", axis=1, tiled=True),
        lax.all_gather(w_up, "dp", axis=1, tiled=True),
        lax.all_gather(w_down, "dp", axis=2, tiled=True),
    )
    sigma = jax.nn.sigmoid(gate_term)
    active = gate_term * sigma
    activated = (active * up_term).astype(jnp.bfloat16)
    back_hidden = jnp.einsum("asd,afd->asf", slot_dy, full_down, preferred_element_type=jnp.float32)
    up_delta = (back_hidden * active).astype(jnp.bfloat16)
    gate_delta = (back_hidden * up_term * sigma * (1.0 + gate_term * (1.0 - sigma))).astype(
        jnp.bfloat16
    )
    pair_grad = (
        jnp.einsum("asf,adf->asd", gate_delta, full_gate, preferred_element_type=jnp.float32)
        + jnp.einsum("asf,adf->asd", up_delta, full_up, preferred_element_type=jnp.float32)
    ).astype(jnp.bfloat16)
    send_back = pair_grad.reshape(local_count, group_count, capacity, model_width).transpose(
        1, 0, 2, 3
    )
    send_back = send_back.reshape(expert_count, capacity, model_width)
    returned = lax.all_to_all(send_back, "expert", split_axis=0, concat_axis=0, tiled=True)
    per_pair = returned.reshape(expert_count * capacity, model_width)[slot_of].astype(jnp.float32)
    input_grad = jnp.sum(per_pair.reshape(tok_rows, top_count, model_width), axis=1).astype(
        jnp.bfloat16
    )
    block_width = local_count * hidden_units
    share_width = model_width // lax.axis_size("dp")
    part_x = slot_x
    term_gate = jnp.einsum("asd,asf->daf", part_x, gate_delta, preferred_element_type=jnp.float32)
    term_up = jnp.einsum("asd,asf->daf", part_x, up_delta, preferred_element_type=jnp.float32)
    term_down = jnp.einsum("asd,asf->daf", slot_dy, activated, preferred_element_type=jnp.float32)
    shares = lax.psum_scatter(
        jnp.concatenate(
            [
                term_gate.reshape(lax.axis_size("dp") * share_width, block_width),
                term_up.reshape(lax.axis_size("dp") * share_width, block_width),
                term_down.reshape(lax.axis_size("dp") * share_width, block_width),
            ],
            axis=1,
        ).astype(jnp.bfloat16),
        "dp",
        scatter_dimension=0,
        tiled=True,
    ).astype(jnp.float32)
    share_rows = shares.shape[0]

    def unpack(which):
        return shares[:, which * block_width : (which + 1) * block_width].reshape(
            share_rows, local_count, hidden_units
        )

    gate_grad = unpack(0).transpose(1, 0, 2).astype(jnp.bfloat16)
    up_grad = unpack(1).transpose(1, 0, 2).astype(jnp.bfloat16)
    down_grad = unpack(2).transpose(1, 2, 0).astype(jnp.bfloat16)
    return (input_grad, gate_grad, up_grad, down_grad)


def lined(dp, expert):
    return dp == 4 and expert == 8


def local(tokens, out_grad, routes, gate_values, w_gate, w_up, w_down):
    experts = lax.axis_size("expert") * w_gate.shape[0]
    capacity = slots_of(tokens.shape[0], routes.shape[1], experts)
    fits = w_gate.shape[0] == 1 and tokens.shape[0] <= 2 * capacity
    if not (fits and lined(lax.axis_size("dp"), lax.axis_size("expert"))):
        return routed(tokens, out_grad, routes, gate_values, w_gate, w_up, w_down)
    return dense(tokens, out_grad, routes, gate_values, w_gate, w_up, w_down)


def solution(mesh):
    return jax.shard_map(
        local,
        mesh=mesh,
        in_specs=(
            P(("dp", "expert"), None),
            P(("dp", "expert"), None),
            P(("dp", "expert"), None),
            P(("dp", "expert"), None),
            P("expert", "dp", None),
            P("expert", "dp", None),
            P("expert", None, "dp"),
        ),
        out_specs=(
            P(("dp", "expert"), None),
            P("expert", "dp", None),
            P("expert", "dp", None),
            P("expert", None, "dp"),
        ),
        check_vma=False,
    )
```

```python
import functools

import jax
import jax.numpy as jnp
from jax import lax
from jax.experimental import pallas as pl
from jax.experimental.pallas import tpu as pltpu
from jax.sharding import PartitionSpec as P


F32 = jnp.float32
BF16 = jnp.bfloat16
ANY = pl.BlockSpec(memory_space=pl.ANY)
VMEM = pl.BlockSpec(memory_space=pltpu.VMEM)
SMEM = pl.BlockSpec(memory_space=pltpu.SMEM)
LIMIT = 24 * 1024 * 1024
LANES = 128
NN = (((1,), (0,)), ((), ()))
NT = (((1,), (1,)), ((), ()))


def mm(a, b, dims):
    return lax.dot_general(a, b, dims, preferred_element_type=F32)


def slots_of(tok_rows, top_count, expert_count):
    return min(tok_rows, max(2, 9 * tok_rows * top_count // (8 * expert_count)))


def call(body, outs, ins, scratch, flops, moved):
    return pl.pallas_call(
        body,
        out_shape=[jax.ShapeDtypeStruct(s, d) for s, d, _ in outs],
        in_specs=[s for _, s in ins],
        out_specs=[s for _, _, s in outs],
        scratch_shapes=scratch,
        compiler_params=pltpu.CompilerParams(vmem_limit_bytes=LIMIT),
        cost_estimate=pl.CostEstimate(flops=flops, bytes_accessed=moved, transcendentals=0),
    )(*[a for a, _ in ins])


TWO = ((0, 2), (1, 3), (2, 0), (3, 1))
OUTER = ((0, 1), (1, 0), (2, 3), (3, 2))
INNER = ((1, 2), (2, 1))


def prep_body(experts, routes, gates, rows, out):
    tok, width = rows.shape
    line = lax.broadcasted_iota(jnp.int32, (LANES, tok), 0)
    term, named = line // experts, line % experts
    value = jnp.zeros((LANES, tok), F32)
    for k in range(routes.shape[0]):
        value += jnp.where(routes[k : k + 1, :] == named, gates[k : k + 1, :], 0.0)
    high = value.astype(BF16).astype(F32)
    mid = (value - high).astype(BF16).astype(F32)
    low = value - high - mid
    value = jnp.where(term == 0, high, jnp.where(term == 1, mid, jnp.where(term == 2, low, 0.0)))
    out[:, :width] = rows[...]
    out[:, width:] = jnp.transpose(value).astype(BF16)


class Copies:
    def __init__(self, sems):
        self.sems, self.used = sems, 0

    def start(self, src, dst):
        copy = pltpu.make_async_copy(src, dst, self.sems.at[self.used])
        self.used += 1
        copy.start()
        return copy

    def pick(self, first, src, other, dst):
        sem = self.sems.at[self.used]
        self.used += 1

        @pl.when(first)
        def _():
            pltpu.make_async_copy(src, dst, sem).start()

        @pl.when(jnp.logical_not(first))
        def _():
            pltpu.make_async_copy(other, dst, sem).start()

        return pltpu.make_async_copy(other, dst, sem)


def load_rows(copies, chip, pieces, dst):
    tok = pieces[0].shape[0]
    middle = jnp.logical_or(chip == 1, chip == 2)
    started = []
    for core in (0, 1):
        own, two, outer, inner, far = pieces[5 * core : 5 * core + 5]
        at = [dst.at[pl.ds((4 * core + s) * tok, tok)] for s in range(4)]
        for src, to in zip((own, two, outer), at):
            started.append(copies.start(src, to))
        started.append(copies.pick(middle, inner, far, at[3]))
    return started


def pre_body(place, *refs):
    pieces, w_gate, w_up = refs[:10], refs[10:14], refs[14:18]
    act, active_out, slope_out, x_out, x, wg, wu, sems = refs[18:]
    me, chip = place[0], place[1]
    copies = Copies(sems)
    rows = load_rows(copies, chip, pieces, x)
    share, hidden = w_gate[0].shape
    weights = []
    for k in range(4):
        at = pl.ds((me ^ k) * share, share)
        weights += [copies.start(w_gate[k], wg.at[at]), copies.start(w_up[k], wu.at[at])]
    for c in rows:
        c.wait()
    out = copies.start(x, x_out)
    for c in weights:
        c.wait()
    tm, tn = x.shape[0] // 2, 256

    def step(i, _):
        r = pl.ds(pl.multiple_of(i // (hidden // tn) * tm, tm), tm)
        c = pl.ds(pl.multiple_of(i % (hidden // tn) * tn, tn), tn)
        lhs = x[r, :]
        gate = mm(lhs, wg[:, c], NN)
        up = mm(lhs, wu[:, c], NN)
        sigma = jax.nn.sigmoid(gate)
        active = gate * sigma
        act[r, c] = (active * up).astype(BF16)
        active_out[r, c] = active
        slope_out[r, c] = up * sigma * (1.0 + gate * (1.0 - sigma))
        return 0

    lax.fori_loop(0, 2 * (hidden // tn), step, 0)
    out.wait()


def down_send_body(experts, place, *refs):
    pieces, act = refs[:10], refs[10]
    send_a, send_b, y, raw, sems = refs[11:]
    chip, expert = place[1], place[2]
    copies = Copies(sems)
    for c in load_rows(copies, chip, pieces, raw):
        c.wait()
    rows, width = y.shape
    tok = rows // 8
    lane = lax.broadcasted_iota(jnp.int32, (tok, LANES), 1)
    mine = jnp.logical_and(lane % experts == expert, lane < 3 * experts)

    def scale(i, _):
        r = pl.ds(pl.multiple_of(i * tok, tok), tok)
        gate = jnp.sum(jnp.where(mine, raw[r, width:].astype(F32), 0.0), axis=1, keepdims=True)
        y[r, :] = (raw[r, :width].astype(F32) * gate).astype(BF16)
        return 0

    lax.fori_loop(0, 8, scale, 0)
    down_blocks(place, act, y, ((0, 1, send_a, 0), (0, 3, send_a, 1), (1, 2, send_b, 0), (1, 3, send_b, 1)))


def down_blocks(place, act, y, wanted):
    share = y.shape[1] // 4
    half = act.shape[1] // 2
    for h in (0, 1):
        turned = jnp.transpose(act[:, h * half : (h + 1) * half])
        for which, k, dst, slot in wanted:
            if which == h:
                cols = pl.ds(pl.multiple_of((place[0] ^ k) * share, share), share)
                value = mm(turned, y[:, cols], NN).astype(BF16)
                if slot is None:
                    dst[...] = value
                else:
                    dst[slot] = value


def down_keep_body(place, act, y, a0, a1, b0, b1):
    down_blocks(place, act, y, ((0, 0, a0, None), (0, 2, a1, None), (1, 0, b0, None), (1, 1, b1, None)))


def back_body(place, y, active, slope, own, from_x, from_y, diag_a, diag_b, gate_delta, up_delta, w, sems):
    me = place[0]
    copies = Copies(sems)
    hidden, share = own.shape
    half = hidden // 2
    started = []
    for k, src in ((0, own), (1, from_x), (2, from_y)):
        started.append(copies.start(src, w.at[me ^ k]))
    started.append(copies.start(diag_a, w.at[me ^ 3, pl.ds(0, half)]))
    started.append(copies.start(diag_b, w.at[me ^ 3, pl.ds(half, half)]))
    for c in started:
        c.wait()
    rows = y.shape[0]
    tm, tn = rows // 2, 256

    def step(i, _):
        r = pl.ds(pl.multiple_of(i // (hidden // tn) * tm, tm), tm)
        c = pl.ds(pl.multiple_of(i % (hidden // tn) * tn, tn), tn)
        back = mm(y[r, 0:share], w[0, c, :], NT)
        for j in range(1, 4):
            back += mm(y[r, j * share : (j + 1) * share], w[j, c, :], NT)
        up_delta[r, c] = (back * active[r, c]).astype(BF16)
        gate_delta[r, c] = (back * slope[r, c]).astype(BF16)
        return 0

    lax.fori_loop(0, 2 * (hidden // tn), step, 0)


def grad_blocks(place, x, wanted):
    share = x.shape[1] // 4
    tm = share // 2
    for k, targets in wanted:

        def step(i, _, k=k, targets=targets):
            cols = pl.ds(pl.multiple_of((place[0] ^ k) * share + i * tm, tm), tm)
            turned = jnp.transpose(x[:, cols])
            part = pl.ds(pl.multiple_of(i * tm, tm), tm)
            for delta, dst, slot in targets:
                value = mm(turned, delta[...], NN).astype(BF16)
                if slot is None:
                    dst[part, :] = value
                else:
                    dst[slot, part, :] = value
            return 0

        lax.fori_loop(0, 2, step, 0)


def grad_send_body(place, x, gd, ud, gate_send, up_send):
    grad_blocks(
        place, x, ((1, [(gd, gate_send, 0)]), (3, [(gd, gate_send, 1), (ud, up_send, 1)]), (2, [(ud, up_send, 0)]))
    )


def grad_keep_body(place, x, gd, ud, g0, g1, u0, u1):
    grad_blocks(place, x, ((2, [(gd, g1, None)]), (1, [(ud, u1, None)]), (0, [(gd, g0, None), (ud, u0, None)])))


def pair_body(place, gate_delta, up_delta, *refs):
    w_gate, w_up = refs[:4], refs[4:8]
    send, keep, wg, wu, sems = refs[8:]
    me = place[0]
    copies = Copies(sems)
    started = []
    for k in range(4):
        started.append((copies.start(w_gate[k], wg.at[k]), copies.start(w_up[k], wu.at[k])))
    share = wg.shape[1]
    tn = share // 2
    rows = keep.shape[0]
    for k in range(4):
        for c in started[k]:
            c.wait()

        def step(i, _, k=k):
            part = pl.ds(pl.multiple_of(i * tn, tn), tn)
            total = mm(gate_delta[...], wg[k, part, :], NT) + mm(up_delta[...], wu[k, part, :], NT)
            cols = pl.ds(pl.multiple_of((me ^ k) * share + i * tn, tn), tn)
            keep[:, cols] = total[:rows].astype(BF16)
            send[:, cols] = total[rows:].astype(BF16)
            return 0

        lax.fori_loop(0, 2, step, 0)


def add(*terms):
    total = terms[0].astype(F32)
    for term in terms[1:]:
        total = total + term.astype(F32)
    return total.astype(BF16)


def dense(tokens, out_grad, routes, gate_values, w_gate, w_up, w_down):
    tok, width = tokens.shape
    experts = lax.axis_size("expert")
    chips = experts // 2
    hidden = w_gate.shape[2]
    share = width // 4
    half = hidden // 2
    rows = experts * tok
    expert = lax.axis_index("expert")
    chip = expert // 2
    place = jnp.stack([lax.axis_index("dp"), chip, expert]).astype(jnp.int32)

    def to_x(block):
        return lax.ppermute(block, "dp", [(i, i ^ 1) for i in range(4)])

    def to_y(block):
        return lax.ppermute(block, "dp", [(i, i ^ 2) for i in range(4)])

    def hop(block, moves):
        return lax.ppermute(block, "expert", [(2 * a + c, 2 * b + c) for a, b in moves for c in (0, 1)])

    def swap(block, at=range(chips)):
        return lax.ppermute(block, "expert", [(2 * z + c, 2 * z + 1 - c) for z in at for c in (0, 1)])

    def line(own):
        two = hop(own, TWO)
        outer = hop(own, OUTER)
        inner = hop(own, INNER)
        far = hop(two, ((2, 3), (1, 0)))
        return [own, two, outer, inner, far] + [
            swap(own), swap(two), swap(outer), swap(inner, (1, 2)), swap(far, (0, 3))
        ]

    x_pieces = line(tokens)
    (y_own,) = call(
        functools.partial(prep_body, experts),
        [((tok, width + LANES), BF16, VMEM)],
        [(routes.T, VMEM), (gate_values.T, VMEM), (out_grad, VMEM)],
        [],
        1000,
        4 * tok * width,
    )
    y_pieces = line(y_own)

    wg0, wu0, wd0 = w_gate[0], w_up[0], w_down[0]
    wg1, wu1 = to_x(wg0), to_y(wu0)
    wg2, wu2 = to_y(wg0), to_x(wu0)
    wg3, wu3 = to_y(wg1), to_x(wu1)
    w_g, w_u = (wg0, wg1, wg2, wg3), (wu0, wu2, wu1, wu3)
    wd1, wd2 = to_x(wd0), to_y(wd0)
    wd3a, wd3b = to_x(wd2[:half]), to_y(wd1[half:])

    def dma(n):
        return pltpu.SemaphoreType.DMA((n,))

    weight = pltpu.VMEM((width, hidden), BF16)
    act, active, slope, x = call(
        pre_body,
        [
            ((rows, hidden), BF16, VMEM),
            ((rows, hidden), F32, VMEM),
            ((rows, hidden), F32, VMEM),
            ((rows, width), BF16, ANY),
        ],
        [(place, SMEM)] + [(a, ANY) for a in x_pieces] + [(a, ANY) for a in w_g + w_u],
        [pltpu.VMEM((rows, width), BF16), weight, weight, dma(17)],
        4 * rows * width * hidden,
        2 * (2 * rows * width + 2 * width * hidden) + 10 * rows * hidden,
    )
    piece = (2, half, share)
    send_a, send_b, y = call(
        functools.partial(down_send_body, experts),
        [(piece, BF16, VMEM)] * 2 + [((rows, width), BF16, VMEM)],
        [(place, SMEM)] + [(a, ANY) for a in y_pieces] + [(act, VMEM)],
        [pltpu.VMEM((rows, width + LANES), BF16), dma(8)],
        rows * width * hidden,
        2 * (2 * rows * width + rows * hidden + width * hidden // 2),
    )
    got_a, got_b = to_x(send_a), to_y(send_b)
    gate_delta, up_delta = call(
        back_body,
        [((rows, hidden), BF16, VMEM)] * 2,
        [(place, SMEM), (y, VMEM), (active, VMEM), (slope, VMEM)] + [(a, ANY) for a in (wd0, wd1, wd2, wd3a, wd3b)],
        [pltpu.VMEM((4, hidden, share), BF16), dma(5)],
        2 * rows * width * hidden,
        2 * (rows * width + width * hidden) + 12 * rows * hidden,
    )
    gate_send, up_send = call(
        grad_send_body,
        [((2, share, hidden), BF16, VMEM)] * 2,
        [(place, SMEM), (x, VMEM), (gate_delta, VMEM), (up_delta, VMEM)],
        [],
        2 * rows * width * hidden,
        2 * (rows * width + 2 * rows * hidden + width * hidden),
    )
    gate_got, up_got = to_x(gate_send), to_y(up_send)
    weight = pltpu.VMEM((4, share, hidden), BF16)
    pair_send, pair_keep = call(
        pair_body,
        [((rows // 2, width), BF16, VMEM)] * 2,
        [(place, SMEM), (gate_delta, VMEM), (up_delta, VMEM)] + [(a, ANY) for a in w_g + w_u],
        [weight, weight, dma(8)],
        4 * rows * width * hidden,
        2 * (rows * width + 2 * rows * hidden + 2 * width * hidden),
    )
    total = add(pair_keep, swap(pair_send)).reshape(chips, tok, width)
    keep_a0, keep_a1, keep_b0, keep_b1 = call(
        down_keep_body,
        [((half, share), BF16, VMEM)] * 4,
        [(place, SMEM), (act, VMEM), (y, VMEM)],
        [],
        rows * width * hidden,
        2 * (rows * width + rows * hidden + width * hidden // 2),
    )
    gate0, gate1, up0, up1 = call(
        grad_keep_body,
        [((share, hidden), BF16, VMEM)] * 4,
        [(place, SMEM), (x, VMEM), (gate_delta, VMEM), (up_delta, VMEM)],
        [],
        2 * rows * width * hidden,
        2 * (rows * width + 2 * rows * hidden + width * hidden),
    )
    down_a, down_b = to_y(add(keep_a1, got_a[1])), to_x(add(keep_b1, got_b[1]))
    gate_last = to_y(add(gate1, gate_got[1]))
    up_last = to_x(add(up1, up_got[1]))
    gate_sum, up_sum = lax.optimization_barrier((add(gate0, gate_got[0]), add(up0, up_got[0])))
    down_grad = jnp.concatenate([add(keep_a0, got_a[0], down_a), add(keep_b0, got_b[0], down_b)], axis=0)
    gate_grad, up_grad = add(gate_sum, gate_last), add(up_sum, up_last)

    far = hop(total[3], ((0, 1), (3, 2)))
    inner = hop(total[3], INNER)
    outer = hop(total[2], OUTER)
    two = hop(add(total[1], far), TWO)
    input_grad = add(total[0], inner, outer, two)
    return input_grad, gate_grad[None], up_grad[None], down_grad[None]


def routed(tokens, out_grad, routes, gate_values, w_gate, w_up, w_down):
    tok_rows, model_width = tokens.shape
    top_count = routes.shape[1]
    group_count = lax.axis_size("expert")
    local_count = w_gate.shape[0]
    expert_count = group_count * local_count
    hidden_units = w_gate.shape[2]
    capacity = slots_of(tok_rows, top_count, expert_count)
    pair_count = tok_rows * top_count
    slot_count = group_count * capacity
    expert_of = routes.reshape(-1)
    onehot = (expert_of[:, None] == jnp.arange(expert_count, dtype=jnp.int32)[None, :]).astype(
        jnp.int32
    )
    before = jnp.cumsum(onehot, axis=0) - onehot
    placed = jnp.sum(before * onehot, axis=1)
    slot_of = expert_of * capacity + placed
    slot_table = jnp.full((expert_count * capacity,), pair_count, jnp.int32)
    slot_table = slot_table.at[slot_of].set(jnp.arange(pair_count, dtype=jnp.int32))
    filled = slot_table < pair_count
    source = jnp.where(filled, slot_table, 0)
    owner_row = source // top_count
    send_x = jnp.where(filled[:, None], tokens[owner_row], jnp.zeros((), jnp.bfloat16))
    scaled = gate_values.reshape(-1)[source][:, None] * out_grad[owner_row].astype(jnp.float32)
    send_dy = jnp.where(filled[:, None], scaled, 0.0).astype(jnp.bfloat16)
    send_x = send_x.reshape(expert_count, capacity, model_width)
    send_dy = send_dy.reshape(expert_count, capacity, model_width)
    recv_x, recv_dy = (
        lax.all_to_all(send_x, "expert", split_axis=0, concat_axis=0, tiled=True),
        lax.all_to_all(send_dy, "expert", split_axis=0, concat_axis=0, tiled=True),
    )

    def to_local(stacked):
        shaped = stacked.reshape(group_count, local_count, capacity, model_width)
        return shaped.transpose(1, 0, 2, 3).reshape(local_count, slot_count, model_width)

    slot_x = to_local(recv_x)
    slot_dy = to_local(recv_dy)
    part_x = slot_x
    gate_term = jnp.einsum(
        "asd,adf->asf",
        part_x,
        lax.all_gather(w_gate, "dp", axis=1, tiled=True),
        preferred_element_type=jnp.float32,
    )
    up_term = jnp.einsum(
        "asd,adf->asf",
        part_x,
        lax.all_gather(w_up, "dp", axis=1, tiled=True),
        preferred_element_type=jnp.float32,
    )
    full_gate, full_up, full_down = (
        lax.all_gather(w_gate, "dp", axis=1, tiled=True),
        lax.all_gather(w_up, "dp", axis=1, tiled=True),
        lax.all_gather(w_down, "dp", axis=2, tiled=True),
    )
    sigma = jax.nn.sigmoid(gate_term)
    active = gate_term * sigma
    activated = (active * up_term).astype(jnp.bfloat16)
    back_hidden = jnp.einsum("asd,afd->asf", slot_dy, full_down, preferred_element_type=jnp.float32)
    up_delta = (back_hidden * active).astype(jnp.bfloat16)
    gate_delta = (back_hidden * up_term * sigma * (1.0 + gate_term * (1.0 - sigma))).astype(
        jnp.bfloat16
    )
    pair_grad = (
        jnp.einsum("asf,adf->asd", gate_delta, full_gate, preferred_element_type=jnp.float32)
        + jnp.einsum("asf,adf->asd", up_delta, full_up, preferred_element_type=jnp.float32)
    ).astype(jnp.bfloat16)
    send_back = pair_grad.reshape(local_count, group_count, capacity, model_width).transpose(
        1, 0, 2, 3
    )
    send_back = send_back.reshape(expert_count, capacity, model_width)
    returned = lax.all_to_all(send_back, "expert", split_axis=0, concat_axis=0, tiled=True)
    per_pair = returned.reshape(expert_count * capacity, model_width)[slot_of].astype(jnp.float32)
    input_grad = jnp.sum(per_pair.reshape(tok_rows, top_count, model_width), axis=1).astype(
        jnp.bfloat16
    )
    block_width = local_count * hidden_units
    share_width = model_width // lax.axis_size("dp")
    part_x = slot_x
    term_gate = jnp.einsum("asd,asf->daf", part_x, gate_delta, preferred_element_type=jnp.float32)
    term_up = jnp.einsum("asd,asf->daf", part_x, up_delta, preferred_element_type=jnp.float32)
    term_down = jnp.einsum("asd,asf->daf", slot_dy, activated, preferred_element_type=jnp.float32)
    shares = lax.psum_scatter(
        jnp.concatenate(
            [
                term_gate.reshape(lax.axis_size("dp") * share_width, block_width),
                term_up.reshape(lax.axis_size("dp") * share_width, block_width),
                term_down.reshape(lax.axis_size("dp") * share_width, block_width),
            ],
            axis=1,
        ).astype(jnp.bfloat16),
        "dp",
        scatter_dimension=0,
        tiled=True,
    ).astype(jnp.float32)
    share_rows = shares.shape[0]

    def unpack(which):
        return shares[:, which * block_width : (which + 1) * block_width].reshape(
            share_rows, local_count, hidden_units
        )

    gate_grad = unpack(0).transpose(1, 0, 2).astype(jnp.bfloat16)
    up_grad = unpack(1).transpose(1, 0, 2).astype(jnp.bfloat16)
    down_grad = unpack(2).transpose(1, 2, 0).astype(jnp.bfloat16)
    return (input_grad, gate_grad, up_grad, down_grad)


def lined(dp, expert):
    return dp == 4 and expert == 8


def local(tokens, out_grad, routes, gate_values, w_gate, w_up, w_down):
    experts = lax.axis_size("expert") * w_gate.shape[0]
    capacity = slots_of(tokens.shape[0], routes.shape[1], experts)
    fits = w_gate.shape[0] == 1 and tokens.shape[0] <= 2 * capacity
    if not (fits and lined(lax.axis_size("dp"), lax.axis_size("expert"))):
        return routed(tokens, out_grad, routes, gate_values, w_gate, w_up, w_down)
    return dense(tokens, out_grad, routes, gate_values, w_gate, w_up, w_down)


def solution(mesh):
    return jax.shard_map(
        local,
        mesh=mesh,
        in_specs=(
            P(("dp", "expert"), None),
            P(("dp", "expert"), None),
            P(("dp", "expert"), None),
            P(("dp", "expert"), None),
            P("expert", "dp", None),
            P("expert", "dp", None),
            P("expert", None, "dp"),
        ),
        out_specs=(
            P(("dp", "expert"), None),
            P("expert", "dp", None),
            P("expert", "dp", None),
            P("expert", None, "dp"),
        ),
        check_vma=False,
    )
```

```python
import functools

import jax
import jax.numpy as jnp
from jax import lax
from jax.experimental import pallas as pl
from jax.experimental.pallas import tpu as pltpu
from jax.sharding import PartitionSpec as P


F32 = jnp.float32
BF16 = jnp.bfloat16
ANY = pl.BlockSpec(memory_space=pl.ANY)
VMEM = pl.BlockSpec(memory_space=pltpu.VMEM)
SMEM = pl.BlockSpec(memory_space=pltpu.SMEM)
LIMIT = 24 * 1024 * 1024
LANES = 128
NN = (((1,), (0,)), ((), ()))
NT = (((1,), (1,)), ((), ()))


def mm(a, b, dims):
    return lax.dot_general(a, b, dims, preferred_element_type=F32)


def slots_of(tok_rows, top_count, expert_count):
    return min(tok_rows, max(2, 9 * tok_rows * top_count // (8 * expert_count)))


def call(body, outs, ins, scratch, flops, moved, aliases=None):
    return pl.pallas_call(
        body,
        input_output_aliases=aliases or {},
        out_shape=[jax.ShapeDtypeStruct(s, d) for s, d, _ in outs],
        in_specs=[s for _, s in ins],
        out_specs=[s for _, _, s in outs],
        scratch_shapes=scratch,
        compiler_params=pltpu.CompilerParams(vmem_limit_bytes=LIMIT),
        cost_estimate=pl.CostEstimate(flops=flops, bytes_accessed=moved, transcendentals=0),
    )(*[a for a, _ in ins])


TWO = ((0, 2), (1, 3), (2, 0), (3, 1))
OUTER = ((0, 1), (1, 0), (2, 3), (3, 2))
INNER = ((1, 2), (2, 1))


def prep_body(experts, routes, gates, rows, out):
    tok, width = rows.shape
    line = lax.broadcasted_iota(jnp.int32, (LANES, tok), 0)
    term, named = line // experts, line % experts
    value = jnp.zeros((LANES, tok), F32)
    for k in range(routes.shape[0]):
        value += jnp.where(routes[k : k + 1, :] == named, gates[k : k + 1, :], 0.0)
    high = value.astype(BF16).astype(F32)
    mid = (value - high).astype(BF16).astype(F32)
    low = value - high - mid
    value = jnp.where(term == 0, high, jnp.where(term == 1, mid, jnp.where(term == 2, low, 0.0)))
    out[:, :width] = rows[...]
    out[:, width:] = jnp.transpose(value).astype(BF16)


class Copies:
    def __init__(self, sems):
        self.sems, self.used = sems, 0

    def start(self, src, dst):
        copy = pltpu.make_async_copy(src, dst, self.sems.at[self.used])
        self.used += 1
        copy.start()
        return copy

    def pick(self, first, src, other, dst):
        sem = self.sems.at[self.used]
        self.used += 1

        @pl.when(first)
        def _():
            pltpu.make_async_copy(src, dst, sem).start()

        @pl.when(jnp.logical_not(first))
        def _():
            pltpu.make_async_copy(other, dst, sem).start()

        return pltpu.make_async_copy(other, dst, sem)


def load_early(copies, pieces, dst):
    tok = pieces[0].shape[0]
    return [copies.start(src, dst.at[pl.ds(i * tok, tok)]) for i, src in enumerate(pieces)]


def load_late(copies, chip, pieces, dst):
    tok = pieces[0].shape[0]
    middle = jnp.logical_or(chip == 1, chip == 2)
    return [
        copies.pick(middle, pieces[2 * core], pieces[2 * core + 1], dst.at[pl.ds(core * tok, tok)]) for core in (0, 1)
    ]


def pre_blocks(x, first, count, wg, wu, act, active_out, slope_out):
    tn = 256

    def step(i, _):
        r = slice(first, first + count)
        c = pl.ds(pl.multiple_of(i * tn, tn), tn)
        lhs = x[r, :]
        gate = mm(lhs, wg[:, c], NN)
        up = mm(lhs, wu[:, c], NN)
        sigma = jax.nn.sigmoid(gate)
        active = gate * sigma
        act[r, c] = (active * up).astype(BF16)
        active_out[r, c] = active
        slope_out[r, c] = up * sigma * (1.0 + gate * (1.0 - sigma))
        return 0

    lax.fori_loop(0, wg.shape[1] // tn, step, 0)


def pre_early_body(place, *refs):
    pieces, w_gate, w_up = refs[:6], refs[6:10], refs[10:14]
    act, active, slope, x, wg, wu, sems = refs[14:]
    copies = Copies(sems)
    share = w_gate[0].shape[0]
    started = load_early(copies, pieces, x)
    for k in range(4):
        at = pl.ds((place[0] ^ k) * share, share)
        started += [copies.start(w_gate[k], wg.at[at]), copies.start(w_up[k], wu.at[at])]
    for c in started:
        c.wait()
    pre_blocks(x, 0, x.shape[0] // 4 * 3, wg, wu, act, active, slope)


def pre_late_body(place, *refs):
    pieces, wg, wu = refs[:4], refs[4], refs[5]
    act, active, slope, x, sems = refs[10:]
    count = x.shape[0] // 4
    for c in load_late(Copies(sems), place[1], pieces, x.at[pl.ds(3 * count, count)]):
        c.wait()
    pre_blocks(x, 3 * count, count, wg, wu, act, active, slope)


def scale(experts, expert, raw, y, first):
    tok, width = raw.shape[0] // 2, y.shape[1]
    lane = lax.broadcasted_iota(jnp.int32, (tok, LANES), 1)
    mine = jnp.logical_and(lane % experts == expert, lane < 3 * experts)
    for i in (0, 1):
        gate = jnp.sum(jnp.where(mine, raw[i * tok : (i + 1) * tok, width:].astype(F32), 0.0), axis=1, keepdims=True)
        y[first + i * tok : first + (i + 1) * tok, :] = (raw[i * tok : (i + 1) * tok, :width].astype(F32) * gate).astype(
            BF16
        )


def scale_early_body(experts, place, *refs):
    pieces = refs[:6]
    y, raw, sems = refs[6:]
    tok = pieces[0].shape[0]
    started = load_early(Copies(sems), pieces, raw)
    for i in range(3):
        started[2 * i].wait()
        started[2 * i + 1].wait()
        scale(experts, place[2], raw.at[pl.ds(2 * i * tok, 2 * tok)], y, 2 * i * tok)


def down_send_body(experts, place, *refs):
    pieces, act = refs[:4], refs[4]
    send_a, send_b, y, raw, sems = refs[6:]
    for c in load_late(Copies(sems), place[1], pieces, raw):
        c.wait()
    scale(experts, place[2], raw, y, y.shape[0] - raw.shape[0])
    down_blocks(place, act, y, ((0, 1, send_a, 0), (0, 3, send_a, 1), (1, 2, send_b, 0), (1, 3, send_b, 1)))


def down_blocks(place, act, y, wanted):
    share = y.shape[1] // 4
    half = act.shape[1] // 2
    for h in (0, 1):
        turned = jnp.transpose(act[:, h * half : (h + 1) * half])
        for which, k, dst, slot in wanted:
            if which == h:
                cols = pl.ds(pl.multiple_of((place[0] ^ k) * share, share), share)
                value = mm(turned, y[:, cols], NN).astype(BF16)
                if slot is None:
                    dst[...] = value
                else:
                    dst[slot] = value


def down_keep_body(place, act, y, a0, a1, b0, b1):
    down_blocks(place, act, y, ((0, 0, a0, None), (0, 2, a1, None), (1, 0, b0, None), (1, 1, b1, None)))


def back_body(place, y, active, slope, own, from_x, from_y, diag_a, diag_b, gate_delta, up_delta, w, sems):
    me = place[0]
    copies = Copies(sems)
    hidden, share = own.shape
    half = hidden // 2
    started = []
    for k, src in ((0, own), (1, from_x), (2, from_y)):
        started.append(copies.start(src, w.at[me ^ k]))
    started.append(copies.start(diag_a, w.at[me ^ 3, pl.ds(0, half)]))
    started.append(copies.start(diag_b, w.at[me ^ 3, pl.ds(half, half)]))
    for c in started:
        c.wait()
    rows = y.shape[0]
    tm, tn = rows // 2, 256

    def step(i, _):
        r = pl.ds(pl.multiple_of(i // (hidden // tn) * tm, tm), tm)
        c = pl.ds(pl.multiple_of(i % (hidden // tn) * tn, tn), tn)
        back = mm(y[r, 0:share], w[0, c, :], NT)
        for j in range(1, 4):
            back += mm(y[r, j * share : (j + 1) * share], w[j, c, :], NT)
        up_delta[r, c] = (back * active[r, c]).astype(BF16)
        gate_delta[r, c] = (back * slope[r, c]).astype(BF16)
        return 0

    lax.fori_loop(0, 2 * (hidden // tn), step, 0)


def grad_blocks(place, x, wanted):
    share = x.shape[1] // 4
    tm = share // 2
    for k, targets in wanted:

        def step(i, _, k=k, targets=targets):
            cols = pl.ds(pl.multiple_of((place[0] ^ k) * share + i * tm, tm), tm)
            turned = jnp.transpose(x[:, cols])
            part = pl.ds(pl.multiple_of(i * tm, tm), tm)
            for delta, dst, slot in targets:
                value = mm(turned, delta[...], NN).astype(BF16)
                if slot is None:
                    dst[part, :] = value
                else:
                    dst[slot, part, :] = value
            return 0

        lax.fori_loop(0, 2, step, 0)


def grad_send_body(place, x, gd, ud, gate_send, up_send):
    grad_blocks(
        place, x, ((1, [(gd, gate_send, 0)]), (3, [(gd, gate_send, 1), (ud, up_send, 1)]), (2, [(ud, up_send, 0)]))
    )


def grad_keep_body(place, x, gd, ud, g0, g1, u0, u1):
    grad_blocks(place, x, ((2, [(gd, g1, None)]), (1, [(ud, u1, None)]), (0, [(gd, g0, None), (ud, u0, None)])))


def pair_body(gate_delta, up_delta, wg, wu, send, keep):
    tn = 256
    part = keep.shape[0] // 4

    def step(i, _):
        c = pl.ds(pl.multiple_of(i * tn, tn), tn)
        total = (mm(gate_delta[...], wg[c, :], NT) + mm(up_delta[...], wu[c, :], NT)).astype(BF16)
        keep[: 3 * part, c] = total[: 3 * part]
        send[: 3 * part, c] = total[3 * part : 6 * part]
        keep[3 * part :, c] = total[6 * part : 7 * part]
        send[3 * part :, c] = total[7 * part :]
        return 0

    lax.fori_loop(0, wg.shape[0] // tn, step, 0)


def add(*terms):
    total = terms[0].astype(F32)
    for term in terms[1:]:
        total = total + term.astype(F32)
    return total.astype(BF16)


def dense(tokens, out_grad, routes, gate_values, w_gate, w_up, w_down):
    tok, width = tokens.shape
    experts = lax.axis_size("expert")
    chips = experts // 2
    hidden = w_gate.shape[2]
    share = width // 4
    half = hidden // 2
    rows = experts * tok
    expert = lax.axis_index("expert")
    chip = expert // 2
    place = jnp.stack([lax.axis_index("dp"), chip, expert]).astype(jnp.int32)

    def to_x(block):
        return lax.ppermute(block, "dp", [(i, i ^ 1) for i in range(4)])

    def to_y(block):
        return lax.ppermute(block, "dp", [(i, i ^ 2) for i in range(4)])

    def hop(block, moves):
        return lax.ppermute(block, "expert", [(2 * a + c, 2 * b + c) for a, b in moves for c in (0, 1)])

    def swap(block, at=range(chips)):
        return lax.ppermute(block, "expert", [(2 * z + c, 2 * z + 1 - c) for z in at for c in (0, 1)])

    def line(own):
        two = hop(own, TWO)
        outer = hop(own, OUTER)
        inner = hop(own, INNER)
        far = hop(two, ((2, 3), (1, 0)))
        early = [own, two, outer, swap(own), swap(two), swap(outer)]
        late = [inner, far, swap(inner, (1, 2)), swap(far, (0, 3))]
        return early, late

    x_early, x_late = line(tokens)
    (y_own,) = call(
        functools.partial(prep_body, experts),
        [((tok, width + LANES), BF16, VMEM)],
        [(routes.T, VMEM), (gate_values.T, VMEM), (out_grad, VMEM)],
        [],
        1000,
        4 * tok * width,
    )
    y_early, y_late = line(y_own)

    wg0, wu0, wd0 = w_gate[0], w_up[0], w_down[0]
    wg1, wu1 = to_x(wg0), to_y(wu0)
    wg2, wu2 = to_y(wg0), to_x(wu0)
    wg3, wu3 = to_y(wg1), to_x(wu1)
    w_g, w_u = (wg0, wg1, wg2, wg3), (wu0, wu2, wu1, wu3)
    wd1, wd2 = to_x(wd0), to_y(wd0)
    wd3a, wd3b = to_x(wd2[:half]), to_y(wd1[half:])

    def dma(n):
        return pltpu.SemaphoreType.DMA((n,))

    def anys(arrays):
        return [(a, ANY) for a in arrays]

    pre_outs = [
        ((rows, hidden), BF16, VMEM),
        ((rows, hidden), F32, VMEM),
        ((rows, hidden), F32, VMEM),
        ((rows, width), BF16, VMEM),
    ]
    weight = ((width, hidden), BF16, VMEM)
    *pre, wg, wu = call(
        pre_early_body,
        pre_outs + [weight] * 2,
        [(place, SMEM)] + anys(x_early) + anys(w_g + w_u),
        [dma(14)],
        3 * rows * width * hidden,
        3 * rows * width + 8 * width * hidden + 8 * rows * hidden,
    )
    act, active, slope, x = call(
        pre_late_body,
        pre_outs,
        [(place, SMEM)] + anys(x_late) + [(wg, VMEM), (wu, VMEM)] + [(a, VMEM) for a in pre],
        [dma(2)],
        rows * width * hidden,
        rows * width + 4 * width * hidden + 3 * rows * hidden,
        {7 + i: i for i in range(4)},
    )
    (y,) = call(
        functools.partial(scale_early_body, experts),
        [((rows, width), BF16, VMEM)],
        [(place, SMEM)] + anys(y_early),
        [pltpu.VMEM((6 * tok, width + LANES), BF16), dma(6)],
        rows * width,
        4 * rows * width,
    )
    piece = (2, half, share)
    send_a, send_b, y = call(
        functools.partial(down_send_body, experts),
        [(piece, BF16, VMEM)] * 2 + [((rows, width), BF16, VMEM)],
        [(place, SMEM)] + anys(y_late) + [(act, VMEM), (y, VMEM)],
        [pltpu.VMEM((2 * tok, width + LANES), BF16), dma(2)],
        rows * width * hidden,
        2 * (2 * rows * width + rows * hidden + width * hidden // 2),
        {6: 2},
    )
    got_a, got_b = to_x(send_a), to_y(send_b)
    gate_delta, up_delta = call(
        back_body,
        [((rows, hidden), BF16, VMEM)] * 2,
        [(place, SMEM), (y, VMEM), (active, VMEM), (slope, VMEM)] + [(a, ANY) for a in (wd0, wd1, wd2, wd3a, wd3b)],
        [pltpu.VMEM((4, hidden, share), BF16), dma(5)],
        2 * rows * width * hidden,
        2 * (rows * width + width * hidden) + 12 * rows * hidden,
    )
    gate_send, up_send = call(
        grad_send_body,
        [((2, share, hidden), BF16, VMEM)] * 2,
        [(place, SMEM), (x, VMEM), (gate_delta, VMEM), (up_delta, VMEM)],
        [],
        2 * rows * width * hidden,
        2 * (rows * width + 2 * rows * hidden + width * hidden),
    )
    gate_got, up_got = to_x(gate_send), to_y(up_send)
    pair_send, pair_keep = call(
        pair_body,
        [((rows // 2, width), BF16, VMEM)] * 2,
        [(gate_delta, VMEM), (up_delta, VMEM), (wg, VMEM), (wu, VMEM)],
        [],
        4 * rows * width * hidden,
        2 * (rows * width + 2 * rows * hidden + 2 * width * hidden),
    )
    total = add(pair_keep, swap(pair_send)).reshape(chips, tok, width)
    keep_a0, keep_a1, keep_b0, keep_b1 = call(
        down_keep_body,
        [((half, share), BF16, VMEM)] * 4,
        [(place, SMEM), (act, VMEM), (y, VMEM)],
        [],
        rows * width * hidden,
        2 * (rows * width + rows * hidden + width * hidden // 2),
    )
    gate0, gate1, up0, up1 = call(
        grad_keep_body,
        [((share, hidden), BF16, VMEM)] * 4,
        [(place, SMEM), (x, VMEM), (gate_delta, VMEM), (up_delta, VMEM)],
        [],
        2 * rows * width * hidden,
        2 * (rows * width + 2 * rows * hidden + width * hidden),
    )
    down_a, down_b = to_y(add(keep_a1, got_a[1])), to_x(add(keep_b1, got_b[1]))
    gate1, up1 = add(gate1, gate_got[1]), add(up1, up_got[1])
    sums = add(gate0, gate_got[0]), add(up0, up_got[0])
    gate_last, up_last = to_y(gate1), to_x(up1)
    gate_sum, up_sum = lax.optimization_barrier(sums)
    down_grad = jnp.concatenate([add(keep_a0, got_a[0], down_a), add(keep_b0, got_b[0], down_b)], axis=0)
    gate_grad, up_grad = add(gate_sum, gate_last), add(up_sum, up_last)

    far = hop(total[3], ((0, 1), (3, 2)))
    inner = hop(total[3], INNER)
    outer = hop(total[2], OUTER)
    two = hop(add(total[1], far), TWO)
    input_grad = add(total[0], inner, outer, two)
    return input_grad, gate_grad[None], up_grad[None], down_grad[None]


def routed(tokens, out_grad, routes, gate_values, w_gate, w_up, w_down):
    tok_rows, model_width = tokens.shape
    top_count = routes.shape[1]
    group_count = lax.axis_size("expert")
    local_count = w_gate.shape[0]
    expert_count = group_count * local_count
    hidden_units = w_gate.shape[2]
    capacity = slots_of(tok_rows, top_count, expert_count)
    pair_count = tok_rows * top_count
    slot_count = group_count * capacity
    expert_of = routes.reshape(-1)
    onehot = (expert_of[:, None] == jnp.arange(expert_count, dtype=jnp.int32)[None, :]).astype(
        jnp.int32
    )
    before = jnp.cumsum(onehot, axis=0) - onehot
    placed = jnp.sum(before * onehot, axis=1)
    slot_of = expert_of * capacity + placed
    slot_table = jnp.full((expert_count * capacity,), pair_count, jnp.int32)
    slot_table = slot_table.at[slot_of].set(jnp.arange(pair_count, dtype=jnp.int32))
    filled = slot_table < pair_count
    source = jnp.where(filled, slot_table, 0)
    owner_row = source // top_count
    send_x = jnp.where(filled[:, None], tokens[owner_row], jnp.zeros((), jnp.bfloat16))
    scaled = gate_values.reshape(-1)[source][:, None] * out_grad[owner_row].astype(jnp.float32)
    send_dy = jnp.where(filled[:, None], scaled, 0.0).astype(jnp.bfloat16)
    send_x = send_x.reshape(expert_count, capacity, model_width)
    send_dy = send_dy.reshape(expert_count, capacity, model_width)
    recv_x, recv_dy = (
        lax.all_to_all(send_x, "expert", split_axis=0, concat_axis=0, tiled=True),
        lax.all_to_all(send_dy, "expert", split_axis=0, concat_axis=0, tiled=True),
    )

    def to_local(stacked):
        shaped = stacked.reshape(group_count, local_count, capacity, model_width)
        return shaped.transpose(1, 0, 2, 3).reshape(local_count, slot_count, model_width)

    slot_x = to_local(recv_x)
    slot_dy = to_local(recv_dy)
    part_x = slot_x
    gate_term = jnp.einsum(
        "asd,adf->asf",
        part_x,
        lax.all_gather(w_gate, "dp", axis=1, tiled=True),
        preferred_element_type=jnp.float32,
    )
    up_term = jnp.einsum(
        "asd,adf->asf",
        part_x,
        lax.all_gather(w_up, "dp", axis=1, tiled=True),
        preferred_element_type=jnp.float32,
    )
    full_gate, full_up, full_down = (
        lax.all_gather(w_gate, "dp", axis=1, tiled=True),
        lax.all_gather(w_up, "dp", axis=1, tiled=True),
        lax.all_gather(w_down, "dp", axis=2, tiled=True),
    )
    sigma = jax.nn.sigmoid(gate_term)
    active = gate_term * sigma
    activated = (active * up_term).astype(jnp.bfloat16)
    back_hidden = jnp.einsum("asd,afd->asf", slot_dy, full_down, preferred_element_type=jnp.float32)
    up_delta = (back_hidden * active).astype(jnp.bfloat16)
    gate_delta = (back_hidden * up_term * sigma * (1.0 + gate_term * (1.0 - sigma))).astype(
        jnp.bfloat16
    )
    pair_grad = (
        jnp.einsum("asf,adf->asd", gate_delta, full_gate, preferred_element_type=jnp.float32)
        + jnp.einsum("asf,adf->asd", up_delta, full_up, preferred_element_type=jnp.float32)
    ).astype(jnp.bfloat16)
    send_back = pair_grad.reshape(local_count, group_count, capacity, model_width).transpose(
        1, 0, 2, 3
    )
    send_back = send_back.reshape(expert_count, capacity, model_width)
    returned = lax.all_to_all(send_back, "expert", split_axis=0, concat_axis=0, tiled=True)
    per_pair = returned.reshape(expert_count * capacity, model_width)[slot_of].astype(jnp.float32)
    input_grad = jnp.sum(per_pair.reshape(tok_rows, top_count, model_width), axis=1).astype(
        jnp.bfloat16
    )
    block_width = local_count * hidden_units
    share_width = model_width // lax.axis_size("dp")
    part_x = slot_x
    term_gate = jnp.einsum("asd,asf->daf", part_x, gate_delta, preferred_element_type=jnp.float32)
    term_up = jnp.einsum("asd,asf->daf", part_x, up_delta, preferred_element_type=jnp.float32)
    term_down = jnp.einsum("asd,asf->daf", slot_dy, activated, preferred_element_type=jnp.float32)
    shares = lax.psum_scatter(
        jnp.concatenate(
            [
                term_gate.reshape(lax.axis_size("dp") * share_width, block_width),
                term_up.reshape(lax.axis_size("dp") * share_width, block_width),
                term_down.reshape(lax.axis_size("dp") * share_width, block_width),
            ],
            axis=1,
        ).astype(jnp.bfloat16),
        "dp",
        scatter_dimension=0,
        tiled=True,
    ).astype(jnp.float32)
    share_rows = shares.shape[0]

    def unpack(which):
        return shares[:, which * block_width : (which + 1) * block_width].reshape(
            share_rows, local_count, hidden_units
        )

    gate_grad = unpack(0).transpose(1, 0, 2).astype(jnp.bfloat16)
    up_grad = unpack(1).transpose(1, 0, 2).astype(jnp.bfloat16)
    down_grad = unpack(2).transpose(1, 2, 0).astype(jnp.bfloat16)
    return (input_grad, gate_grad, up_grad, down_grad)


def lined(dp, expert):
    return dp == 4 and expert == 8


def local(tokens, out_grad, routes, gate_values, w_gate, w_up, w_down):
    experts = lax.axis_size("expert") * w_gate.shape[0]
    capacity = slots_of(tokens.shape[0], routes.shape[1], experts)
    fits = w_gate.shape[0] == 1 and tokens.shape[0] <= 2 * capacity
    if not (fits and lined(lax.axis_size("dp"), lax.axis_size("expert"))):
        return routed(tokens, out_grad, routes, gate_values, w_gate, w_up, w_down)
    return dense(tokens, out_grad, routes, gate_values, w_gate, w_up, w_down)


def solution(mesh):
    return jax.shard_map(
        local,
        mesh=mesh,
        in_specs=(
            P(("dp", "expert"), None),
            P(("dp", "expert"), None),
            P(("dp", "expert"), None),
            P(("dp", "expert"), None),
            P("expert", "dp", None),
            P("expert", "dp", None),
            P("expert", None, "dp"),
        ),
        out_specs=(
            P(("dp", "expert"), None),
            P("expert", "dp", None),
            P("expert", "dp", None),
            P("expert", None, "dp"),
        ),
        check_vma=False,
    )
```

```python
import functools

import jax
import jax.numpy as jnp
from jax import lax
from jax.experimental import pallas as pl
from jax.experimental.pallas import tpu as pltpu
from jax.sharding import PartitionSpec as P


F32 = jnp.float32
BF16 = jnp.bfloat16
ANY = pl.BlockSpec(memory_space=pl.ANY)
VMEM = pl.BlockSpec(memory_space=pltpu.VMEM)
SMEM = pl.BlockSpec(memory_space=pltpu.SMEM)
LIMIT = 24 * 1024 * 1024
LANES = 128
NN = (((1,), (0,)), ((), ()))
NT = (((1,), (1,)), ((), ()))


def mm(a, b, dims):
    return lax.dot_general(a, b, dims, preferred_element_type=F32)


def slots_of(tok_rows, top_count, expert_count):
    return min(tok_rows, max(2, 9 * tok_rows * top_count // (8 * expert_count)))


def call(body, outs, ins, scratch, flops, moved, aliases=None):
    return pl.pallas_call(
        body,
        input_output_aliases=aliases or {},
        out_shape=[jax.ShapeDtypeStruct(s, d) for s, d, _ in outs],
        in_specs=[s for _, s in ins],
        out_specs=[s for _, _, s in outs],
        scratch_shapes=scratch,
        compiler_params=pltpu.CompilerParams(vmem_limit_bytes=LIMIT),
        cost_estimate=pl.CostEstimate(flops=flops, bytes_accessed=moved, transcendentals=0),
    )(*[a for a, _ in ins])


TWO = ((0, 2), (1, 3), (2, 0), (3, 1))
OUTER = ((0, 1), (1, 0), (2, 3), (3, 2))
INNER = ((1, 2), (2, 1))


def prep_body(experts, routes, gates, rows, out):
    tok, width = rows.shape
    line = lax.broadcasted_iota(jnp.int32, (LANES, tok), 0)
    term, named = line // experts, line % experts
    value = jnp.zeros((LANES, tok), F32)
    for k in range(routes.shape[0]):
        value += jnp.where(routes[k : k + 1, :] == named, gates[k : k + 1, :], 0.0)
    high = value.astype(BF16).astype(F32)
    mid = (value - high).astype(BF16).astype(F32)
    low = value - high - mid
    value = jnp.where(term == 0, high, jnp.where(term == 1, mid, jnp.where(term == 2, low, 0.0)))
    out[:, :width] = rows[...]
    out[:, width:] = jnp.transpose(value).astype(BF16)


class Copies:
    def __init__(self, sems):
        self.sems, self.used = sems, 0

    def start(self, src, dst):
        copy = pltpu.make_async_copy(src, dst, self.sems.at[self.used])
        self.used += 1
        copy.start()
        return copy

    def pick(self, first, src, other, dst):
        sem = self.sems.at[self.used]
        self.used += 1

        @pl.when(first)
        def _():
            pltpu.make_async_copy(src, dst, sem).start()

        @pl.when(jnp.logical_not(first))
        def _():
            pltpu.make_async_copy(other, dst, sem).start()

        return pltpu.make_async_copy(other, dst, sem)


def load_early(copies, pieces, dst, first=0):
    tok = pieces[0].shape[0]
    return [copies.start(src, dst.at[pl.ds((first + i) * tok, tok)]) for i, src in enumerate(pieces)]


def load_weights(copies, place, which, pieces, wg, wu):
    share = pieces[0].shape[0]
    started = []
    for i, k in enumerate(which):
        at = pl.ds((place[0] ^ k) * share, share)
        started += [copies.start(pieces[2 * i], wg.at[at]), copies.start(pieces[2 * i + 1], wu.at[at])]
    return started


def own_body(place, tokens, w_gate, w_up, x, wg, wu, sems):
    copies = Copies(sems)
    started = load_early(copies, (tokens,), x) + load_weights(copies, place, (0,), (w_gate, w_up), wg, wu)
    for c in started:
        c.wait()


def near_body(place, *refs):
    pieces, weights = refs[:5], refs[5:9]
    x, wg, wu, sems = refs[12:]
    copies = Copies(sems)
    for c in load_early(copies, pieces, x, 1) + load_weights(copies, place, (1, 2), weights, wg, wu):
        c.wait()


def load_late(copies, chip, pieces, dst):
    tok = pieces[0].shape[0]
    middle = jnp.logical_or(chip == 1, chip == 2)
    return [
        copies.pick(middle, pieces[2 * core], pieces[2 * core + 1], dst.at[pl.ds(core * tok, tok)]) for core in (0, 1)
    ]


def pre_blocks(x, first, count, wg, wu, act, active_out, slope_out):
    tn = 256

    def step(i, _):
        r = slice(first, first + count)
        c = pl.ds(pl.multiple_of(i * tn, tn), tn)
        lhs = x[r, :]
        gate = mm(lhs, wg[:, c], NN)
        up = mm(lhs, wu[:, c], NN)
        sigma = jax.nn.sigmoid(gate)
        active = gate * sigma
        act[r, c] = (active * up).astype(BF16)
        active_out[r, c] = active
        slope_out[r, c] = up * sigma * (1.0 + gate * (1.0 - sigma))
        return 0

    lax.fori_loop(0, wg.shape[1] // tn, step, 0)


def pre_early_body(place, *refs):
    act, active, slope, wg, wu, sems = refs[5:]
    for c in load_weights(Copies(sems), place, (3,), refs[:2], wg, wu):
        c.wait()
    x = refs[2]
    pre_blocks(x, 0, x.shape[0] // 4 * 3, wg, wu, act, active, slope)


def pre_late_body(place, *refs):
    pieces, wg, wu = refs[:4], refs[4], refs[5]
    act, active, slope, x, sems = refs[10:]
    count = x.shape[0] // 4
    for c in load_late(Copies(sems), place[1], pieces, x.at[pl.ds(3 * count, count)]):
        c.wait()
    pre_blocks(x, 3 * count, count, wg, wu, act, active, slope)


def scale(experts, expert, raw, y, first):
    tok, width = raw.shape[0] // 2, y.shape[1]
    lane = lax.broadcasted_iota(jnp.int32, (tok, LANES), 1)
    mine = jnp.logical_and(lane % experts == expert, lane < 3 * experts)
    for i in (0, 1):
        gate = jnp.sum(jnp.where(mine, raw[i * tok : (i + 1) * tok, width:].astype(F32), 0.0), axis=1, keepdims=True)
        y[first + i * tok : first + (i + 1) * tok, :] = (raw[i * tok : (i + 1) * tok, :width].astype(F32) * gate).astype(
            BF16
        )


def scale_early_body(experts, place, *refs):
    pieces = refs[:6]
    y, raw, sems = refs[6:]
    tok = pieces[0].shape[0]
    started = load_early(Copies(sems), pieces, raw)
    for i in range(3):
        started[2 * i].wait()
        started[2 * i + 1].wait()
        scale(experts, place[2], raw.at[pl.ds(2 * i * tok, 2 * tok)], y, 2 * i * tok)


def down_send_body(experts, place, *refs):
    pieces, act = refs[:4], refs[4]
    send_a, send_b, y, raw, sems = refs[6:]
    for c in load_late(Copies(sems), place[1], pieces, raw):
        c.wait()
    scale(experts, place[2], raw, y, y.shape[0] - raw.shape[0])
    down_blocks(place, act, y, ((0, 1, send_a, 0), (0, 3, send_a, 1), (1, 2, send_b, 0), (1, 3, send_b, 1)))


def down_blocks(place, act, y, wanted):
    share = y.shape[1] // 4
    half = act.shape[1] // 2
    for h in (0, 1):
        turned = jnp.transpose(act[:, h * half : (h + 1) * half])
        for which, k, dst, slot in wanted:
            if which == h:
                cols = pl.ds(pl.multiple_of((place[0] ^ k) * share, share), share)
                value = mm(turned, y[:, cols], NN).astype(BF16)
                if slot is None:
                    dst[...] = value
                else:
                    dst[slot] = value


def down_keep_body(place, act, y, a0, a1, b0, b1):
    down_blocks(place, act, y, ((0, 0, a0, None), (0, 2, a1, None), (1, 0, b0, None), (1, 1, b1, None)))


def back_body(place, y, active, slope, own, from_x, from_y, diag_a, diag_b, gate_delta, up_delta, w, sems):
    me = place[0]
    copies = Copies(sems)
    hidden, share = own.shape
    half = hidden // 2
    started = []
    for k, src in ((0, own), (1, from_x), (2, from_y)):
        started.append(copies.start(src, w.at[me ^ k]))
    started.append(copies.start(diag_a, w.at[me ^ 3, pl.ds(0, half)]))
    started.append(copies.start(diag_b, w.at[me ^ 3, pl.ds(half, half)]))
    for c in started:
        c.wait()
    rows = y.shape[0]
    tm, tn = rows // 2, 256

    def step(i, _):
        r = pl.ds(pl.multiple_of(i // (hidden // tn) * tm, tm), tm)
        c = pl.ds(pl.multiple_of(i % (hidden // tn) * tn, tn), tn)
        back = mm(y[r, 0:share], w[0, c, :], NT)
        for j in range(1, 4):
            back += mm(y[r, j * share : (j + 1) * share], w[j, c, :], NT)
        up_delta[r, c] = (back * active[r, c]).astype(BF16)
        gate_delta[r, c] = (back * slope[r, c]).astype(BF16)
        return 0

    lax.fori_loop(0, 2 * (hidden // tn), step, 0)


def grad_blocks(place, x, wanted):
    share = x.shape[1] // 4
    tm = share // 2
    for k, targets in wanted:

        def step(i, _, k=k, targets=targets):
            cols = pl.ds(pl.multiple_of((place[0] ^ k) * share + i * tm, tm), tm)
            turned = jnp.transpose(x[:, cols])
            part = pl.ds(pl.multiple_of(i * tm, tm), tm)
            for delta, dst, slot in targets:
                value = mm(turned, delta[...], NN).astype(BF16)
                if slot is None:
                    dst[part, :] = value
                else:
                    dst[slot, part, :] = value
            return 0

        lax.fori_loop(0, 2, step, 0)


def grad_send_body(place, x, gd, ud, gate_send, up_send):
    grad_blocks(
        place, x, ((1, [(gd, gate_send, 0)]), (3, [(gd, gate_send, 1), (ud, up_send, 1)]), (2, [(ud, up_send, 0)]))
    )


def grad_keep_body(place, x, gd, ud, g0, g1, u0, u1):
    grad_blocks(place, x, ((2, [(gd, g1, None)]), (1, [(ud, u1, None)]), (0, [(gd, g0, None), (ud, u0, None)])))


def pair_body(gate_delta, up_delta, wg, wu, send, keep):
    tn = 256
    part = keep.shape[0] // 4

    def step(i, _):
        c = pl.ds(pl.multiple_of(i * tn, tn), tn)
        total = (mm(gate_delta[...], wg[c, :], NT) + mm(up_delta[...], wu[c, :], NT)).astype(BF16)
        keep[: 3 * part, c] = total[: 3 * part]
        send[: 3 * part, c] = total[3 * part : 6 * part]
        keep[3 * part :, c] = total[6 * part : 7 * part]
        send[3 * part :, c] = total[7 * part :]
        return 0

    lax.fori_loop(0, wg.shape[0] // tn, step, 0)


def add(*terms):
    total = terms[0].astype(F32)
    for term in terms[1:]:
        total = total + term.astype(F32)
    return total.astype(BF16)


def dense(tokens, out_grad, routes, gate_values, w_gate, w_up, w_down):
    tok, width = tokens.shape
    experts = lax.axis_size("expert")
    chips = experts // 2
    hidden = w_gate.shape[2]
    share = width // 4
    half = hidden // 2
    rows = experts * tok
    expert = lax.axis_index("expert")
    chip = expert // 2
    place = jnp.stack([lax.axis_index("dp"), chip, expert]).astype(jnp.int32)

    def to_x(block):
        return lax.ppermute(block, "dp", [(i, i ^ 1) for i in range(4)])

    def to_y(block):
        return lax.ppermute(block, "dp", [(i, i ^ 2) for i in range(4)])

    def hop(block, moves):
        return lax.ppermute(block, "expert", [(2 * a + c, 2 * b + c) for a, b in moves for c in (0, 1)])

    def swap(block, at=range(chips)):
        return lax.ppermute(block, "expert", [(2 * z + c, 2 * z + 1 - c) for z in at for c in (0, 1)])

    def line(own):
        two = hop(own, TWO)
        outer = hop(own, OUTER)
        inner = hop(own, INNER)
        far = hop(two, ((2, 3), (1, 0)))
        early = [own, two, outer, swap(own), swap(two), swap(outer)]
        late = [inner, far, swap(inner, (1, 2)), swap(far, (0, 3))]
        return early, late

    x_early, x_late = line(tokens)
    (y_own,) = call(
        functools.partial(prep_body, experts),
        [((tok, width + LANES), BF16, VMEM)],
        [(routes.T, VMEM), (gate_values.T, VMEM), (out_grad, VMEM)],
        [],
        1000,
        4 * tok * width,
    )
    y_early, y_late = line(y_own)

    wg0, wu0, wd0 = w_gate[0], w_up[0], w_down[0]
    wg1, wu2 = to_x(wg0), to_y(wu0)
    wg2, wu1 = to_y(wg0), to_x(wu0)
    wg3, wu3 = to_y(wg1), to_x(wu2)
    wd1, wd2 = to_x(wd0), to_y(wd0)
    wd3a, wd3b = to_x(wd2[:half]), to_y(wd1[half:])

    def dma(n):
        return pltpu.SemaphoreType.DMA((n,))

    def anys(arrays):
        return [(a, ANY) for a in arrays]

    x_out = ((rows, width), BF16, VMEM)
    weight = ((width, hidden), BF16, VMEM)
    flat = ((rows, hidden), BF16, VMEM)
    wide = ((rows, hidden), F32, VMEM)
    x, wg, wu = call(
        own_body,
        [x_out, weight, weight],
        [(place, SMEM)] + anys((tokens, wg0, wu0)),
        [dma(3)],
        1000,
        width * (2 * tok + hidden),
    )
    x, wg, wu = call(
        near_body,
        [x_out, weight, weight],
        [(place, SMEM)] + anys(x_early[1:]) + anys((wg1, wu1, wg2, wu2)) + [(x, VMEM), (wg, VMEM), (wu, VMEM)],
        [dma(9)],
        1000,
        width * (10 * tok + 2 * hidden),
        {10: 0, 11: 1, 12: 2},
    )
    *pre, wg, wu = call(
        pre_early_body,
        [flat, wide, wide, weight, weight],
        [(place, SMEM)] + anys((wg3, wu3)) + [(x, VMEM), (wg, VMEM), (wu, VMEM)],
        [dma(2)],
        3 * rows * width * hidden,
        3 * rows * width + 8 * width * hidden + 8 * rows * hidden,
        {4: 3, 5: 4},
    )
    act, active, slope, x = call(
        pre_late_body,
        [flat, wide, wide, x_out],
        [(place, SMEM)] + anys(x_late) + [(a, VMEM) for a in (wg, wu, *pre, x)],
        [dma(2)],
        rows * width * hidden,
        rows * width + 4 * width * hidden + 3 * rows * hidden,
        {7 + i: i for i in range(4)},
    )
    (y,) = call(
        functools.partial(scale_early_body, experts),
        [((rows, width), BF16, VMEM)],
        [(place, SMEM)] + anys(y_early),
        [pltpu.VMEM((6 * tok, width + LANES), BF16), dma(6)],
        rows * width,
        4 * rows * width,
    )
    piece = (2, half, share)
    send_a, send_b, y = call(
        functools.partial(down_send_body, experts),
        [(piece, BF16, VMEM)] * 2 + [((rows, width), BF16, VMEM)],
        [(place, SMEM)] + anys(y_late) + [(act, VMEM), (y, VMEM)],
        [pltpu.VMEM((2 * tok, width + LANES), BF16), dma(2)],
        rows * width * hidden,
        2 * (2 * rows * width + rows * hidden + width * hidden // 2),
        {6: 2},
    )
    got_a, got_b = to_x(send_a), to_y(send_b)
    gate_delta, up_delta = call(
        back_body,
        [((rows, hidden), BF16, VMEM)] * 2,
        [(place, SMEM), (y, VMEM), (active, VMEM), (slope, VMEM)] + [(a, ANY) for a in (wd0, wd1, wd2, wd3a, wd3b)],
        [pltpu.VMEM((4, hidden, share), BF16), dma(5)],
        2 * rows * width * hidden,
        2 * (rows * width + width * hidden) + 12 * rows * hidden,
    )
    gate_send, up_send = call(
        grad_send_body,
        [((2, share, hidden), BF16, VMEM)] * 2,
        [(place, SMEM), (x, VMEM), (gate_delta, VMEM), (up_delta, VMEM)],
        [],
        2 * rows * width * hidden,
        2 * (rows * width + 2 * rows * hidden + width * hidden),
    )
    gate_got, up_got = to_x(gate_send), to_y(up_send)
    pair_send, pair_keep = call(
        pair_body,
        [((rows // 2, width), BF16, VMEM)] * 2,
        [(gate_delta, VMEM), (up_delta, VMEM), (wg, VMEM), (wu, VMEM)],
        [],
        4 * rows * width * hidden,
        2 * (rows * width + 2 * rows * hidden + 2 * width * hidden),
    )
    total = add(pair_keep, swap(pair_send)).reshape(chips, tok, width)
    keep_a0, keep_a1, keep_b0, keep_b1 = call(
        down_keep_body,
        [((half, share), BF16, VMEM)] * 4,
        [(place, SMEM), (act, VMEM), (y, VMEM)],
        [],
        rows * width * hidden,
        2 * (rows * width + rows * hidden + width * hidden // 2),
    )
    gate0, gate1, up0, up1 = call(
        grad_keep_body,
        [((share, hidden), BF16, VMEM)] * 4,
        [(place, SMEM), (x, VMEM), (gate_delta, VMEM), (up_delta, VMEM)],
        [],
        2 * rows * width * hidden,
        2 * (rows * width + 2 * rows * hidden + width * hidden),
    )
    down_a, down_b = to_y(add(keep_a1, got_a[1])), to_x(add(keep_b1, got_b[1]))
    gate1, up1 = add(gate1, gate_got[1]), add(up1, up_got[1])
    sums = add(gate0, gate_got[0]), add(up0, up_got[0])
    gate_last, up_last = to_y(gate1), to_x(up1)
    gate_sum, up_sum = lax.optimization_barrier(sums)
    down_grad = jnp.concatenate([add(keep_a0, got_a[0], down_a), add(keep_b0, got_b[0], down_b)], axis=0)
    gate_grad, up_grad = add(gate_sum, gate_last), add(up_sum, up_last)

    far = hop(total[3], ((0, 1), (3, 2)))
    inner = hop(total[3], INNER)
    outer = hop(total[2], OUTER)
    two = hop(add(total[1], far), TWO)
    input_grad = add(total[0], inner, outer, two)
    return input_grad, gate_grad[None], up_grad[None], down_grad[None]


def routed(tokens, out_grad, routes, gate_values, w_gate, w_up, w_down):
    tok_rows, model_width = tokens.shape
    top_count = routes.shape[1]
    group_count = lax.axis_size("expert")
    local_count = w_gate.shape[0]
    expert_count = group_count * local_count
    hidden_units = w_gate.shape[2]
    capacity = slots_of(tok_rows, top_count, expert_count)
    pair_count = tok_rows * top_count
    slot_count = group_count * capacity
    expert_of = routes.reshape(-1)
    onehot = (expert_of[:, None] == jnp.arange(expert_count, dtype=jnp.int32)[None, :]).astype(
        jnp.int32
    )
    before = jnp.cumsum(onehot, axis=0) - onehot
    placed = jnp.sum(before * onehot, axis=1)
    slot_of = expert_of * capacity + placed
    slot_table = jnp.full((expert_count * capacity,), pair_count, jnp.int32)
    slot_table = slot_table.at[slot_of].set(jnp.arange(pair_count, dtype=jnp.int32))
    filled = slot_table < pair_count
    source = jnp.where(filled, slot_table, 0)
    owner_row = source // top_count
    send_x = jnp.where(filled[:, None], tokens[owner_row], jnp.zeros((), jnp.bfloat16))
    scaled = gate_values.reshape(-1)[source][:, None] * out_grad[owner_row].astype(jnp.float32)
    send_dy = jnp.where(filled[:, None], scaled, 0.0).astype(jnp.bfloat16)
    send_x = send_x.reshape(expert_count, capacity, model_width)
    send_dy = send_dy.reshape(expert_count, capacity, model_width)
    recv_x, recv_dy = (
        lax.all_to_all(send_x, "expert", split_axis=0, concat_axis=0, tiled=True),
        lax.all_to_all(send_dy, "expert", split_axis=0, concat_axis=0, tiled=True),
    )

    def to_local(stacked):
        shaped = stacked.reshape(group_count, local_count, capacity, model_width)
        return shaped.transpose(1, 0, 2, 3).reshape(local_count, slot_count, model_width)

    slot_x = to_local(recv_x)
    slot_dy = to_local(recv_dy)
    part_x = slot_x
    gate_term = jnp.einsum(
        "asd,adf->asf",
        part_x,
        lax.all_gather(w_gate, "dp", axis=1, tiled=True),
        preferred_element_type=jnp.float32,
    )
    up_term = jnp.einsum(
        "asd,adf->asf",
        part_x,
        lax.all_gather(w_up, "dp", axis=1, tiled=True),
        preferred_element_type=jnp.float32,
    )
    full_gate, full_up, full_down = (
        lax.all_gather(w_gate, "dp", axis=1, tiled=True),
        lax.all_gather(w_up, "dp", axis=1, tiled=True),
        lax.all_gather(w_down, "dp", axis=2, tiled=True),
    )
    sigma = jax.nn.sigmoid(gate_term)
    active = gate_term * sigma
    activated = (active * up_term).astype(jnp.bfloat16)
    back_hidden = jnp.einsum("asd,afd->asf", slot_dy, full_down, preferred_element_type=jnp.float32)
    up_delta = (back_hidden * active).astype(jnp.bfloat16)
    gate_delta = (back_hidden * up_term * sigma * (1.0 + gate_term * (1.0 - sigma))).astype(
        jnp.bfloat16
    )
    pair_grad = (
        jnp.einsum("asf,adf->asd", gate_delta, full_gate, preferred_element_type=jnp.float32)
        + jnp.einsum("asf,adf->asd", up_delta, full_up, preferred_element_type=jnp.float32)
    ).astype(jnp.bfloat16)
    send_back = pair_grad.reshape(local_count, group_count, capacity, model_width).transpose(
        1, 0, 2, 3
    )
    send_back = send_back.reshape(expert_count, capacity, model_width)
    returned = lax.all_to_all(send_back, "expert", split_axis=0, concat_axis=0, tiled=True)
    per_pair = returned.reshape(expert_count * capacity, model_width)[slot_of].astype(jnp.float32)
    input_grad = jnp.sum(per_pair.reshape(tok_rows, top_count, model_width), axis=1).astype(
        jnp.bfloat16
    )
    block_width = local_count * hidden_units
    share_width = model_width // lax.axis_size("dp")
    part_x = slot_x
    term_gate = jnp.einsum("asd,asf->daf", part_x, gate_delta, preferred_element_type=jnp.float32)
    term_up = jnp.einsum("asd,asf->daf", part_x, up_delta, preferred_element_type=jnp.float32)
    term_down = jnp.einsum("asd,asf->daf", slot_dy, activated, preferred_element_type=jnp.float32)
    shares = lax.psum_scatter(
        jnp.concatenate(
            [
                term_gate.reshape(lax.axis_size("dp") * share_width, block_width),
                term_up.reshape(lax.axis_size("dp") * share_width, block_width),
                term_down.reshape(lax.axis_size("dp") * share_width, block_width),
            ],
            axis=1,
        ).astype(jnp.bfloat16),
        "dp",
        scatter_dimension=0,
        tiled=True,
    ).astype(jnp.float32)
    share_rows = shares.shape[0]

    def unpack(which):
        return shares[:, which * block_width : (which + 1) * block_width].reshape(
            share_rows, local_count, hidden_units
        )

    gate_grad = unpack(0).transpose(1, 0, 2).astype(jnp.bfloat16)
    up_grad = unpack(1).transpose(1, 0, 2).astype(jnp.bfloat16)
    down_grad = unpack(2).transpose(1, 2, 0).astype(jnp.bfloat16)
    return (input_grad, gate_grad, up_grad, down_grad)


def lined(dp, expert):
    return dp == 4 and expert == 8


def local(tokens, out_grad, routes, gate_values, w_gate, w_up, w_down):
    experts = lax.axis_size("expert") * w_gate.shape[0]
    capacity = slots_of(tokens.shape[0], routes.shape[1], experts)
    fits = w_gate.shape[0] == 1 and tokens.shape[0] <= 2 * capacity
    if not (fits and lined(lax.axis_size("dp"), lax.axis_size("expert"))):
        return routed(tokens, out_grad, routes, gate_values, w_gate, w_up, w_down)
    return dense(tokens, out_grad, routes, gate_values, w_gate, w_up, w_down)


def solution(mesh):
    return jax.shard_map(
        local,
        mesh=mesh,
        in_specs=(
            P(("dp", "expert"), None),
            P(("dp", "expert"), None),
            P(("dp", "expert"), None),
            P(("dp", "expert"), None),
            P("expert", "dp", None),
            P("expert", "dp", None),
            P("expert", None, "dp"),
        ),
        out_specs=(
            P(("dp", "expert"), None),
            P("expert", "dp", None),
            P("expert", "dp", None),
            P("expert", None, "dp"),
        ),
        check_vma=False,
    )
```

```python
import jax
import jax.numpy as jnp
from jax import lax
from jax.experimental import pallas as pl
from jax.experimental.pallas import tpu as pltpu
from jax.sharding import PartitionSpec as P


F32 = jnp.float32
BF16 = jnp.bfloat16
ANY = pl.BlockSpec(memory_space=pl.ANY)
VMEM = pl.BlockSpec(memory_space=pltpu.VMEM)
SMEM = pl.BlockSpec(memory_space=pltpu.SMEM)
LIMIT = 24 * 1024 * 1024
NN = (((1,), (0,)), ((), ()))
NT = (((1,), (1,)), ((), ()))


def mm(a, b, dims):
    return lax.dot_general(a, b, dims, preferred_element_type=F32)


def slots_of(tok_rows, top_count, expert_count):
    return min(tok_rows, max(2, 9 * tok_rows * top_count // (8 * expert_count)))


def call(body, outs, ins, scratch, flops, moved, aliases=None):
    return pl.pallas_call(
        body,
        input_output_aliases=aliases or {},
        out_shape=[jax.ShapeDtypeStruct(s, d) for s, d, _ in outs],
        in_specs=[s for _, s in ins],
        out_specs=[s for _, _, s in outs],
        scratch_shapes=scratch,
        compiler_params=pltpu.CompilerParams(vmem_limit_bytes=LIMIT),
        cost_estimate=pl.CostEstimate(flops=flops, bytes_accessed=moved, transcendentals=0),
    )(*[a for a, _ in ins])


TWO = ((0, 2), (1, 3), (2, 0), (3, 1))
OUTER = ((0, 1), (1, 0), (2, 3), (3, 2))
INNER = ((1, 2), (2, 1))


class Copies:
    def __init__(self, sems):
        self.sems, self.used = sems, 0

    def start(self, src, dst):
        copy = pltpu.make_async_copy(src, dst, self.sems.at[self.used])
        self.used += 1
        copy.start()
        return copy

    def pick(self, first, src, other, dst):
        sem = self.sems.at[self.used]
        self.used += 1

        @pl.when(first)
        def _():
            pltpu.make_async_copy(src, dst, sem).start()

        @pl.when(jnp.logical_not(first))
        def _():
            pltpu.make_async_copy(other, dst, sem).start()

        return pltpu.make_async_copy(other, dst, sem)


def load_early(copies, pieces, dst, first=0):
    tok = pieces[0].shape[0]
    return [copies.start(src, dst.at[pl.ds((first + i) * tok, tok)]) for i, src in enumerate(pieces)]


def load_weights(copies, place, which, pieces, wg, wu):
    share = pieces[0].shape[0]
    started = []
    for i, k in enumerate(which):
        at = pl.ds((place[0] ^ k) * share, share)
        started += [copies.start(pieces[2 * i], wg.at[at]), copies.start(pieces[2 * i + 1], wu.at[at])]
    return started


def own_body(place, tokens, w_gate, w_up, x, wg, wu, sems):
    copies = Copies(sems)
    started = load_early(copies, (tokens,), x) + load_weights(copies, place, (0,), (w_gate, w_up), wg, wu)
    for c in started:
        c.wait()


def near_body(place, *refs):
    pieces, weights = refs[:5], refs[5:9]
    x, wg, wu, sems = refs[12:]
    copies = Copies(sems)
    for c in load_early(copies, pieces, x, 1) + load_weights(copies, place, (1, 2), weights, wg, wu):
        c.wait()


def load_late(copies, chip, pieces, dst):
    tok = pieces[0].shape[0]
    middle = jnp.logical_or(chip == 1, chip == 2)
    return [
        copies.pick(middle, pieces[2 * core], pieces[2 * core + 1], dst.at[pl.ds(core * tok, tok)]) for core in (0, 1)
    ]


def pre_blocks(x, first, count, wg, wu, act, active_out, slope_out):
    tn = 256

    def step(i, _):
        r = slice(first, first + count)
        c = pl.ds(pl.multiple_of(i * tn, tn), tn)
        lhs = x[r, :]
        gate = mm(lhs, wg[:, c], NN)
        up = mm(lhs, wu[:, c], NN)
        sigma = jax.nn.sigmoid(gate)
        active = gate * sigma
        act[r, c] = (active * up).astype(BF16)
        active_out[r, c] = active
        slope_out[r, c] = up * sigma * (1.0 + gate * (1.0 - sigma))
        return 0

    lax.fori_loop(0, wg.shape[1] // tn, step, 0)


def pre_early_body(place, *refs):
    act, active, slope, wg, wu, sems = refs[5:]
    for c in load_weights(Copies(sems), place, (3,), refs[:2], wg, wu):
        c.wait()
    x = refs[2]
    pre_blocks(x, 0, x.shape[0] // 4 * 3, wg, wu, act, active, slope)


def pre_late_body(place, *refs):
    pieces, wg, wu = refs[:4], refs[4], refs[5]
    act, active, slope, x, sems = refs[10:]
    count = x.shape[0] // 4
    for c in load_late(Copies(sems), place[1], pieces, x.at[pl.ds(3 * count, count)]):
        c.wait()
    pre_blocks(x, 3 * count, count, wg, wu, act, active, slope)


def scale(gates, place, which, raw, y, first):
    tok = raw.shape[0] // 2
    chip, core = place[1], place[2] % 2
    source = {"own": chip, "two": (chip + 2) % 4, "outer": chip ^ 1, "last": 3 - chip}[which]
    column = jnp.transpose(gates[...])
    lane = lax.broadcasted_iota(jnp.int32, column.shape, 1)
    for i in (0, 1):
        gate = jnp.sum(jnp.where(lane == 2 * source + (core ^ i), column, 0.0), axis=1, keepdims=True)
        r = slice(i * tok, (i + 1) * tok)
        y[pl.ds(first[i], tok), :] = (raw[r, :].astype(F32) * gate).astype(BF16)


def scale_early_body(place, *refs):
    pieces, gates = refs[:6], refs[6]
    y, raw, sems = refs[7:]
    tok = pieces[0].shape[0]
    copies = Copies(sems)
    started = []
    for i in range(3):
        at = [raw.at[pl.ds((2 * i + c) * tok, tok)] for c in (0, 1)]
        started.append((copies.start(pieces[i], at[0]), copies.start(pieces[3 + i], at[1])))
    for i, which in enumerate(("own", "two", "outer")):
        for c in started[i]:
            c.wait()
        scale(gates, place, which, raw.at[pl.ds(2 * i * tok, 2 * tok)], y, (i * tok, (3 + i) * tok))


def down_send_body(place, *refs):
    pieces, gates, act = refs[:4], refs[4], refs[5]
    send_a, send_b, y, raw, sems = refs[7:]
    tok = raw.shape[0] // 2
    for c in load_late(Copies(sems), place[1], pieces, raw):
        c.wait()
    scale(gates, place, "last", raw, y, (6 * tok, 7 * tok))
    down_blocks(place, act, y, ((0, 1, send_a, 0), (0, 3, send_a, 1), (1, 2, send_b, 0), (1, 3, send_b, 1)))


def down_blocks(place, act, y, wanted):
    share = y.shape[1] // 4
    half = act.shape[1] // 2
    for h in (0, 1):
        turned = jnp.transpose(act[:, h * half : (h + 1) * half])
        for which, k, dst, slot in wanted:
            if which == h:
                cols = pl.ds(pl.multiple_of((place[0] ^ k) * share, share), share)
                value = mm(turned, y[:, cols], NN).astype(BF16)
                if slot is None:
                    dst[...] = value
                else:
                    dst[slot] = value


def down_keep_body(place, act, y, a0, a1, b0, b1):
    down_blocks(place, act, y, ((0, 0, a0, None), (0, 2, a1, None), (1, 0, b0, None), (1, 1, b1, None)))


def back_body(place, y, active, slope, *refs):
    own, halves = refs[0], refs[1:7]
    gate_delta, up_delta, w, sems = refs[7:]
    me = place[0]
    copies = Copies(sems)
    hidden, share = own.shape
    half = hidden // 2
    started = [copies.start(own, w.at[me])]
    for i, src in enumerate(halves):
        started.append(copies.start(src, w.at[me ^ (1 + i // 2), pl.ds(i % 2 * half, half)]))
    for c in started:
        c.wait()
    rows = y.shape[0]
    tm, tn = rows // 2, 256

    def step(i, _):
        r = pl.ds(pl.multiple_of(i // (hidden // tn) * tm, tm), tm)
        c = pl.ds(pl.multiple_of(i % (hidden // tn) * tn, tn), tn)
        back = mm(y[r, 0:share], w[0, c, :], NT)
        for j in range(1, 4):
            back += mm(y[r, j * share : (j + 1) * share], w[j, c, :], NT)
        up_delta[r, c] = (back * active[r, c]).astype(BF16)
        gate_delta[r, c] = (back * slope[r, c]).astype(BF16)
        return 0

    lax.fori_loop(0, 2 * (hidden // tn), step, 0)


def grad_blocks(place, x, wanted):
    share = x.shape[1] // 4
    tm = share // 2
    for k, targets in wanted:

        def step(i, _, k=k, targets=targets):
            cols = pl.ds(pl.multiple_of((place[0] ^ k) * share + i * tm, tm), tm)
            turned = jnp.transpose(x[:, cols])
            part = pl.ds(pl.multiple_of(i * tm, tm), tm)
            for delta, dst, slot in targets:
                value = mm(turned, delta[...], NN).astype(BF16)
                if slot is None:
                    dst[part, :] = value
                else:
                    dst[slot, part, :] = value
            return 0

        lax.fori_loop(0, 2, step, 0)


def grad_send_body(place, x, gd, ud, gate_send, up_send):
    grad_blocks(
        place, x, ((1, [(gd, gate_send, 0)]), (3, [(gd, gate_send, 1), (ud, up_send, 1)]), (2, [(ud, up_send, 0)]))
    )


def grad_keep_body(place, x, gd, ud, g0, g1, u0, u1):
    grad_blocks(place, x, ((2, [(gd, g1, None)]), (1, [(ud, u1, None)]), (0, [(gd, g0, None), (ud, u0, None)])))


def pair_body(gate_delta, up_delta, wg, wu, send, keep):
    tn = 256
    part = keep.shape[0] // 4

    def step(i, _):
        c = pl.ds(pl.multiple_of(i * tn, tn), tn)
        total = (mm(gate_delta[...], wg[c, :], NT) + mm(up_delta[...], wu[c, :], NT)).astype(BF16)
        keep[: 3 * part, c] = total[: 3 * part]
        send[: 3 * part, c] = total[3 * part : 6 * part]
        keep[3 * part :, c] = total[6 * part : 7 * part]
        send[3 * part :, c] = total[7 * part :]
        return 0

    lax.fori_loop(0, wg.shape[0] // tn, step, 0)


def add(*terms):
    total = terms[0].astype(F32)
    for term in terms[1:]:
        total = total + term.astype(F32)
    return total.astype(BF16)


def dense(tokens, out_grad, routes, gate_values, w_gate, w_up, w_down):
    tok, width = tokens.shape
    experts = lax.axis_size("expert")
    chips = experts // 2
    hidden = w_gate.shape[2]
    share = width // 4
    half = hidden // 2
    rows = experts * tok
    expert = lax.axis_index("expert")
    chip = expert // 2
    place = jnp.stack([lax.axis_index("dp"), chip, expert]).astype(jnp.int32)

    def to_x(block):
        return lax.ppermute(block, "dp", [(i, i ^ 1) for i in range(4)])

    def to_y(block):
        return lax.ppermute(block, "dp", [(i, i ^ 2) for i in range(4)])

    def hop(block, moves):
        return lax.ppermute(block, "expert", [(2 * a + c, 2 * b + c) for a, b in moves for c in (0, 1)])

    def swap(block, at=range(chips)):
        return lax.ppermute(block, "expert", [(2 * z + c, 2 * z + 1 - c) for z in at for c in (0, 1)])

    def line(own):
        two = hop(own, TWO)
        outer = hop(own, OUTER)
        inner = hop(own, INNER)
        far = hop(two, ((2, 3), (1, 0)))
        early = [own, two, outer, swap(own), swap(two), swap(outer)]
        late = [inner, far, swap(inner, (1, 2)), swap(far, (0, 3))]
        return early, late

    x_early, x_late = line(tokens)
    onehot = routes[:, :, None] == jnp.arange(experts, dtype=routes.dtype)
    gates = jnp.sum(jnp.where(onehot, gate_values[:, :, None], 0.0), axis=1).T.reshape(experts, 1, tok)
    gates = lax.all_to_all(gates, "expert", split_axis=0, concat_axis=0, tiled=True)
    gates = gates.reshape(experts, tok)
    y_early, y_late = line(out_grad)

    wg0, wu0, wd0 = w_gate[0], w_up[0], w_down[0]
    wg1, wu2 = to_x(wg0), to_y(wu0)
    wg2, wu1 = to_y(wg0), to_x(wu0)
    wg3, wu3 = to_y(wg1), to_x(wu2)
    da0, db0 = wd0[:half], wd0[half:]
    da1, db2 = to_x(da0), to_y(db0)
    da2, db1 = to_y(da0), to_x(db0)
    da3, db3 = to_y(da1), to_x(db2)

    def dma(n):
        return pltpu.SemaphoreType.DMA((n,))

    def anys(arrays):
        return [(a, ANY) for a in arrays]

    x_out = ((rows, width), BF16, VMEM)
    weight = ((width, hidden), BF16, VMEM)
    flat = ((rows, hidden), BF16, VMEM)
    wide = ((rows, hidden), F32, VMEM)
    x, wg, wu = call(
        own_body,
        [x_out, weight, weight],
        [(place, SMEM)] + anys((tokens, wg0, wu0)),
        [dma(3)],
        1000,
        width * (2 * tok + hidden),
    )
    x, wg, wu = call(
        near_body,
        [x_out, weight, weight],
        [(place, SMEM)] + anys(x_early[1:]) + anys((wg1, wu1, wg2, wu2)) + [(x, VMEM), (wg, VMEM), (wu, VMEM)],
        [dma(9)],
        1000,
        width * (10 * tok + 2 * hidden),
        {10: 0, 11: 1, 12: 2},
    )
    *pre, wg, wu = call(
        pre_early_body,
        [flat, wide, wide, weight, weight],
        [(place, SMEM)] + anys((wg3, wu3)) + [(x, VMEM), (wg, VMEM), (wu, VMEM)],
        [dma(2)],
        3 * rows * width * hidden,
        3 * rows * width + 8 * width * hidden + 8 * rows * hidden,
        {4: 3, 5: 4},
    )
    act, active, slope, x = call(
        pre_late_body,
        [flat, wide, wide, x_out],
        [(place, SMEM)] + anys(x_late) + [(a, VMEM) for a in (wg, wu, *pre, x)],
        [dma(2)],
        rows * width * hidden,
        rows * width + 4 * width * hidden + 3 * rows * hidden,
        {7 + i: i for i in range(4)},
    )
    (y,) = call(
        scale_early_body,
        [((rows, width), BF16, VMEM)],
        [(place, SMEM)] + anys(y_early) + [(gates, VMEM)],
        [pltpu.VMEM((6 * tok, width), BF16), dma(6)],
        rows * width,
        4 * rows * width,
    )
    piece = (2, half, share)
    send_a, send_b, y = call(
        down_send_body,
        [(piece, BF16, VMEM)] * 2 + [((rows, width), BF16, VMEM)],
        [(place, SMEM)] + anys(y_late) + [(gates, VMEM), (act, VMEM), (y, VMEM)],
        [pltpu.VMEM((2 * tok, width), BF16), dma(2)],
        rows * width * hidden,
        2 * (2 * rows * width + rows * hidden + width * hidden // 2),
        {7: 2},
    )
    got_a, got_b = to_x(send_a), to_y(send_b)
    gate_delta, up_delta = call(
        back_body,
        [((rows, hidden), BF16, VMEM)] * 2,
        [(place, SMEM), (y, VMEM), (active, VMEM), (slope, VMEM)] + anys((wd0, da1, db1, da2, db2, da3, db3)),
        [pltpu.VMEM((4, hidden, share), BF16), dma(7)],
        2 * rows * width * hidden,
        2 * (rows * width + width * hidden) + 12 * rows * hidden,
    )
    gate_send, up_send = call(
        grad_send_body,
        [((2, share, hidden), BF16, VMEM)] * 2,
        [(place, SMEM), (x, VMEM), (gate_delta, VMEM), (up_delta, VMEM)],
        [],
        2 * rows * width * hidden,
        2 * (rows * width + 2 * rows * hidden + width * hidden),
    )
    gate_got, up_got = to_x(gate_send), to_y(up_send)
    pair_send, pair_keep = call(
        pair_body,
        [((rows // 2, width), BF16, VMEM)] * 2,
        [(gate_delta, VMEM), (up_delta, VMEM), (wg, VMEM), (wu, VMEM)],
        [],
        4 * rows * width * hidden,
        2 * (rows * width + 2 * rows * hidden + 2 * width * hidden),
    )
    total = add(pair_keep, swap(pair_send)).reshape(chips, tok, width)
    keep_a0, keep_a1, keep_b0, keep_b1 = call(
        down_keep_body,
        [((half, share), BF16, VMEM)] * 4,
        [(place, SMEM), (act, VMEM), (y, VMEM)],
        [],
        rows * width * hidden,
        2 * (rows * width + rows * hidden + width * hidden // 2),
    )
    gate0, gate1, up0, up1 = call(
        grad_keep_body,
        [((share, hidden), BF16, VMEM)] * 4,
        [(place, SMEM), (x, VMEM), (gate_delta, VMEM), (up_delta, VMEM)],
        [],
        2 * rows * width * hidden,
        2 * (rows * width + 2 * rows * hidden + width * hidden),
    )
    down_a, down_b = to_y(add(keep_a1, got_a[1])), to_x(add(keep_b1, got_b[1]))
    gate1, up1 = add(gate1, gate_got[1]), add(up1, up_got[1])
    sums = add(gate0, gate_got[0]), add(up0, up_got[0])
    gate_last, up_last = to_y(gate1), to_x(up1)
    gate_sum, up_sum = lax.optimization_barrier(sums)
    down_grad = jnp.concatenate([add(keep_a0, got_a[0], down_a), add(keep_b0, got_b[0], down_b)], axis=0)
    gate_grad, up_grad = add(gate_sum, gate_last), add(up_sum, up_last)

    far = hop(total[3], ((0, 1), (3, 2)))
    inner = hop(total[3], INNER)
    outer = hop(total[2], OUTER)
    two = hop(add(total[1], far), TWO)
    input_grad = add(total[0], inner, outer, two)
    return input_grad, gate_grad[None], up_grad[None], down_grad[None]


def routed(tokens, out_grad, routes, gate_values, w_gate, w_up, w_down):
    tok_rows, model_width = tokens.shape
    top_count = routes.shape[1]
    group_count = lax.axis_size("expert")
    local_count = w_gate.shape[0]
    expert_count = group_count * local_count
    hidden_units = w_gate.shape[2]
    capacity = slots_of(tok_rows, top_count, expert_count)
    pair_count = tok_rows * top_count
    slot_count = group_count * capacity
    expert_of = routes.reshape(-1)
    onehot = (expert_of[:, None] == jnp.arange(expert_count, dtype=jnp.int32)[None, :]).astype(
        jnp.int32
    )
    before = jnp.cumsum(onehot, axis=0) - onehot
    placed = jnp.sum(before * onehot, axis=1)
    slot_of = expert_of * capacity + placed
    slot_table = jnp.full((expert_count * capacity,), pair_count, jnp.int32)
    slot_table = slot_table.at[slot_of].set(jnp.arange(pair_count, dtype=jnp.int32))
    filled = slot_table < pair_count
    source = jnp.where(filled, slot_table, 0)
    owner_row = source // top_count
    send_x = jnp.where(filled[:, None], tokens[owner_row], jnp.zeros((), jnp.bfloat16))
    scaled = gate_values.reshape(-1)[source][:, None] * out_grad[owner_row].astype(jnp.float32)
    send_dy = jnp.where(filled[:, None], scaled, 0.0).astype(jnp.bfloat16)
    send_x = send_x.reshape(expert_count, capacity, model_width)
    send_dy = send_dy.reshape(expert_count, capacity, model_width)
    recv_x, recv_dy = (
        lax.all_to_all(send_x, "expert", split_axis=0, concat_axis=0, tiled=True),
        lax.all_to_all(send_dy, "expert", split_axis=0, concat_axis=0, tiled=True),
    )

    def to_local(stacked):
        shaped = stacked.reshape(group_count, local_count, capacity, model_width)
        return shaped.transpose(1, 0, 2, 3).reshape(local_count, slot_count, model_width)

    slot_x = to_local(recv_x)
    slot_dy = to_local(recv_dy)
    part_x = slot_x
    gate_term = jnp.einsum(
        "asd,adf->asf",
        part_x,
        lax.all_gather(w_gate, "dp", axis=1, tiled=True),
        preferred_element_type=jnp.float32,
    )
    up_term = jnp.einsum(
        "asd,adf->asf",
        part_x,
        lax.all_gather(w_up, "dp", axis=1, tiled=True),
        preferred_element_type=jnp.float32,
    )
    full_gate, full_up, full_down = (
        lax.all_gather(w_gate, "dp", axis=1, tiled=True),
        lax.all_gather(w_up, "dp", axis=1, tiled=True),
        lax.all_gather(w_down, "dp", axis=2, tiled=True),
    )
    sigma = jax.nn.sigmoid(gate_term)
    active = gate_term * sigma
    activated = (active * up_term).astype(jnp.bfloat16)
    back_hidden = jnp.einsum("asd,afd->asf", slot_dy, full_down, preferred_element_type=jnp.float32)
    up_delta = (back_hidden * active).astype(jnp.bfloat16)
    gate_delta = (back_hidden * up_term * sigma * (1.0 + gate_term * (1.0 - sigma))).astype(
        jnp.bfloat16
    )
    pair_grad = (
        jnp.einsum("asf,adf->asd", gate_delta, full_gate, preferred_element_type=jnp.float32)
        + jnp.einsum("asf,adf->asd", up_delta, full_up, preferred_element_type=jnp.float32)
    ).astype(jnp.bfloat16)
    send_back = pair_grad.reshape(local_count, group_count, capacity, model_width).transpose(
        1, 0, 2, 3
    )
    send_back = send_back.reshape(expert_count, capacity, model_width)
    returned = lax.all_to_all(send_back, "expert", split_axis=0, concat_axis=0, tiled=True)
    per_pair = returned.reshape(expert_count * capacity, model_width)[slot_of].astype(jnp.float32)
    input_grad = jnp.sum(per_pair.reshape(tok_rows, top_count, model_width), axis=1).astype(
        jnp.bfloat16
    )
    block_width = local_count * hidden_units
    share_width = model_width // lax.axis_size("dp")
    part_x = slot_x
    term_gate = jnp.einsum("asd,asf->daf", part_x, gate_delta, preferred_element_type=jnp.float32)
    term_up = jnp.einsum("asd,asf->daf", part_x, up_delta, preferred_element_type=jnp.float32)
    term_down = jnp.einsum("asd,asf->daf", slot_dy, activated, preferred_element_type=jnp.float32)
    shares = lax.psum_scatter(
        jnp.concatenate(
            [
                term_gate.reshape(lax.axis_size("dp") * share_width, block_width),
                term_up.reshape(lax.axis_size("dp") * share_width, block_width),
                term_down.reshape(lax.axis_size("dp") * share_width, block_width),
            ],
            axis=1,
        ).astype(jnp.bfloat16),
        "dp",
        scatter_dimension=0,
        tiled=True,
    ).astype(jnp.float32)
    share_rows = shares.shape[0]

    def unpack(which):
        return shares[:, which * block_width : (which + 1) * block_width].reshape(
            share_rows, local_count, hidden_units
        )

    gate_grad = unpack(0).transpose(1, 0, 2).astype(jnp.bfloat16)
    up_grad = unpack(1).transpose(1, 0, 2).astype(jnp.bfloat16)
    down_grad = unpack(2).transpose(1, 2, 0).astype(jnp.bfloat16)
    return (input_grad, gate_grad, up_grad, down_grad)


def lined(dp, expert):
    return dp == 4 and expert == 8


def local(tokens, out_grad, routes, gate_values, w_gate, w_up, w_down):
    experts = lax.axis_size("expert") * w_gate.shape[0]
    capacity = slots_of(tokens.shape[0], routes.shape[1], experts)
    fits = w_gate.shape[0] == 1 and tokens.shape[0] <= 2 * capacity
    if not (fits and lined(lax.axis_size("dp"), lax.axis_size("expert"))):
        return routed(tokens, out_grad, routes, gate_values, w_gate, w_up, w_down)
    return dense(tokens, out_grad, routes, gate_values, w_gate, w_up, w_down)


def solution(mesh):
    return jax.shard_map(
        local,
        mesh=mesh,
        in_specs=(
            P(("dp", "expert"), None),
            P(("dp", "expert"), None),
            P(("dp", "expert"), None),
            P(("dp", "expert"), None),
            P("expert", "dp", None),
            P("expert", "dp", None),
            P("expert", None, "dp"),
        ),
        out_specs=(
            P(("dp", "expert"), None),
            P("expert", "dp", None),
            P("expert", "dp", None),
            P("expert", None, "dp"),
        ),
        check_vma=False,
    )
```

```python
import jax
import jax.numpy as jnp
from jax import lax
from jax.experimental import pallas as pl
from jax.experimental.pallas import tpu as pltpu
from jax.sharding import PartitionSpec as P


F32 = jnp.float32
BF16 = jnp.bfloat16
ANY = pl.BlockSpec(memory_space=pl.ANY)
VMEM = pl.BlockSpec(memory_space=pltpu.VMEM)
SMEM = pl.BlockSpec(memory_space=pltpu.SMEM)
LIMIT = 12 * 1024 * 1024
NN = (((1,), (0,)), ((), ()))
NT = (((1,), (1,)), ((), ()))


def mm(a, b, dims):
    return lax.dot_general(a, b, dims, preferred_element_type=F32)


def slots_of(tok_rows, top_count, expert_count):
    return min(tok_rows, max(2, 9 * tok_rows * top_count // (8 * expert_count)))


def call(body, outs, ins, scratch, flops, moved, aliases=None):
    return pl.pallas_call(
        body,
        input_output_aliases=aliases or {},
        out_shape=[jax.ShapeDtypeStruct(s, d) for s, d, _ in outs],
        in_specs=[s for _, s in ins],
        out_specs=[s for _, _, s in outs],
        scratch_shapes=scratch,
        compiler_params=pltpu.CompilerParams(vmem_limit_bytes=LIMIT),
        cost_estimate=pl.CostEstimate(flops=flops, bytes_accessed=moved, transcendentals=0),
    )(*[a for a, _ in ins])


TWO = ((0, 2), (1, 3), (2, 0), (3, 1))
OUTER = ((0, 1), (1, 0), (2, 3), (3, 2))
INNER = ((1, 2), (2, 1))


class Copies:
    def __init__(self, sems):
        self.sems, self.used = sems, 0

    def start(self, src, dst):
        copy = pltpu.make_async_copy(src, dst, self.sems.at[self.used])
        self.used += 1
        copy.start()
        return copy

    def pick(self, first, src, other, dst):
        sem = self.sems.at[self.used]
        self.used += 1

        @pl.when(first)
        def _():
            pltpu.make_async_copy(src, dst, sem).start()

        @pl.when(jnp.logical_not(first))
        def _():
            pltpu.make_async_copy(other, dst, sem).start()

        return pltpu.make_async_copy(other, dst, sem)


def load_early(copies, pieces, dst, first=0):
    tok = pieces[0].shape[0]
    return [copies.start(src, dst.at[pl.ds((first + i) * tok, tok)]) for i, src in enumerate(pieces)]


def load_weights(copies, place, which, pieces, wg, wu):
    share = pieces[0].shape[0]
    started = []
    for i, k in enumerate(which):
        at = pl.ds((place[0] ^ k) * share, share)
        started += [copies.start(pieces[2 * i], wg.at[at]), copies.start(pieces[2 * i + 1], wu.at[at])]
    return started


def own_body(place, gates, tokens, w_gate, w_up, column, x, wg, wu, sems):
    copies = Copies(sems)
    started = load_early(copies, (tokens,), x) + load_weights(copies, place, (0,), (w_gate, w_up), wg, wu)
    column[...] = jnp.transpose(gates[...])
    for c in started:
        c.wait()


def near_body(place, *refs):
    pieces, weights = refs[:5], refs[5:9]
    x, wg, wu, sems = refs[12:]
    copies = Copies(sems)
    for c in load_early(copies, pieces, x, 1) + load_weights(copies, place, (1, 2), weights, wg, wu):
        c.wait()


def load_late(copies, chip, pieces, dst):
    tok = pieces[0].shape[0]
    middle = jnp.logical_or(chip == 1, chip == 2)
    return [
        copies.pick(middle, pieces[2 * core], pieces[2 * core + 1], dst.at[pl.ds(core * tok, tok)]) for core in (0, 1)
    ]


def pre_blocks(x, first, count, wg, wu, act, active_out, slope_out):
    tn = 256

    def step(i, _):
        r = slice(first, first + count)
        c = pl.ds(pl.multiple_of(i * tn, tn), tn)
        lhs = x[r, :]
        gate = mm(lhs, wg[:, c], NN)
        up = mm(lhs, wu[:, c], NN)
        sigma = jax.nn.sigmoid(gate)
        active = gate * sigma
        act[r, c] = (active * up).astype(BF16)
        active_out[r, c] = active
        slope_out[r, c] = up * sigma * (1.0 + gate * (1.0 - sigma))
        return 0

    lax.fori_loop(0, wg.shape[1] // tn, step, 0)


def pre_early_body(place, *refs):
    act, active, slope, wg, wu, sems = refs[5:]
    for c in load_weights(Copies(sems), place, (3,), refs[:2], wg, wu):
        c.wait()
    x = refs[2]
    pre_blocks(x, 0, x.shape[0] // 4 * 3, wg, wu, act, active, slope)


def pre_late_body(place, *refs):
    pieces, wg, wu = refs[:4], refs[4], refs[5]
    act, active, slope, x, sems = refs[10:]
    count = x.shape[0] // 4
    for c in load_late(Copies(sems), place[1], pieces, x.at[pl.ds(3 * count, count)]):
        c.wait()
    pre_blocks(x, 3 * count, count, wg, wu, act, active, slope)


def scale(gates, place, which, raw, y, first):
    tok = raw.shape[0] // 2
    chip, core = place[1], place[2] % 2
    source = {"own": chip, "two": (chip + 2) % 4, "outer": chip ^ 1, "last": 3 - chip}[which]
    lane = lax.broadcasted_iota(jnp.int32, gates.shape, 1)
    for i in (0, 1):
        gate = jnp.sum(jnp.where(lane == 2 * source + (core ^ i), gates[...], 0.0), axis=1, keepdims=True)
        r = slice(i * tok, (i + 1) * tok)
        y[pl.ds(first[i], tok), :] = (raw[r, :].astype(F32) * gate).astype(BF16)


def scale_early_body(place, *refs):
    pieces, gates = refs[:6], refs[6]
    y, raw, sems = refs[7:]
    tok = pieces[0].shape[0]
    copies = Copies(sems)
    started = []
    for i in range(3):
        at = [raw.at[pl.ds((2 * i + c) * tok, tok)] for c in (0, 1)]
        started.append((copies.start(pieces[i], at[0]), copies.start(pieces[3 + i], at[1])))
    for i, which in enumerate(("own", "two", "outer")):
        for c in started[i]:
            c.wait()
        scale(gates, place, which, raw.at[pl.ds(2 * i * tok, 2 * tok)], y, (i * tok, (3 + i) * tok))


def down_send_body(place, *refs):
    pieces, gates, act = refs[:4], refs[4], refs[5]
    send_a, send_b, y, raw, sems = refs[7:]
    tok = raw.shape[0] // 2
    for c in load_late(Copies(sems), place[1], pieces, raw):
        c.wait()
    scale(gates, place, "last", raw, y, (6 * tok, 7 * tok))
    down_blocks(place, act, y, ((0, 1, send_a, 0), (0, 3, send_a, 1), (1, 2, send_b, 0), (1, 3, send_b, 1)))


def down_blocks(place, act, y, wanted):
    share = y.shape[1] // 4
    half = act.shape[1] // 2
    for h in (0, 1):
        turned = jnp.transpose(act[:, h * half : (h + 1) * half])
        for which, k, dst, slot in wanted:
            if which == h:
                cols = pl.ds(pl.multiple_of((place[0] ^ k) * share, share), share)
                value = mm(turned, y[:, cols], NN).astype(BF16)
                if slot is None:
                    dst[...] = value
                else:
                    dst[slot] = value


def down_keep_body(place, act, y, a0, a1, b0, b1):
    down_blocks(place, act, y, ((0, 0, a0, None), (0, 2, a1, None), (1, 0, b0, None), (1, 1, b1, None)))


def back_body(place, y, active, slope, *refs):
    own, halves = refs[0], refs[1:7]
    gate_delta, up_delta, w, sems = refs[7:]
    me = place[0]
    copies = Copies(sems)
    hidden, share = own.shape
    half = hidden // 2
    started = [copies.start(own, w.at[me])]
    for i, src in enumerate(halves):
        started.append(copies.start(src, w.at[me ^ (1 + i // 2), pl.ds(i % 2 * half, half)]))
    for c in started:
        c.wait()
    rows = y.shape[0]
    tm, tn = rows // 2, 256

    def step(i, _):
        r = pl.ds(pl.multiple_of(i // (hidden // tn) * tm, tm), tm)
        c = pl.ds(pl.multiple_of(i % (hidden // tn) * tn, tn), tn)
        back = mm(y[r, 0:share], w[0, c, :], NT)
        for j in range(1, 4):
            back += mm(y[r, j * share : (j + 1) * share], w[j, c, :], NT)
        up_delta[r, c] = (back * active[r, c]).astype(BF16)
        gate_delta[r, c] = (back * slope[r, c]).astype(BF16)
        return 0

    lax.fori_loop(0, 2 * (hidden // tn), step, 0)


def grad_blocks(place, x, wanted):
    share = x.shape[1] // 4
    tm = share // 2
    for k, targets in wanted:

        def step(i, _, k=k, targets=targets):
            cols = pl.ds(pl.multiple_of((place[0] ^ k) * share + i * tm, tm), tm)
            turned = jnp.transpose(x[:, cols])
            part = pl.ds(pl.multiple_of(i * tm, tm), tm)
            for delta, dst, slot in targets:
                value = mm(turned, delta[...], NN).astype(BF16)
                if slot is None:
                    dst[part, :] = value
                else:
                    dst[slot, part, :] = value
            return 0

        lax.fori_loop(0, 2, step, 0)


def grad_send_body(place, x, gd, ud, gate_send, up_send):
    grad_blocks(
        place, x, ((1, [(gd, gate_send, 0)]), (3, [(gd, gate_send, 1), (ud, up_send, 1)]), (2, [(ud, up_send, 0)]))
    )


def grad_keep_body(place, x, gd, ud, g0, g1, u0, u1):
    grad_blocks(place, x, ((2, [(gd, g1, None)]), (1, [(ud, u1, None)]), (0, [(gd, g0, None), (ud, u0, None)])))


def pair_body(gate_delta, up_delta, wg, wu, send, keep):
    tn = 256
    part = keep.shape[0] // 4

    def step(i, _):
        c = pl.ds(pl.multiple_of(i * tn, tn), tn)
        total = (mm(gate_delta[...], wg[c, :], NT) + mm(up_delta[...], wu[c, :], NT)).astype(BF16)
        keep[: 3 * part, c] = total[: 3 * part]
        send[: 3 * part, c] = total[3 * part : 6 * part]
        keep[3 * part :, c] = total[6 * part : 7 * part]
        send[3 * part :, c] = total[7 * part :]
        return 0

    lax.fori_loop(0, wg.shape[0] // tn, step, 0)


def add(*terms):
    total = terms[0].astype(F32)
    for term in terms[1:]:
        total = total + term.astype(F32)
    return total.astype(BF16)


def dense(tokens, out_grad, routes, gate_values, w_gate, w_up, w_down):
    tok, width = tokens.shape
    experts = lax.axis_size("expert")
    chips = experts // 2
    hidden = w_gate.shape[2]
    share = width // 4
    half = hidden // 2
    rows = experts * tok
    expert = lax.axis_index("expert")
    chip = expert // 2
    place = jnp.stack([lax.axis_index("dp"), chip, expert]).astype(jnp.int32)

    def to_x(block):
        return lax.ppermute(block, "dp", [(i, i ^ 1) for i in range(4)])

    def to_y(block):
        return lax.ppermute(block, "dp", [(i, i ^ 2) for i in range(4)])

    def hop(block, moves):
        return lax.ppermute(block, "expert", [(2 * a + c, 2 * b + c) for a, b in moves for c in (0, 1)])

    def swap(block, at=range(chips)):
        return lax.ppermute(block, "expert", [(2 * z + c, 2 * z + 1 - c) for z in at for c in (0, 1)])

    def line(own):
        two = hop(own, TWO)
        outer = hop(own, OUTER)
        inner = hop(own, INNER)
        far = hop(two, ((2, 3), (1, 0)))
        early = [own, two, outer, swap(own), swap(two), swap(outer)]
        late = [inner, far, swap(inner, (1, 2)), swap(far, (0, 3))]
        return early, late

    x_early, x_late = line(tokens)
    onehot = routes[:, :, None] == jnp.arange(experts, dtype=routes.dtype)
    gates = jnp.sum(jnp.where(onehot, gate_values[:, :, None], 0.0), axis=1).T.reshape(experts, 1, tok)
    gates = lax.all_to_all(gates, "expert", split_axis=0, concat_axis=0, tiled=True)
    gates = gates.reshape(experts, tok)
    y_early, y_late = line(out_grad)

    wg0, wu0, wd0 = w_gate[0], w_up[0], w_down[0]
    wg1, wu2 = to_x(wg0), to_y(wu0)
    wg2, wu1 = to_y(wg0), to_x(wu0)
    wg3, wu3 = to_y(wg1), to_x(wu2)
    da0, db0 = wd0[:half], wd0[half:]
    da1, db2 = to_x(da0), to_y(db0)
    da2, db1 = to_y(da0), to_x(db0)
    da3, db3 = to_y(da1), to_x(db2)

    def dma(n):
        return pltpu.SemaphoreType.DMA((n,))

    def anys(arrays):
        return [(a, ANY) for a in arrays]

    x_out = ((rows, width), BF16, VMEM)
    weight = ((width, hidden), BF16, VMEM)
    flat = ((rows, hidden), BF16, VMEM)
    wide = ((rows, hidden), F32, VMEM)
    gates, x, wg, wu = call(
        own_body,
        [((tok, experts), F32, VMEM), x_out, weight, weight],
        [(place, SMEM), (gates, VMEM)] + anys((tokens, wg0, wu0)),
        [dma(3)],
        1000,
        width * (2 * tok + hidden),
    )
    x, wg, wu = call(
        near_body,
        [x_out, weight, weight],
        [(place, SMEM)] + anys(x_early[1:]) + anys((wg1, wu1, wg2, wu2)) + [(x, VMEM), (wg, VMEM), (wu, VMEM)],
        [dma(9)],
        1000,
        width * (10 * tok + 2 * hidden),
        {10: 0, 11: 1, 12: 2},
    )
    *pre, wg, wu = call(
        pre_early_body,
        [flat, wide, wide, weight, weight],
        [(place, SMEM)] + anys((wg3, wu3)) + [(x, VMEM), (wg, VMEM), (wu, VMEM)],
        [dma(2)],
        3 * rows * width * hidden,
        3 * rows * width + 8 * width * hidden + 8 * rows * hidden,
        {4: 3, 5: 4},
    )
    act, active, slope, x = call(
        pre_late_body,
        [flat, wide, wide, x_out],
        [(place, SMEM)] + anys(x_late) + [(a, VMEM) for a in (wg, wu, *pre, x)],
        [dma(2)],
        rows * width * hidden,
        rows * width + 4 * width * hidden + 3 * rows * hidden,
        {7 + i: i for i in range(4)},
    )
    (y,) = call(
        scale_early_body,
        [((rows, width), BF16, VMEM)],
        [(place, SMEM)] + anys(y_early) + [(gates, VMEM)],
        [pltpu.VMEM((6 * tok, width), BF16), dma(6)],
        rows * width,
        4 * rows * width,
    )
    piece = (2, half, share)
    send_a, send_b, y = call(
        down_send_body,
        [(piece, BF16, VMEM)] * 2 + [((rows, width), BF16, VMEM)],
        [(place, SMEM)] + anys(y_late) + [(gates, VMEM), (act, VMEM), (y, VMEM)],
        [pltpu.VMEM((2 * tok, width), BF16), dma(2)],
        rows * width * hidden,
        2 * (2 * rows * width + rows * hidden + width * hidden // 2),
        {7: 2},
    )
    got_a, got_b = to_x(send_a), to_y(send_b)
    gate_delta, up_delta = call(
        back_body,
        [((rows, hidden), BF16, VMEM)] * 2,
        [(place, SMEM), (y, VMEM), (active, VMEM), (slope, VMEM)] + anys((wd0, da1, db1, da2, db2, da3, db3)),
        [pltpu.VMEM((4, hidden, share), BF16), dma(7)],
        2 * rows * width * hidden,
        2 * (rows * width + width * hidden) + 12 * rows * hidden,
    )
    gate_send, up_send = call(
        grad_send_body,
        [((2, share, hidden), BF16, VMEM)] * 2,
        [(place, SMEM), (x, VMEM), (gate_delta, VMEM), (up_delta, VMEM)],
        [],
        2 * rows * width * hidden,
        2 * (rows * width + 2 * rows * hidden + width * hidden),
    )
    gate_got, up_got = to_x(gate_send), to_y(up_send)
    pair_send, pair_keep = call(
        pair_body,
        [((rows // 2, width), BF16, VMEM)] * 2,
        [(gate_delta, VMEM), (up_delta, VMEM), (wg, VMEM), (wu, VMEM)],
        [],
        4 * rows * width * hidden,
        2 * (rows * width + 2 * rows * hidden + 2 * width * hidden),
    )
    total = add(pair_keep, swap(pair_send)).reshape(chips, tok, width)
    keep_a0, keep_a1, keep_b0, keep_b1 = call(
        down_keep_body,
        [((half, share), BF16, VMEM)] * 4,
        [(place, SMEM), (act, VMEM), (y, VMEM)],
        [],
        rows * width * hidden,
        2 * (rows * width + rows * hidden + width * hidden // 2),
    )
    gate0, gate1, up0, up1 = call(
        grad_keep_body,
        [((share, hidden), BF16, VMEM)] * 4,
        [(place, SMEM), (x, VMEM), (gate_delta, VMEM), (up_delta, VMEM)],
        [],
        2 * rows * width * hidden,
        2 * (rows * width + 2 * rows * hidden + width * hidden),
    )
    down_a, down_b = to_y(add(keep_a1, got_a[1])), to_x(add(keep_b1, got_b[1]))
    gate1, up1 = add(gate1, gate_got[1]), add(up1, up_got[1])
    sums = add(gate0, gate_got[0]), add(up0, up_got[0])
    gate_last, up_last = to_y(gate1), to_x(up1)
    gate_sum, up_sum = lax.optimization_barrier(sums)
    down_grad = jnp.concatenate([add(keep_a0, got_a[0], down_a), add(keep_b0, got_b[0], down_b)], axis=0)
    gate_grad, up_grad = add(gate_sum, gate_last), add(up_sum, up_last)

    far = hop(total[3], ((0, 1), (3, 2)))
    inner = hop(total[3], INNER)
    outer = hop(total[2], OUTER)
    two = hop(add(total[1], far), TWO)
    input_grad = add(total[0], inner, outer, two)
    return input_grad, gate_grad[None], up_grad[None], down_grad[None]


def routed(tokens, out_grad, routes, gate_values, w_gate, w_up, w_down):
    tok_rows, model_width = tokens.shape
    top_count = routes.shape[1]
    group_count = lax.axis_size("expert")
    local_count = w_gate.shape[0]
    expert_count = group_count * local_count
    hidden_units = w_gate.shape[2]
    capacity = slots_of(tok_rows, top_count, expert_count)
    pair_count = tok_rows * top_count
    slot_count = group_count * capacity
    expert_of = routes.reshape(-1)
    onehot = (expert_of[:, None] == jnp.arange(expert_count, dtype=jnp.int32)[None, :]).astype(
        jnp.int32
    )
    before = jnp.cumsum(onehot, axis=0) - onehot
    placed = jnp.sum(before * onehot, axis=1)
    slot_of = expert_of * capacity + placed
    slot_table = jnp.full((expert_count * capacity,), pair_count, jnp.int32)
    slot_table = slot_table.at[slot_of].set(jnp.arange(pair_count, dtype=jnp.int32))
    filled = slot_table < pair_count
    source = jnp.where(filled, slot_table, 0)
    owner_row = source // top_count
    send_x = jnp.where(filled[:, None], tokens[owner_row], jnp.zeros((), jnp.bfloat16))
    scaled = gate_values.reshape(-1)[source][:, None] * out_grad[owner_row].astype(jnp.float32)
    send_dy = jnp.where(filled[:, None], scaled, 0.0).astype(jnp.bfloat16)
    send_x = send_x.reshape(expert_count, capacity, model_width)
    send_dy = send_dy.reshape(expert_count, capacity, model_width)
    recv_x, recv_dy = (
        lax.all_to_all(send_x, "expert", split_axis=0, concat_axis=0, tiled=True),
        lax.all_to_all(send_dy, "expert", split_axis=0, concat_axis=0, tiled=True),
    )

    def to_local(stacked):
        shaped = stacked.reshape(group_count, local_count, capacity, model_width)
        return shaped.transpose(1, 0, 2, 3).reshape(local_count, slot_count, model_width)

    slot_x = to_local(recv_x)
    slot_dy = to_local(recv_dy)
    part_x = slot_x
    gate_term = jnp.einsum(
        "asd,adf->asf",
        part_x,
        lax.all_gather(w_gate, "dp", axis=1, tiled=True),
        preferred_element_type=jnp.float32,
    )
    up_term = jnp.einsum(
        "asd,adf->asf",
        part_x,
        lax.all_gather(w_up, "dp", axis=1, tiled=True),
        preferred_element_type=jnp.float32,
    )
    full_gate, full_up, full_down = (
        lax.all_gather(w_gate, "dp", axis=1, tiled=True),
        lax.all_gather(w_up, "dp", axis=1, tiled=True),
        lax.all_gather(w_down, "dp", axis=2, tiled=True),
    )
    sigma = jax.nn.sigmoid(gate_term)
    active = gate_term * sigma
    activated = (active * up_term).astype(jnp.bfloat16)
    back_hidden = jnp.einsum("asd,afd->asf", slot_dy, full_down, preferred_element_type=jnp.float32)
    up_delta = (back_hidden * active).astype(jnp.bfloat16)
    gate_delta = (back_hidden * up_term * sigma * (1.0 + gate_term * (1.0 - sigma))).astype(
        jnp.bfloat16
    )
    pair_grad = (
        jnp.einsum("asf,adf->asd", gate_delta, full_gate, preferred_element_type=jnp.float32)
        + jnp.einsum("asf,adf->asd", up_delta, full_up, preferred_element_type=jnp.float32)
    ).astype(jnp.bfloat16)
    send_back = pair_grad.reshape(local_count, group_count, capacity, model_width).transpose(
        1, 0, 2, 3
    )
    send_back = send_back.reshape(expert_count, capacity, model_width)
    returned = lax.all_to_all(send_back, "expert", split_axis=0, concat_axis=0, tiled=True)
    per_pair = returned.reshape(expert_count * capacity, model_width)[slot_of].astype(jnp.float32)
    input_grad = jnp.sum(per_pair.reshape(tok_rows, top_count, model_width), axis=1).astype(
        jnp.bfloat16
    )
    block_width = local_count * hidden_units
    share_width = model_width // lax.axis_size("dp")
    part_x = slot_x
    term_gate = jnp.einsum("asd,asf->daf", part_x, gate_delta, preferred_element_type=jnp.float32)
    term_up = jnp.einsum("asd,asf->daf", part_x, up_delta, preferred_element_type=jnp.float32)
    term_down = jnp.einsum("asd,asf->daf", slot_dy, activated, preferred_element_type=jnp.float32)
    shares = lax.psum_scatter(
        jnp.concatenate(
            [
                term_gate.reshape(lax.axis_size("dp") * share_width, block_width),
                term_up.reshape(lax.axis_size("dp") * share_width, block_width),
                term_down.reshape(lax.axis_size("dp") * share_width, block_width),
            ],
            axis=1,
        ).astype(jnp.bfloat16),
        "dp",
        scatter_dimension=0,
        tiled=True,
    ).astype(jnp.float32)
    share_rows = shares.shape[0]

    def unpack(which):
        return shares[:, which * block_width : (which + 1) * block_width].reshape(
            share_rows, local_count, hidden_units
        )

    gate_grad = unpack(0).transpose(1, 0, 2).astype(jnp.bfloat16)
    up_grad = unpack(1).transpose(1, 0, 2).astype(jnp.bfloat16)
    down_grad = unpack(2).transpose(1, 2, 0).astype(jnp.bfloat16)
    return (input_grad, gate_grad, up_grad, down_grad)


def lined(dp, expert):
    return dp == 4 and expert == 8


def local(tokens, out_grad, routes, gate_values, w_gate, w_up, w_down):
    experts = lax.axis_size("expert") * w_gate.shape[0]
    capacity = slots_of(tokens.shape[0], routes.shape[1], experts)
    fits = w_gate.shape[0] == 1 and tokens.shape[0] <= 2 * capacity
    if not (fits and lined(lax.axis_size("dp"), lax.axis_size("expert"))):
        return routed(tokens, out_grad, routes, gate_values, w_gate, w_up, w_down)
    return dense(tokens, out_grad, routes, gate_values, w_gate, w_up, w_down)


def solution(mesh):
    return jax.shard_map(
        local,
        mesh=mesh,
        in_specs=(
            P(("dp", "expert"), None),
            P(("dp", "expert"), None),
            P(("dp", "expert"), None),
            P(("dp", "expert"), None),
            P("expert", "dp", None),
            P("expert", "dp", None),
            P("expert", None, "dp"),
        ),
        out_specs=(
            P(("dp", "expert"), None),
            P("expert", "dp", None),
            P("expert", "dp", None),
            P("expert", None, "dp"),
        ),
        check_vma=False,
    )
```

```python
import functools

import jax
import jax.numpy as jnp
from jax import lax
from jax.experimental import pallas as pl
from jax.experimental.pallas import tpu as pltpu
from jax.sharding import PartitionSpec as P


F32 = jnp.float32
BF16 = jnp.bfloat16
ANY = pl.BlockSpec(memory_space=pl.ANY)
VMEM = pl.BlockSpec(memory_space=pltpu.VMEM)
SMEM = pl.BlockSpec(memory_space=pltpu.SMEM)
LIMIT = 12 * 1024 * 1024
LANES = 128
NN = (((1,), (0,)), ((), ()))
NT = (((1,), (1,)), ((), ()))


def mm(a, b, dims):
    return lax.dot_general(a, b, dims, preferred_element_type=F32)


def slots_of(tok_rows, top_count, expert_count):
    return min(tok_rows, max(2, 9 * tok_rows * top_count // (8 * expert_count)))


def call(body, outs, ins, scratch, flops, moved, aliases=None):
    return pl.pallas_call(
        body,
        input_output_aliases=aliases or {},
        out_shape=[jax.ShapeDtypeStruct(s, d) for s, d, _ in outs],
        in_specs=[s for _, s in ins],
        out_specs=[s for _, _, s in outs],
        scratch_shapes=scratch,
        compiler_params=pltpu.CompilerParams(vmem_limit_bytes=LIMIT),
        cost_estimate=pl.CostEstimate(flops=flops, bytes_accessed=moved, transcendentals=0),
    )(*[a for a, _ in ins])


TWO = ((0, 2), (1, 3), (2, 0), (3, 1))
OUTER = ((0, 1), (1, 0), (2, 3), (3, 2))
INNER = ((1, 2), (2, 1))


def prep_body(experts, routes, gates, rows, out):
    tok, width = rows.shape
    line = lax.broadcasted_iota(jnp.int32, (LANES, tok), 0)
    term, named = line // experts, line % experts
    value = jnp.zeros((LANES, tok), F32)
    for k in range(routes.shape[0]):
        value += jnp.where(routes[k : k + 1, :] == named, gates[k : k + 1, :], 0.0)
    high = value.astype(BF16).astype(F32)
    mid = (value - high).astype(BF16).astype(F32)
    low = value - high - mid
    value = jnp.where(term == 0, high, jnp.where(term == 1, mid, jnp.where(term == 2, low, 0.0)))
    out[:, :width] = rows[...]
    out[:, width:] = jnp.transpose(value).astype(BF16)


class Copies:
    def __init__(self, sems):
        self.sems, self.used = sems, 0

    def start(self, src, dst):
        copy = pltpu.make_async_copy(src, dst, self.sems.at[self.used])
        self.used += 1
        copy.start()
        return copy

    def pick(self, first, src, other, dst):
        sem = self.sems.at[self.used]
        self.used += 1

        @pl.when(first)
        def _():
            pltpu.make_async_copy(src, dst, sem).start()

        @pl.when(jnp.logical_not(first))
        def _():
            pltpu.make_async_copy(other, dst, sem).start()

        return pltpu.make_async_copy(other, dst, sem)


def load_early(copies, pieces, dst, first=0):
    tok = pieces[0].shape[0]
    return [copies.start(src, dst.at[pl.ds((first + i) * tok, tok)]) for i, src in enumerate(pieces)]


def load_weights(copies, place, which, pieces, wg, wu):
    share = pieces[0].shape[0]
    started = []
    for i, k in enumerate(which):
        at = pl.ds((place[0] ^ k) * share, share)
        started += [copies.start(pieces[2 * i], wg.at[at]), copies.start(pieces[2 * i + 1], wu.at[at])]
    return started


def own_body(place, tokens, w_gate, w_up, x, wg, wu, sems):
    copies = Copies(sems)
    started = load_early(copies, (tokens,), x) + load_weights(copies, place, (0,), (w_gate, w_up), wg, wu)
    for c in started:
        c.wait()


def near_body(place, *refs):
    pieces, weights = refs[:5], refs[5:9]
    x, wg, wu, sems = refs[12:]
    copies = Copies(sems)
    for c in load_early(copies, pieces, x, 1) + load_weights(copies, place, (1, 2), weights, wg, wu):
        c.wait()


def load_late(copies, chip, pieces, dst):
    tok = pieces[0].shape[0]
    middle = jnp.logical_or(chip == 1, chip == 2)
    return [
        copies.pick(middle, pieces[2 * core], pieces[2 * core + 1], dst.at[pl.ds(core * tok, tok)]) for core in (0, 1)
    ]


def pre_blocks(x, first, count, wg, wu, act, active_out, slope_out):
    tn = 256

    def step(i, _):
        r = slice(first, first + count)
        c = pl.ds(pl.multiple_of(i * tn, tn), tn)
        lhs = x[r, :]
        gate = mm(lhs, wg[:, c], NN)
        up = mm(lhs, wu[:, c], NN)
        sigma = jax.nn.sigmoid(gate)
        active = gate * sigma
        act[r, c] = (active * up).astype(BF16)
        active_out[r, c] = active
        slope_out[r, c] = up * sigma * (1.0 + gate * (1.0 - sigma))
        return 0

    lax.fori_loop(0, wg.shape[1] // tn, step, 0)


def pre_early_body(place, *refs):
    act, active, slope, wg, wu, sems = refs[5:]
    for c in load_weights(Copies(sems), place, (3,), refs[:2], wg, wu):
        c.wait()
    x = refs[2]
    pre_blocks(x, 0, x.shape[0] // 4 * 3, wg, wu, act, active, slope)


def pre_late_body(place, *refs):
    pieces, wg, wu = refs[:4], refs[4], refs[5]
    act, active, slope, x, sems = refs[10:]
    count = x.shape[0] // 4
    for c in load_late(Copies(sems), place[1], pieces, x.at[pl.ds(3 * count, count)]):
        c.wait()
    pre_blocks(x, 3 * count, count, wg, wu, act, active, slope)


def scale(experts, expert, raw, y, first):
    tok, width = raw.shape[0] // 2, y.shape[1]
    lane = lax.broadcasted_iota(jnp.int32, (tok, LANES), 1)
    mine = jnp.logical_and(lane % experts == expert, lane < 3 * experts)
    for i in (0, 1):
        gate = jnp.sum(jnp.where(mine, raw[i * tok : (i + 1) * tok, width:].astype(F32), 0.0), axis=1, keepdims=True)
        y[first + i * tok : first + (i + 1) * tok, :] = (raw[i * tok : (i + 1) * tok, :width].astype(F32) * gate).astype(
            BF16
        )


def scale_early_body(experts, place, *refs):
    pieces = refs[:6]
    y, raw, sems = refs[6:]
    tok = pieces[0].shape[0]
    started = load_early(Copies(sems), pieces, raw)
    for i in range(3):
        started[2 * i].wait()
        started[2 * i + 1].wait()
        scale(experts, place[2], raw.at[pl.ds(2 * i * tok, 2 * tok)], y, 2 * i * tok)


def down_send_body(experts, place, *refs):
    pieces, act = refs[:4], refs[4]
    send_a, send_b, y, raw, sems = refs[6:]
    for c in load_late(Copies(sems), place[1], pieces, raw):
        c.wait()
    scale(experts, place[2], raw, y, y.shape[0] - raw.shape[0])
    down_blocks(place, act, y, ((0, 1, send_a, 0), (0, 3, send_a, 1), (1, 2, send_b, 0), (1, 3, send_b, 1)))


def down_blocks(place, act, y, wanted):
    share = y.shape[1] // 4
    half = act.shape[1] // 2
    for h in (0, 1):
        turned = jnp.transpose(act[:, h * half : (h + 1) * half])
        for which, k, dst, slot in wanted:
            if which == h:
                cols = pl.ds(pl.multiple_of((place[0] ^ k) * share, share), share)
                value = mm(turned, y[:, cols], NN).astype(BF16)
                if slot is None:
                    dst[...] = value
                else:
                    dst[slot] = value


def down_keep_body(place, act, y, a0, a1, b0, b1):
    down_blocks(place, act, y, ((0, 0, a0, None), (0, 2, a1, None), (1, 0, b0, None), (1, 1, b1, None)))


def back_body(place, y, active, slope, *refs):
    own, halves = refs[0], refs[1:7]
    gate_delta, up_delta, w, sems = refs[7:]
    me = place[0]
    copies = Copies(sems)
    hidden, share = own.shape
    half = hidden // 2
    started = [copies.start(own, w.at[me])]
    for i, src in enumerate(halves):
        started.append(copies.start(src, w.at[me ^ (1 + i // 2), pl.ds(i % 2 * half, half)]))
    for c in started:
        c.wait()
    rows = y.shape[0]
    tm, tn = rows // 2, 256

    def step(i, _):
        r = pl.ds(pl.multiple_of(i // (hidden // tn) * tm, tm), tm)
        c = pl.ds(pl.multiple_of(i % (hidden // tn) * tn, tn), tn)
        back = mm(y[r, 0:share], w[0, c, :], NT)
        for j in range(1, 4):
            back += mm(y[r, j * share : (j + 1) * share], w[j, c, :], NT)
        up_delta[r, c] = (back * active[r, c]).astype(BF16)
        gate_delta[r, c] = (back * slope[r, c]).astype(BF16)
        return 0

    lax.fori_loop(0, 2 * (hidden // tn), step, 0)


def grad_blocks(place, x, wanted):
    share = x.shape[1] // 4
    tm = share // 2
    for k, targets in wanted:

        def step(i, _, k=k, targets=targets):
            cols = pl.ds(pl.multiple_of((place[0] ^ k) * share + i * tm, tm), tm)
            turned = jnp.transpose(x[:, cols])
            part = pl.ds(pl.multiple_of(i * tm, tm), tm)
            for delta, dst, slot in targets:
                value = mm(turned, delta[...], NN).astype(BF16)
                if slot is None:
                    dst[part, :] = value
                else:
                    dst[slot, part, :] = value
            return 0

        lax.fori_loop(0, 2, step, 0)


def grad_send_body(place, x, gd, ud, gate_send, up_send):
    grad_blocks(
        place, x, ((1, [(gd, gate_send, 0)]), (3, [(gd, gate_send, 1), (ud, up_send, 1)]), (2, [(ud, up_send, 0)]))
    )


def grad_keep_body(place, x, gd, ud, g0, g1, u0, u1):
    grad_blocks(place, x, ((2, [(gd, g1, None)]), (1, [(ud, u1, None)]), (0, [(gd, g0, None), (ud, u0, None)])))


def pair_body(gate_delta, up_delta, wg, wu, send, keep):
    tn = 256
    part = keep.shape[0] // 4

    def step(i, _):
        c = pl.ds(pl.multiple_of(i * tn, tn), tn)
        total = (mm(gate_delta[...], wg[c, :], NT) + mm(up_delta[...], wu[c, :], NT)).astype(BF16)
        keep[: 3 * part, c] = total[: 3 * part]
        send[: 3 * part, c] = total[3 * part : 6 * part]
        keep[3 * part :, c] = total[6 * part : 7 * part]
        send[3 * part :, c] = total[7 * part :]
        return 0

    lax.fori_loop(0, wg.shape[0] // tn, step, 0)


def add(*terms):
    total = terms[0].astype(F32)
    for term in terms[1:]:
        total = total + term.astype(F32)
    return total.astype(BF16)


def dense(tokens, out_grad, routes, gate_values, w_gate, w_up, w_down):
    tok, width = tokens.shape
    experts = lax.axis_size("expert")
    chips = experts // 2
    hidden = w_gate.shape[2]
    share = width // 4
    half = hidden // 2
    rows = experts * tok
    expert = lax.axis_index("expert")
    chip = expert // 2
    place = jnp.stack([lax.axis_index("dp"), chip, expert]).astype(jnp.int32)

    def to_x(block):
        return lax.ppermute(block, "dp", [(i, i ^ 1) for i in range(4)])

    def to_y(block):
        return lax.ppermute(block, "dp", [(i, i ^ 2) for i in range(4)])

    def hop(block, moves):
        return lax.ppermute(block, "expert", [(2 * a + c, 2 * b + c) for a, b in moves for c in (0, 1)])

    def swap(block, at=range(chips)):
        return lax.ppermute(block, "expert", [(2 * z + c, 2 * z + 1 - c) for z in at for c in (0, 1)])

    def line(own):
        two = hop(own, TWO)
        outer = hop(own, OUTER)
        inner = hop(own, INNER)
        far = hop(two, ((2, 3), (1, 0)))
        early = [own, two, outer, swap(own), swap(two), swap(outer)]
        late = [inner, far, swap(inner, (1, 2)), swap(far, (0, 3))]
        return early, late

    x_early, x_late = line(tokens)
    (y_own,) = call(
        functools.partial(prep_body, experts),
        [((tok, width + LANES), BF16, VMEM)],
        [(routes.T, VMEM), (gate_values.T, VMEM), (out_grad, VMEM)],
        [],
        1000,
        4 * tok * width,
    )
    y_early, y_late = line(y_own)

    wg0, wu0, wd0 = w_gate[0], w_up[0], w_down[0]
    wg1, wu2 = to_x(wg0), to_y(wu0)
    wg2, wu1 = to_y(wg0), to_x(wu0)
    wg3, wu3 = to_y(wg1), to_x(wu2)
    da0, db0 = wd0[:half], wd0[half:]
    da1, db2 = to_x(da0), to_y(db0)
    da2, db1 = to_y(da0), to_x(db0)
    da3, db3 = to_y(da1), to_x(db2)

    def dma(n):
        return pltpu.SemaphoreType.DMA((n,))

    def anys(arrays):
        return [(a, ANY) for a in arrays]

    x_out = ((rows, width), BF16, VMEM)
    weight = ((width, hidden), BF16, VMEM)
    flat = ((rows, hidden), BF16, VMEM)
    wide = ((rows, hidden), F32, VMEM)
    x, wg, wu = call(
        own_body,
        [x_out, weight, weight],
        [(place, SMEM)] + anys((tokens, wg0, wu0)),
        [dma(3)],
        1000,
        width * (2 * tok + hidden),
    )
    x, wg, wu = call(
        near_body,
        [x_out, weight, weight],
        [(place, SMEM)] + anys(x_early[1:]) + anys((wg1, wu1, wg2, wu2)) + [(x, VMEM), (wg, VMEM), (wu, VMEM)],
        [dma(9)],
        1000,
        width * (10 * tok + 2 * hidden),
        {10: 0, 11: 1, 12: 2},
    )
    *pre, wg, wu = call(
        pre_early_body,
        [flat, wide, wide, weight, weight],
        [(place, SMEM)] + anys((wg3, wu3)) + [(x, VMEM), (wg, VMEM), (wu, VMEM)],
        [dma(2)],
        3 * rows * width * hidden,
        3 * rows * width + 8 * width * hidden + 8 * rows * hidden,
        {4: 3, 5: 4},
    )
    act, active, slope, x = call(
        pre_late_body,
        [flat, wide, wide, x_out],
        [(place, SMEM)] + anys(x_late) + [(a, VMEM) for a in (wg, wu, *pre, x)],
        [dma(2)],
        rows * width * hidden,
        rows * width + 4 * width * hidden + 3 * rows * hidden,
        {7 + i: i for i in range(4)},
    )
    (y,) = call(
        functools.partial(scale_early_body, experts),
        [((rows, width), BF16, VMEM)],
        [(place, SMEM)] + anys(y_early),
        [pltpu.VMEM((6 * tok, width + LANES), BF16), dma(6)],
        rows * width,
        4 * rows * width,
    )
    piece = (2, half, share)
    send_a, send_b, y = call(
        functools.partial(down_send_body, experts),
        [(piece, BF16, VMEM)] * 2 + [((rows, width), BF16, VMEM)],
        [(place, SMEM)] + anys(y_late) + [(act, VMEM), (y, VMEM)],
        [pltpu.VMEM((2 * tok, width + LANES), BF16), dma(2)],
        rows * width * hidden,
        2 * (2 * rows * width + rows * hidden + width * hidden // 2),
        {6: 2},
    )
    got_a, got_b = to_x(send_a), to_y(send_b)
    gate_delta, up_delta = call(
        back_body,
        [((rows, hidden), BF16, VMEM)] * 2,
        [(place, SMEM), (y, VMEM), (active, VMEM), (slope, VMEM)] + anys((wd0, da1, db1, da2, db2, da3, db3)),
        [pltpu.VMEM((4, hidden, share), BF16), dma(7)],
        2 * rows * width * hidden,
        2 * (rows * width + width * hidden) + 12 * rows * hidden,
    )
    gate_send, up_send = call(
        grad_send_body,
        [((2, share, hidden), BF16, VMEM)] * 2,
        [(place, SMEM), (x, VMEM), (gate_delta, VMEM), (up_delta, VMEM)],
        [],
        2 * rows * width * hidden,
        2 * (rows * width + 2 * rows * hidden + width * hidden),
    )
    gate_got, up_got = to_x(gate_send), to_y(up_send)
    pair_send, pair_keep = call(
        pair_body,
        [((rows // 2, width), BF16, VMEM)] * 2,
        [(gate_delta, VMEM), (up_delta, VMEM), (wg, VMEM), (wu, VMEM)],
        [],
        4 * rows * width * hidden,
        2 * (rows * width + 2 * rows * hidden + 2 * width * hidden),
    )
    total = add(pair_keep, swap(pair_send)).reshape(chips, tok, width)
    keep_a0, keep_a1, keep_b0, keep_b1 = call(
        down_keep_body,
        [((half, share), BF16, VMEM)] * 4,
        [(place, SMEM), (act, VMEM), (y, VMEM)],
        [],
        rows * width * hidden,
        2 * (rows * width + rows * hidden + width * hidden // 2),
    )
    gate0, gate1, up0, up1 = call(
        grad_keep_body,
        [((share, hidden), BF16, VMEM)] * 4,
        [(place, SMEM), (x, VMEM), (gate_delta, VMEM), (up_delta, VMEM)],
        [],
        2 * rows * width * hidden,
        2 * (rows * width + 2 * rows * hidden + width * hidden),
    )
    down_a, down_b = to_y(add(keep_a1, got_a[1])), to_x(add(keep_b1, got_b[1]))
    gate1, up1 = add(gate1, gate_got[1]), add(up1, up_got[1])
    sums = add(gate0, gate_got[0]), add(up0, up_got[0])
    gate_last, up_last = to_y(gate1), to_x(up1)
    gate_sum, up_sum = lax.optimization_barrier(sums)
    down_grad = jnp.concatenate([add(keep_a0, got_a[0], down_a), add(keep_b0, got_b[0], down_b)], axis=0)
    gate_grad, up_grad = add(gate_sum, gate_last), add(up_sum, up_last)

    far = hop(total[3], ((0, 1), (3, 2)))
    inner = hop(total[3], INNER)
    outer = hop(total[2], OUTER)
    two = hop(add(total[1], far), TWO)
    input_grad = add(total[0], inner, outer, two)
    return input_grad, gate_grad[None], up_grad[None], down_grad[None]


def routed(tokens, out_grad, routes, gate_values, w_gate, w_up, w_down):
    tok_rows, model_width = tokens.shape
    top_count = routes.shape[1]
    group_count = lax.axis_size("expert")
    local_count = w_gate.shape[0]
    expert_count = group_count * local_count
    hidden_units = w_gate.shape[2]
    capacity = slots_of(tok_rows, top_count, expert_count)
    pair_count = tok_rows * top_count
    slot_count = group_count * capacity
    expert_of = routes.reshape(-1)
    onehot = (expert_of[:, None] == jnp.arange(expert_count, dtype=jnp.int32)[None, :]).astype(
        jnp.int32
    )
    before = jnp.cumsum(onehot, axis=0) - onehot
    placed = jnp.sum(before * onehot, axis=1)
    slot_of = expert_of * capacity + placed
    slot_table = jnp.full((expert_count * capacity,), pair_count, jnp.int32)
    slot_table = slot_table.at[slot_of].set(jnp.arange(pair_count, dtype=jnp.int32))
    filled = slot_table < pair_count
    source = jnp.where(filled, slot_table, 0)
    owner_row = source // top_count
    send_x = jnp.where(filled[:, None], tokens[owner_row], jnp.zeros((), jnp.bfloat16))
    scaled = gate_values.reshape(-1)[source][:, None] * out_grad[owner_row].astype(jnp.float32)
    send_dy = jnp.where(filled[:, None], scaled, 0.0).astype(jnp.bfloat16)
    send_x = send_x.reshape(expert_count, capacity, model_width)
    send_dy = send_dy.reshape(expert_count, capacity, model_width)
    recv_x, recv_dy = (
        lax.all_to_all(send_x, "expert", split_axis=0, concat_axis=0, tiled=True),
        lax.all_to_all(send_dy, "expert", split_axis=0, concat_axis=0, tiled=True),
    )

    def to_local(stacked):
        shaped = stacked.reshape(group_count, local_count, capacity, model_width)
        return shaped.transpose(1, 0, 2, 3).reshape(local_count, slot_count, model_width)

    slot_x = to_local(recv_x)
    slot_dy = to_local(recv_dy)
    part_x = slot_x
    gate_term = jnp.einsum(
        "asd,adf->asf",
        part_x,
        lax.all_gather(w_gate, "dp", axis=1, tiled=True),
        preferred_element_type=jnp.float32,
    )
    up_term = jnp.einsum(
        "asd,adf->asf",
        part_x,
        lax.all_gather(w_up, "dp", axis=1, tiled=True),
        preferred_element_type=jnp.float32,
    )
    full_gate, full_up, full_down = (
        lax.all_gather(w_gate, "dp", axis=1, tiled=True),
        lax.all_gather(w_up, "dp", axis=1, tiled=True),
        lax.all_gather(w_down, "dp", axis=2, tiled=True),
    )
    sigma = jax.nn.sigmoid(gate_term)
    active = gate_term * sigma
    activated = (active * up_term).astype(jnp.bfloat16)
    back_hidden = jnp.einsum("asd,afd->asf", slot_dy, full_down, preferred_element_type=jnp.float32)
    up_delta = (back_hidden * active).astype(jnp.bfloat16)
    gate_delta = (back_hidden * up_term * sigma * (1.0 + gate_term * (1.0 - sigma))).astype(
        jnp.bfloat16
    )
    pair_grad = (
        jnp.einsum("asf,adf->asd", gate_delta, full_gate, preferred_element_type=jnp.float32)
        + jnp.einsum("asf,adf->asd", up_delta, full_up, preferred_element_type=jnp.float32)
    ).astype(jnp.bfloat16)
    send_back = pair_grad.reshape(local_count, group_count, capacity, model_width).transpose(
        1, 0, 2, 3
    )
    send_back = send_back.reshape(expert_count, capacity, model_width)
    returned = lax.all_to_all(send_back, "expert", split_axis=0, concat_axis=0, tiled=True)
    per_pair = returned.reshape(expert_count * capacity, model_width)[slot_of].astype(jnp.float32)
    input_grad = jnp.sum(per_pair.reshape(tok_rows, top_count, model_width), axis=1).astype(
        jnp.bfloat16
    )
    block_width = local_count * hidden_units
    share_width = model_width // lax.axis_size("dp")
    part_x = slot_x
    term_gate = jnp.einsum("asd,asf->daf", part_x, gate_delta, preferred_element_type=jnp.float32)
    term_up = jnp.einsum("asd,asf->daf", part_x, up_delta, preferred_element_type=jnp.float32)
    term_down = jnp.einsum("asd,asf->daf", slot_dy, activated, preferred_element_type=jnp.float32)
    shares = lax.psum_scatter(
        jnp.concatenate(
            [
                term_gate.reshape(lax.axis_size("dp") * share_width, block_width),
                term_up.reshape(lax.axis_size("dp") * share_width, block_width),
                term_down.reshape(lax.axis_size("dp") * share_width, block_width),
            ],
            axis=1,
        ).astype(jnp.bfloat16),
        "dp",
        scatter_dimension=0,
        tiled=True,
    ).astype(jnp.float32)
    share_rows = shares.shape[0]

    def unpack(which):
        return shares[:, which * block_width : (which + 1) * block_width].reshape(
            share_rows, local_count, hidden_units
        )

    gate_grad = unpack(0).transpose(1, 0, 2).astype(jnp.bfloat16)
    up_grad = unpack(1).transpose(1, 0, 2).astype(jnp.bfloat16)
    down_grad = unpack(2).transpose(1, 2, 0).astype(jnp.bfloat16)
    return (input_grad, gate_grad, up_grad, down_grad)


def lined(dp, expert):
    return dp == 4 and expert == 8


def local(tokens, out_grad, routes, gate_values, w_gate, w_up, w_down):
    experts = lax.axis_size("expert") * w_gate.shape[0]
    capacity = slots_of(tokens.shape[0], routes.shape[1], experts)
    fits = w_gate.shape[0] == 1 and tokens.shape[0] <= 2 * capacity
    if not (fits and lined(lax.axis_size("dp"), lax.axis_size("expert"))):
        return routed(tokens, out_grad, routes, gate_values, w_gate, w_up, w_down)
    return dense(tokens, out_grad, routes, gate_values, w_gate, w_up, w_down)


def solution(mesh):
    return jax.shard_map(
        local,
        mesh=mesh,
        in_specs=(
            P(("dp", "expert"), None),
            P(("dp", "expert"), None),
            P(("dp", "expert"), None),
            P(("dp", "expert"), None),
            P("expert", "dp", None),
            P("expert", "dp", None),
            P("expert", None, "dp"),
        ),
        out_specs=(
            P(("dp", "expert"), None),
            P("expert", "dp", None),
            P("expert", "dp", None),
            P("expert", None, "dp"),
        ),
        check_vma=False,
    )
```

```python
import functools

import jax
import jax.numpy as jnp
from jax import lax
from jax.experimental import pallas as pl
from jax.experimental.pallas import tpu as pltpu
from jax.sharding import PartitionSpec as P


F32 = jnp.float32
BF16 = jnp.bfloat16
ANY = pl.BlockSpec(memory_space=pl.ANY)
VMEM = pl.BlockSpec(memory_space=pltpu.VMEM)
SMEM = pl.BlockSpec(memory_space=pltpu.SMEM)
LIMIT = 12 * 1024 * 1024
LANES = 128
NN = (((1,), (0,)), ((), ()))
NT = (((1,), (1,)), ((), ()))


def mm(a, b, dims):
    return lax.dot_general(a, b, dims, preferred_element_type=F32)


def slots_of(tok_rows, top_count, expert_count):
    return min(tok_rows, max(2, 9 * tok_rows * top_count // (8 * expert_count)))


def call(body, outs, ins, scratch, flops, moved, aliases=None):
    return pl.pallas_call(
        body,
        input_output_aliases=aliases or {},
        out_shape=[jax.ShapeDtypeStruct(s, d) for s, d, _ in outs],
        in_specs=[s for _, s in ins],
        out_specs=[s for _, _, s in outs],
        scratch_shapes=scratch,
        compiler_params=pltpu.CompilerParams(vmem_limit_bytes=LIMIT),
        cost_estimate=pl.CostEstimate(flops=flops, bytes_accessed=moved, transcendentals=0),
    )(*[a for a, _ in ins])


TWO = ((0, 2), (1, 3), (2, 0), (3, 1))
OUTER = ((0, 1), (1, 0), (2, 3), (3, 2))
INNER = ((1, 2), (2, 1))


def prep_body(experts, routes, gates, rows, out):
    tok, width = rows.shape
    line = lax.broadcasted_iota(jnp.int32, (LANES, tok), 0)
    term, named = line // experts, line % experts
    value = jnp.zeros((LANES, tok), F32)
    for k in range(routes.shape[0]):
        value += jnp.where(routes[k : k + 1, :] == named, gates[k : k + 1, :], 0.0)
    high = value.astype(BF16).astype(F32)
    mid = (value - high).astype(BF16).astype(F32)
    low = value - high - mid
    value = jnp.where(term == 0, high, jnp.where(term == 1, mid, jnp.where(term == 2, low, 0.0)))
    out[:, :width] = rows[...]
    out[:, width:] = jnp.transpose(value).astype(BF16)


class Copies:
    def __init__(self, sems):
        self.sems, self.used = sems, 0

    def start(self, src, dst):
        copy = pltpu.make_async_copy(src, dst, self.sems.at[self.used])
        self.used += 1
        copy.start()
        return copy

    def pick(self, first, src, other, dst):
        sem = self.sems.at[self.used]
        self.used += 1

        @pl.when(first)
        def _():
            pltpu.make_async_copy(src, dst, sem).start()

        @pl.when(jnp.logical_not(first))
        def _():
            pltpu.make_async_copy(other, dst, sem).start()

        return pltpu.make_async_copy(other, dst, sem)


def load_early(copies, pieces, dst, first=0):
    tok = pieces[0].shape[0]
    return [copies.start(src, dst.at[pl.ds((first + i) * tok, tok)]) for i, src in enumerate(pieces)]


def load_weights(copies, place, which, pieces, wg, wu):
    share = pieces[0].shape[0]
    started = []
    for i, k in enumerate(which):
        at = pl.ds((place[0] ^ k) * share, share)
        started += [copies.start(pieces[2 * i], wg.at[at]), copies.start(pieces[2 * i + 1], wu.at[at])]
    return started


def own_body(place, tokens, w_gate, w_up, x, wg, wu, sems):
    copies = Copies(sems)
    started = load_early(copies, (tokens,), x) + load_weights(copies, place, (0,), (w_gate, w_up), wg, wu)
    for c in started:
        c.wait()


def near_body(place, *refs):
    pieces, weights = refs[:5], refs[5:9]
    x, wg, wu, sems = refs[12:]
    copies = Copies(sems)
    for c in load_early(copies, pieces, x, 1) + load_weights(copies, place, (1, 2), weights, wg, wu):
        c.wait()


def load_late(copies, chip, pieces, dst):
    tok = pieces[0].shape[0]
    middle = jnp.logical_or(chip == 1, chip == 2)
    return [
        copies.pick(middle, pieces[2 * core], pieces[2 * core + 1], dst.at[pl.ds(core * tok, tok)]) for core in (0, 1)
    ]


def pre_blocks(x, first, count, wg, wu, act, active_out, slope_out):
    tn = 256

    def step(i, _):
        r = slice(first, first + count)
        c = pl.ds(pl.multiple_of(i * tn, tn), tn)
        lhs = x[r, :]
        gate = mm(lhs, wg[:, c], NN)
        up = mm(lhs, wu[:, c], NN)
        sigma = jax.nn.sigmoid(gate)
        active = gate * sigma
        act[r, c] = (active * up).astype(BF16)
        active_out[r, c] = active
        slope_out[r, c] = up * sigma * (1.0 + gate * (1.0 - sigma))
        return 0

    lax.fori_loop(0, wg.shape[1] // tn, step, 0)


def pre_early_body(place, *refs):
    act, active, slope, wg, wu, sems = refs[5:]
    for c in load_weights(Copies(sems), place, (3,), refs[:2], wg, wu):
        c.wait()
    x = refs[2]
    pre_blocks(x, 0, x.shape[0] // 4 * 3, wg, wu, act, active, slope)


def pre_late_body(place, *refs):
    pieces, wg, wu = refs[:4], refs[4], refs[5]
    act, active, slope, x, sems = refs[10:]
    count = x.shape[0] // 4
    for c in load_late(Copies(sems), place[1], pieces, x.at[pl.ds(3 * count, count)]):
        c.wait()
    pre_blocks(x, 3 * count, count, wg, wu, act, active, slope)


def scale(experts, expert, raw, y, first):
    tok, width = raw.shape[0] // 2, y.shape[1]
    lane = lax.broadcasted_iota(jnp.int32, (tok, LANES), 1)
    mine = jnp.logical_and(lane % experts == expert, lane < 3 * experts)
    for i in (0, 1):
        gate = jnp.sum(jnp.where(mine, raw[i * tok : (i + 1) * tok, width:].astype(F32), 0.0), axis=1, keepdims=True)
        y[first + i * tok : first + (i + 1) * tok, :] = (raw[i * tok : (i + 1) * tok, :width].astype(F32) * gate).astype(
            BF16
        )


def scale_early_body(experts, place, *refs):
    pieces = refs[:6]
    y, raw, sems = refs[6:]
    tok = pieces[0].shape[0]
    started = load_early(Copies(sems), pieces, raw)
    for i in range(3):
        started[2 * i].wait()
        started[2 * i + 1].wait()
        scale(experts, place[2], raw.at[pl.ds(2 * i * tok, 2 * tok)], y, 2 * i * tok)


def down_blocks(place, act, y, first, count, wanted, put):
    share = y.shape[1] // 4
    half = act.shape[1] // 2
    rows = slice(first, first + count)
    for h in (0, 1):
        turned = jnp.transpose(act[rows, h * half : (h + 1) * half])
        for which, k, target in wanted:
            if which == h:
                cols = pl.ds(pl.multiple_of((place[0] ^ k) * share, share), share)
                put(target, mm(turned, y[rows, cols], NN))


def down_early_body(place, act, y, part):
    def put(target, value):
        part[target] = value

    early = y.shape[0] // 4 * 3
    down_blocks(place, act, y, 0, early, ((0, 1, 0), (0, 3, 1), (1, 2, 2), (1, 3, 3)), put)


def down_send_body(experts, place, *refs):
    pieces, act, part = refs[:4], refs[4], refs[5]
    send_a, send_b, y, raw, sems = refs[7:]
    for c in load_late(Copies(sems), place[1], pieces, raw):
        c.wait()
    count = raw.shape[0]
    first = y.shape[0] - count
    scale(experts, place[2], raw, y, first)

    def put(target, value):
        dst = (send_a, send_b)[target // 2]
        dst[target % 2] = (part[target] + value).astype(BF16)

    down_blocks(place, act, y, first, count, ((0, 1, 0), (0, 3, 1), (1, 2, 2), (1, 3, 3)), put)


def down_keep_body(place, act, y, a0, a1, b0, b1):
    def put(target, value):
        target[...] = value.astype(BF16)

    down_blocks(place, act, y, 0, y.shape[0], ((0, 0, a0), (0, 2, a1), (1, 0, b0), (1, 1, b1)), put)


def last_body(gate_sum, gate_last, up_sum, up_last, gate_out, up_out, gate, up, sems):
    copies = Copies(sems)
    part = gate.shape[1] // 2
    started = []
    for total, last, held, out in ((gate_sum, gate_last, gate, gate_out), (up_sum, up_last, up, up_out)):
        for i in (0, 1):
            r = slice(i * part, (i + 1) * part)
            held[0, r, :] = (total[r, :].astype(F32) + last[r, :].astype(F32)).astype(BF16)
            at = pl.ds(i * part, part)
            started.append(copies.start(held.at[0, at], out.at[0, at]))
    for c in started:
        c.wait()


def back_body(place, y, active, slope, *refs):
    own, halves = refs[0], refs[1:7]
    gate_delta, up_delta, w, sems = refs[7:]
    me = place[0]
    copies = Copies(sems)
    hidden, share = own.shape
    half = hidden // 2
    started = [copies.start(own, w.at[me])]
    for i, src in enumerate(halves):
        started.append(copies.start(src, w.at[me ^ (1 + i // 2), pl.ds(i % 2 * half, half)]))
    for c in started:
        c.wait()
    rows = y.shape[0]
    tm, tn = rows // 2, 256

    def step(i, _):
        r = pl.ds(pl.multiple_of(i // (hidden // tn) * tm, tm), tm)
        c = pl.ds(pl.multiple_of(i % (hidden // tn) * tn, tn), tn)
        back = mm(y[r, 0:share], w[0, c, :], NT)
        for j in range(1, 4):
            back += mm(y[r, j * share : (j + 1) * share], w[j, c, :], NT)
        up_delta[r, c] = (back * active[r, c]).astype(BF16)
        gate_delta[r, c] = (back * slope[r, c]).astype(BF16)
        return 0

    lax.fori_loop(0, 2 * (hidden // tn), step, 0)


def grad_blocks(place, x, wanted):
    share = x.shape[1] // 4
    tm = share // 2
    for k, targets in wanted:

        def step(i, _, k=k, targets=targets):
            cols = pl.ds(pl.multiple_of((place[0] ^ k) * share + i * tm, tm), tm)
            turned = jnp.transpose(x[:, cols])
            part = pl.ds(pl.multiple_of(i * tm, tm), tm)
            for delta, dst, slot in targets:
                value = mm(turned, delta[...], NN).astype(BF16)
                if slot is None:
                    dst[part, :] = value
                else:
                    dst[slot, part, :] = value
            return 0

        lax.fori_loop(0, 2, step, 0)


def grad_send_body(place, x, gd, ud, gate_send, up_send):
    grad_blocks(
        place, x, ((1, [(gd, gate_send, 0)]), (3, [(gd, gate_send, 1), (ud, up_send, 1)]), (2, [(ud, up_send, 0)]))
    )


def grad_keep_body(place, x, gd, ud, g0, g1, u0, u1):
    grad_blocks(place, x, ((2, [(gd, g1, None)]), (1, [(ud, u1, None)]), (0, [(gd, g0, None), (ud, u0, None)])))


def pair_body(gate_delta, up_delta, wg, wu, send, keep):
    tn = 256
    part = keep.shape[0] // 4

    def step(i, _):
        c = pl.ds(pl.multiple_of(i * tn, tn), tn)
        total = (mm(gate_delta[...], wg[c, :], NT) + mm(up_delta[...], wu[c, :], NT)).astype(BF16)
        keep[: 3 * part, c] = total[: 3 * part]
        send[: 3 * part, c] = total[3 * part : 6 * part]
        keep[3 * part :, c] = total[6 * part : 7 * part]
        send[3 * part :, c] = total[7 * part :]
        return 0

    lax.fori_loop(0, wg.shape[0] // tn, step, 0)


def add(*terms):
    total = terms[0].astype(F32)
    for term in terms[1:]:
        total = total + term.astype(F32)
    return total.astype(BF16)


def dense(tokens, out_grad, routes, gate_values, w_gate, w_up, w_down):
    tok, width = tokens.shape
    experts = lax.axis_size("expert")
    chips = experts // 2
    hidden = w_gate.shape[2]
    share = width // 4
    half = hidden // 2
    rows = experts * tok
    expert = lax.axis_index("expert")
    chip = expert // 2
    place = jnp.stack([lax.axis_index("dp"), chip, expert]).astype(jnp.int32)

    def to_x(block):
        return lax.ppermute(block, "dp", [(i, i ^ 1) for i in range(4)])

    def to_y(block):
        return lax.ppermute(block, "dp", [(i, i ^ 2) for i in range(4)])

    def hop(block, moves):
        return lax.ppermute(block, "expert", [(2 * a + c, 2 * b + c) for a, b in moves for c in (0, 1)])

    def swap(block, at=range(chips)):
        return lax.ppermute(block, "expert", [(2 * z + c, 2 * z + 1 - c) for z in at for c in (0, 1)])

    def line(own):
        two = hop(own, TWO)
        outer = hop(own, OUTER)
        inner = hop(own, INNER)
        far = hop(two, ((2, 3), (1, 0)))
        early = [own, two, outer, swap(own), swap(two), swap(outer)]
        late = [inner, far, swap(inner, (1, 2)), swap(far, (0, 3))]
        return early, late

    x_early, x_late = line(tokens)
    (y_own,) = call(
        functools.partial(prep_body, experts),
        [((tok, width + LANES), BF16, VMEM)],
        [(routes.T, VMEM), (gate_values.T, VMEM), (out_grad, VMEM)],
        [],
        1000,
        4 * tok * width,
    )
    y_early, y_late = line(y_own)

    wg0, wu0, wd0 = w_gate[0], w_up[0], w_down[0]
    wg1, wu2 = to_x(wg0), to_y(wu0)
    wg2, wu1 = to_y(wg0), to_x(wu0)
    wg3, wu3 = to_y(wg1), to_x(wu2)
    da0, db0 = wd0[:half], wd0[half:]
    da1, db2 = to_x(da0), to_y(db0)
    da2, db1 = to_y(da0), to_x(db0)
    da3, db3 = to_y(da1), to_x(db2)

    def dma(n):
        return pltpu.SemaphoreType.DMA((n,))

    def anys(arrays):
        return [(a, ANY) for a in arrays]

    x_out = ((rows, width), BF16, VMEM)
    weight = ((width, hidden), BF16, VMEM)
    flat = ((rows, hidden), BF16, VMEM)
    wide = ((rows, hidden), F32, VMEM)
    x, wg, wu = call(
        own_body,
        [x_out, weight, weight],
        [(place, SMEM)] + anys((tokens, wg0, wu0)),
        [dma(3)],
        1000,
        width * (2 * tok + hidden),
    )
    x, wg, wu = call(
        near_body,
        [x_out, weight, weight],
        [(place, SMEM)] + anys(x_early[1:]) + anys((wg1, wu1, wg2, wu2)) + [(x, VMEM), (wg, VMEM), (wu, VMEM)],
        [dma(9)],
        1000,
        width * (10 * tok + 2 * hidden),
        {10: 0, 11: 1, 12: 2},
    )
    *pre, wg, wu = call(
        pre_early_body,
        [flat, wide, wide, weight, weight],
        [(place, SMEM)] + anys((wg3, wu3)) + [(x, VMEM), (wg, VMEM), (wu, VMEM)],
        [dma(2)],
        3 * rows * width * hidden,
        3 * rows * width + 8 * width * hidden + 8 * rows * hidden,
        {4: 3, 5: 4},
    )
    act, active, slope, x = call(
        pre_late_body,
        [flat, wide, wide, x_out],
        [(place, SMEM)] + anys(x_late) + [(a, VMEM) for a in (wg, wu, *pre, x)],
        [dma(2)],
        rows * width * hidden,
        rows * width + 4 * width * hidden + 3 * rows * hidden,
        {7 + i: i for i in range(4)},
    )
    (y,) = call(
        functools.partial(scale_early_body, experts),
        [((rows, width), BF16, VMEM)],
        [(place, SMEM)] + anys(y_early),
        [pltpu.VMEM((6 * tok, width + LANES), BF16), dma(6)],
        rows * width,
        4 * rows * width,
    )
    piece = (2, half, share)
    (part,) = call(
        down_early_body,
        [((4, half, share), F32, VMEM)],
        [(place, SMEM), (act, VMEM), (y, VMEM)],
        [],
        3 * rows * width * hidden // 4,
        2 * (rows * width + rows * hidden + width * hidden),
    )
    send_a, send_b, y = call(
        functools.partial(down_send_body, experts),
        [(piece, BF16, VMEM)] * 2 + [((rows, width), BF16, VMEM)],
        [(place, SMEM)] + anys(y_late) + [(act, VMEM), (part, VMEM), (y, VMEM)],
        [pltpu.VMEM((2 * tok, width + LANES), BF16), dma(2)],
        rows * width * hidden // 4,
        2 * (rows * width + rows * hidden // 4 + width * hidden),
        {7: 2},
    )
    got_a, got_b = to_x(send_a), to_y(send_b)
    gate_delta, up_delta = call(
        back_body,
        [((rows, hidden), BF16, VMEM)] * 2,
        [(place, SMEM), (y, VMEM), (active, VMEM), (slope, VMEM)] + anys((wd0, da1, db1, da2, db2, da3, db3)),
        [pltpu.VMEM((4, hidden, share), BF16), dma(7)],
        2 * rows * width * hidden,
        2 * (rows * width + width * hidden) + 12 * rows * hidden,
    )
    gate_send, up_send = call(
        grad_send_body,
        [((2, share, hidden), BF16, VMEM)] * 2,
        [(place, SMEM), (x, VMEM), (gate_delta, VMEM), (up_delta, VMEM)],
        [],
        2 * rows * width * hidden,
        2 * (rows * width + 2 * rows * hidden + width * hidden),
    )
    gate_got, up_got = to_x(gate_send), to_y(up_send)
    pair_send, pair_keep = call(
        pair_body,
        [((rows // 2, width), BF16, VMEM)] * 2,
        [(gate_delta, VMEM), (up_delta, VMEM), (wg, VMEM), (wu, VMEM)],
        [],
        4 * rows * width * hidden,
        2 * (rows * width + 2 * rows * hidden + 2 * width * hidden),
    )
    total = add(pair_keep, swap(pair_send)).reshape(chips, tok, width)
    keep_a0, keep_a1, keep_b0, keep_b1 = call(
        down_keep_body,
        [((half, share), BF16, VMEM)] * 4,
        [(place, SMEM), (act, VMEM), (y, VMEM)],
        [],
        rows * width * hidden,
        2 * (rows * width + rows * hidden + width * hidden // 2),
    )
    gate0, gate1, up0, up1 = call(
        grad_keep_body,
        [((share, hidden), BF16, VMEM)] * 4,
        [(place, SMEM), (x, VMEM), (gate_delta, VMEM), (up_delta, VMEM)],
        [],
        2 * rows * width * hidden,
        2 * (rows * width + 2 * rows * hidden + width * hidden),
    )
    down_a, down_b = to_y(add(keep_a1, got_a[1])), to_x(add(keep_b1, got_b[1]))
    gate1, up1 = add(gate1, gate_got[1]), add(up1, up_got[1])
    sums = add(gate0, gate_got[0]), add(up0, up_got[0])
    gate_last, up_last = to_y(gate1), to_x(up1)
    gate_sum, up_sum = lax.optimization_barrier(sums)
    down_grad = jnp.concatenate([add(keep_a0, got_a[0], down_a), add(keep_b0, got_b[0], down_b)], axis=0)
    result = (1, share, hidden)
    gate_grad, up_grad = call(
        last_body,
        [(result, BF16, ANY)] * 2,
        [(a, VMEM) for a in (gate_sum, gate_last, up_sum, up_last)],
        [pltpu.VMEM(result, BF16)] * 2 + [dma(4)],
        share * hidden,
        12 * share * hidden,
    )

    far = hop(total[3], ((0, 1), (3, 2)))
    inner = hop(total[3], INNER)
    outer = hop(total[2], OUTER)
    two = hop(add(total[1], far), TWO)
    input_grad = add(total[0], inner, outer, two)
    return input_grad, gate_grad, up_grad, down_grad[None]


def routed(tokens, out_grad, routes, gate_values, w_gate, w_up, w_down):
    tok_rows, model_width = tokens.shape
    top_count = routes.shape[1]
    group_count = lax.axis_size("expert")
    local_count = w_gate.shape[0]
    expert_count = group_count * local_count
    hidden_units = w_gate.shape[2]
    capacity = slots_of(tok_rows, top_count, expert_count)
    pair_count = tok_rows * top_count
    slot_count = group_count * capacity
    expert_of = routes.reshape(-1)
    onehot = (expert_of[:, None] == jnp.arange(expert_count, dtype=jnp.int32)[None, :]).astype(
        jnp.int32
    )
    before = jnp.cumsum(onehot, axis=0) - onehot
    placed = jnp.sum(before * onehot, axis=1)
    slot_of = expert_of * capacity + placed
    slot_table = jnp.full((expert_count * capacity,), pair_count, jnp.int32)
    slot_table = slot_table.at[slot_of].set(jnp.arange(pair_count, dtype=jnp.int32))
    filled = slot_table < pair_count
    source = jnp.where(filled, slot_table, 0)
    owner_row = source // top_count
    send_x = jnp.where(filled[:, None], tokens[owner_row], jnp.zeros((), jnp.bfloat16))
    scaled = gate_values.reshape(-1)[source][:, None] * out_grad[owner_row].astype(jnp.float32)
    send_dy = jnp.where(filled[:, None], scaled, 0.0).astype(jnp.bfloat16)
    send_x = send_x.reshape(expert_count, capacity, model_width)
    send_dy = send_dy.reshape(expert_count, capacity, model_width)
    recv_x, recv_dy = (
        lax.all_to_all(send_x, "expert", split_axis=0, concat_axis=0, tiled=True),
        lax.all_to_all(send_dy, "expert", split_axis=0, concat_axis=0, tiled=True),
    )

    def to_local(stacked):
        shaped = stacked.reshape(group_count, local_count, capacity, model_width)
        return shaped.transpose(1, 0, 2, 3).reshape(local_count, slot_count, model_width)

    slot_x = to_local(recv_x)
    slot_dy = to_local(recv_dy)
    part_x = slot_x
    gate_term = jnp.einsum(
        "asd,adf->asf",
        part_x,
        lax.all_gather(w_gate, "dp", axis=1, tiled=True),
        preferred_element_type=jnp.float32,
    )
    up_term = jnp.einsum(
        "asd,adf->asf",
        part_x,
        lax.all_gather(w_up, "dp", axis=1, tiled=True),
        preferred_element_type=jnp.float32,
    )
    full_gate, full_up, full_down = (
        lax.all_gather(w_gate, "dp", axis=1, tiled=True),
        lax.all_gather(w_up, "dp", axis=1, tiled=True),
        lax.all_gather(w_down, "dp", axis=2, tiled=True),
    )
    sigma = jax.nn.sigmoid(gate_term)
    active = gate_term * sigma
    activated = (active * up_term).astype(jnp.bfloat16)
    back_hidden = jnp.einsum("asd,afd->asf", slot_dy, full_down, preferred_element_type=jnp.float32)
    up_delta = (back_hidden * active).astype(jnp.bfloat16)
    gate_delta = (back_hidden * up_term * sigma * (1.0 + gate_term * (1.0 - sigma))).astype(
        jnp.bfloat16
    )
    pair_grad = (
        jnp.einsum("asf,adf->asd", gate_delta, full_gate, preferred_element_type=jnp.float32)
        + jnp.einsum("asf,adf->asd", up_delta, full_up, preferred_element_type=jnp.float32)
    ).astype(jnp.bfloat16)
    send_back = pair_grad.reshape(local_count, group_count, capacity, model_width).transpose(
        1, 0, 2, 3
    )
    send_back = send_back.reshape(expert_count, capacity, model_width)
    returned = lax.all_to_all(send_back, "expert", split_axis=0, concat_axis=0, tiled=True)
    per_pair = returned.reshape(expert_count * capacity, model_width)[slot_of].astype(jnp.float32)
    input_grad = jnp.sum(per_pair.reshape(tok_rows, top_count, model_width), axis=1).astype(
        jnp.bfloat16
    )
    block_width = local_count * hidden_units
    share_width = model_width // lax.axis_size("dp")
    part_x = slot_x
    term_gate = jnp.einsum("asd,asf->daf", part_x, gate_delta, preferred_element_type=jnp.float32)
    term_up = jnp.einsum("asd,asf->daf", part_x, up_delta, preferred_element_type=jnp.float32)
    term_down = jnp.einsum("asd,asf->daf", slot_dy, activated, preferred_element_type=jnp.float32)
    shares = lax.psum_scatter(
        jnp.concatenate(
            [
                term_gate.reshape(lax.axis_size("dp") * share_width, block_width),
                term_up.reshape(lax.axis_size("dp") * share_width, block_width),
                term_down.reshape(lax.axis_size("dp") * share_width, block_width),
            ],
            axis=1,
        ).astype(jnp.bfloat16),
        "dp",
        scatter_dimension=0,
        tiled=True,
    ).astype(jnp.float32)
    share_rows = shares.shape[0]

    def unpack(which):
        return shares[:, which * block_width : (which + 1) * block_width].reshape(
            share_rows, local_count, hidden_units
        )

    gate_grad = unpack(0).transpose(1, 0, 2).astype(jnp.bfloat16)
    up_grad = unpack(1).transpose(1, 0, 2).astype(jnp.bfloat16)
    down_grad = unpack(2).transpose(1, 2, 0).astype(jnp.bfloat16)
    return (input_grad, gate_grad, up_grad, down_grad)


def lined(dp, expert):
    return dp == 4 and expert == 8


def local(tokens, out_grad, routes, gate_values, w_gate, w_up, w_down):
    experts = lax.axis_size("expert") * w_gate.shape[0]
    capacity = slots_of(tokens.shape[0], routes.shape[1], experts)
    fits = w_gate.shape[0] == 1 and tokens.shape[0] <= 2 * capacity
    if not (fits and lined(lax.axis_size("dp"), lax.axis_size("expert"))):
        return routed(tokens, out_grad, routes, gate_values, w_gate, w_up, w_down)
    return dense(tokens, out_grad, routes, gate_values, w_gate, w_up, w_down)


def solution(mesh):
    return jax.shard_map(
        local,
        mesh=mesh,
        in_specs=(
            P(("dp", "expert"), None),
            P(("dp", "expert"), None),
            P(("dp", "expert"), None),
            P(("dp", "expert"), None),
            P("expert", "dp", None),
            P("expert", "dp", None),
            P("expert", None, "dp"),
        ),
        out_specs=(
            P(("dp", "expert"), None),
            P("expert", "dp", None),
            P("expert", "dp", None),
            P("expert", None, "dp"),
        ),
        check_vma=False,
    )
```

```python
import functools

import jax
import jax.numpy as jnp
from jax import lax
from jax.experimental import pallas as pl
from jax.experimental.pallas import tpu as pltpu
from jax.sharding import PartitionSpec as P


F32 = jnp.float32
BF16 = jnp.bfloat16
ANY = pl.BlockSpec(memory_space=pl.ANY)
VMEM = pl.BlockSpec(memory_space=pltpu.VMEM)
SMEM = pl.BlockSpec(memory_space=pltpu.SMEM)
LIMIT = 12 * 1024 * 1024
LANES = 128
NN = (((1,), (0,)), ((), ()))
NT = (((1,), (1,)), ((), ()))


def mm(a, b, dims):
    return lax.dot_general(a, b, dims, preferred_element_type=F32)


def slots_of(tok_rows, top_count, expert_count):
    return min(tok_rows, max(2, 9 * tok_rows * top_count // (8 * expert_count)))


def call(body, outs, ins, scratch, flops, moved, aliases=None):
    return pl.pallas_call(
        body,
        input_output_aliases=aliases or {},
        out_shape=[jax.ShapeDtypeStruct(s, d) for s, d, _ in outs],
        in_specs=[s for _, s in ins],
        out_specs=[s for _, _, s in outs],
        scratch_shapes=scratch,
        compiler_params=pltpu.CompilerParams(vmem_limit_bytes=LIMIT),
        cost_estimate=pl.CostEstimate(flops=flops, bytes_accessed=moved, transcendentals=0),
    )(*[a for a, _ in ins])


TWO = ((0, 2), (1, 3), (2, 0), (3, 1))
OUTER = ((0, 1), (1, 0), (2, 3), (3, 2))
INNER = ((1, 2), (2, 1))


def prep_body(experts, routes, gates, rows, out):
    tok, width = rows.shape
    line = lax.broadcasted_iota(jnp.int32, (LANES, tok), 0)
    term, named = line // experts, line % experts
    value = jnp.zeros((LANES, tok), F32)
    for k in range(routes.shape[0]):
        value += jnp.where(routes[k : k + 1, :] == named, gates[k : k + 1, :], 0.0)
    high = value.astype(BF16).astype(F32)
    mid = (value - high).astype(BF16).astype(F32)
    low = value - high - mid
    value = jnp.where(term == 0, high, jnp.where(term == 1, mid, jnp.where(term == 2, low, 0.0)))
    out[:, :width] = rows[...]
    out[:, width:] = jnp.transpose(value).astype(BF16)


class Copies:
    def __init__(self, sems):
        self.sems, self.used = sems, 0

    def start(self, src, dst):
        copy = pltpu.make_async_copy(src, dst, self.sems.at[self.used])
        self.used += 1
        copy.start()
        return copy

    def pick(self, first, src, other, dst):
        sem = self.sems.at[self.used]
        self.used += 1

        @pl.when(first)
        def _():
            pltpu.make_async_copy(src, dst, sem).start()

        @pl.when(jnp.logical_not(first))
        def _():
            pltpu.make_async_copy(other, dst, sem).start()

        return pltpu.make_async_copy(other, dst, sem)


def load_early(copies, pieces, dst, first=0):
    tok = pieces[0].shape[0]
    return [copies.start(src, dst.at[pl.ds((first + i) * tok, tok)]) for i, src in enumerate(pieces)]


def load_weights(copies, place, which, pieces, wg, wu):
    share = pieces[0].shape[0]
    started = []
    for i, k in enumerate(which):
        at = pl.ds((place[0] ^ k) * share, share)
        started += [copies.start(pieces[2 * i], wg.at[at]), copies.start(pieces[2 * i + 1], wu.at[at])]
    return started


def own_body(place, tokens, w_gate, w_up, x, wg, wu, sems):
    copies = Copies(sems)
    started = load_early(copies, (tokens,), x) + load_weights(copies, place, (0,), (w_gate, w_up), wg, wu)
    for c in started:
        c.wait()


def near_body(place, *refs):
    pieces, weights = refs[:5], refs[5:9]
    x, wg, wu, sems = refs[12:]
    copies = Copies(sems)
    for c in load_early(copies, pieces, x, 1) + load_weights(copies, place, (1, 2), weights, wg, wu):
        c.wait()


def load_late(copies, chip, pieces, dst):
    tok = pieces[0].shape[0]
    middle = jnp.logical_or(chip == 1, chip == 2)
    return [
        copies.pick(middle, pieces[2 * core], pieces[2 * core + 1], dst.at[pl.ds(core * tok, tok)]) for core in (0, 1)
    ]


def pre_blocks(x, first, count, wg, wu, act, active_out, slope_out):
    tn = 256

    def step(i, _):
        r = slice(first, first + count)
        c = pl.ds(pl.multiple_of(i * tn, tn), tn)
        lhs = x[r, :]
        gate = mm(lhs, wg[:, c], NN)
        up = mm(lhs, wu[:, c], NN)
        activate(gate, up, r, c, act, active_out, slope_out)
        return 0

    lax.fori_loop(0, wg.shape[1] // tn, step, 0)


def activate(gate, up, r, c, act, active_out, slope_out):
    sigma = jax.nn.sigmoid(gate)
    active = gate * sigma
    act[r, c] = (active * up).astype(BF16)
    active_out[r, c] = active
    slope_out[r, c] = up * sigma * (1.0 + gate * (1.0 - sigma))


def pre_part_body(place, x, wg, wu, gate_part, up_part):
    tn, share = 256, wg.shape[0] // 4
    r = slice(0, x.shape[0] // 4 * 3)

    def step(i, _):
        c = pl.ds(pl.multiple_of(i * tn, tn), tn)
        gate = up = None
        for k in range(3):
            block = pl.ds(pl.multiple_of((place[0] ^ k) * share, share), share)
            lhs = x[r, block]
            more = mm(lhs, wg[block, c], NN), mm(lhs, wu[block, c], NN)
            gate, up = more if gate is None else (gate + more[0], up + more[1])
        gate_part[r, c] = gate
        up_part[r, c] = up
        return 0

    lax.fori_loop(0, wg.shape[1] // tn, step, 0)


def pre_early_body(place, *refs):
    x, gate_part, up_part = refs[2:5]
    act, active, slope, wg, wu, sems = refs[7:]
    for c in load_weights(Copies(sems), place, (3,), refs[:2], wg, wu):
        c.wait()
    tn, share = 256, wg.shape[0] // 4
    r = slice(0, x.shape[0] // 4 * 3)
    block = pl.ds(pl.multiple_of((place[0] ^ 3) * share, share), share)

    def step(i, _):
        c = pl.ds(pl.multiple_of(i * tn, tn), tn)
        lhs = x[r, block]
        gate = gate_part[r, c] + mm(lhs, wg[block, c], NN)
        up = up_part[r, c] + mm(lhs, wu[block, c], NN)
        activate(gate, up, r, c, act, active, slope)
        return 0

    lax.fori_loop(0, wg.shape[1] // tn, step, 0)


def pre_late_body(place, *refs):
    pieces, wg, wu = refs[:4], refs[4], refs[5]
    act, active, slope, x, sems = refs[10:]
    count = x.shape[0] // 4
    for c in load_late(Copies(sems), place[1], pieces, x.at[pl.ds(3 * count, count)]):
        c.wait()
    pre_blocks(x, 3 * count, count, wg, wu, act, active, slope)


def scale(experts, expert, raw, y, row):
    tok, width = raw.shape[0], y.shape[1]
    lane = lax.broadcasted_iota(jnp.int32, (tok, LANES), 1)
    mine = jnp.logical_and(lane % experts == expert, lane < 3 * experts)
    gate = jnp.sum(jnp.where(mine, raw[:, width:].astype(F32), 0.0), axis=1, keepdims=True)
    y[row : row + tok, :] = (raw[:, :width].astype(F32) * gate).astype(BF16)


def load_scaled(experts, expert, copies, pieces, raw, y, blocks):
    tok = pieces[0].shape[0]
    at = [raw.at[pl.ds(i * tok, tok)] for i in range(len(pieces))]
    started = [copies.start(src, dst) for src, dst in zip(pieces, at)]
    for copy, dst, block in zip(started, at, blocks):
        copy.wait()
        scale(experts, expert, dst, y, block * tok)


def scale_early_body(experts, place, *refs):
    y, raw, sems = refs[4:]
    load_scaled(experts, place[2], Copies(sems), refs[:4], raw, y, (0, 1, 3, 4))


def down_blocks(place, act, y, first, count, wanted, put):
    share = y.shape[1] // 4
    half = act.shape[1] // 2
    rows = slice(first, first + count)
    for h in (0, 1):
        turned = jnp.transpose(act[rows, h * half : (h + 1) * half])
        for which, k, target in wanted:
            if which == h:
                cols = pl.ds(pl.multiple_of((place[0] ^ k) * share, share), share)
                put(target, mm(turned, y[rows, cols], NN))


def down_early_body(experts, place, *refs):
    pieces, act = refs[:2], refs[2]
    part, y, raw, sems = refs[4:]
    load_scaled(experts, place[2], Copies(sems), pieces, raw, y, (2, 5))

    def put(target, value):
        part[target] = value

    early = y.shape[0] // 4 * 3
    down_blocks(place, act, y, 0, early, ((0, 1, 0), (0, 3, 1), (1, 2, 2), (1, 3, 3)), put)


def down_send_body(experts, place, *refs):
    pieces, act, part = refs[:4], refs[4], refs[5]
    send_a, send_b, y, raw, sems = refs[7:]
    for c in load_late(Copies(sems), place[1], pieces, raw):
        c.wait()
    count = raw.shape[0]
    first = y.shape[0] - count
    for core in (0, 1):
        tok = count // 2
        scale(experts, place[2], raw.at[pl.ds(core * tok, tok)], y, first + core * tok)

    def put(target, value):
        dst = (send_a, send_b)[target // 2]
        dst[target % 2] = (part[target] + value).astype(BF16)

    down_blocks(place, act, y, first, count, ((0, 1, 0), (0, 3, 1), (1, 2, 2), (1, 3, 3)), put)


def down_keep_body(place, act, y, a0, a1, b0, b1):
    def put(target, value):
        target[...] = value.astype(BF16)

    down_blocks(place, act, y, 0, y.shape[0], ((0, 0, a0), (0, 2, a1), (1, 0, b0), (1, 1, b1)), put)


def last_body(gate_sum, gate_last, up_sum, up_last, gate_out, up_out, gate, up, sems):
    copies = Copies(sems)
    part = gate.shape[1] // 2
    started = []
    for total, last, held, out in ((gate_sum, gate_last, gate, gate_out), (up_sum, up_last, up, up_out)):
        for i in (0, 1):
            r = slice(i * part, (i + 1) * part)
            held[0, r, :] = (total[r, :].astype(F32) + last[r, :].astype(F32)).astype(BF16)
            at = pl.ds(i * part, part)
            started.append(copies.start(held.at[0, at], out.at[0, at]))
    for c in started:
        c.wait()


def back_body(place, y, active, slope, *refs):
    own, halves = refs[0], refs[1:7]
    gate_delta, up_delta, w, sems = refs[7:]
    me = place[0]
    copies = Copies(sems)
    hidden, share = own.shape
    half = hidden // 2
    started = [copies.start(own, w.at[me])]
    for i, src in enumerate(halves):
        started.append(copies.start(src, w.at[me ^ (1 + i // 2), pl.ds(i % 2 * half, half)]))
    for c in started:
        c.wait()
    rows = y.shape[0]
    tm, tn = rows // 2, 256

    def step(i, _):
        r = pl.ds(pl.multiple_of(i // (hidden // tn) * tm, tm), tm)
        c = pl.ds(pl.multiple_of(i % (hidden // tn) * tn, tn), tn)
        back = mm(y[r, 0:share], w[0, c, :], NT)
        for j in range(1, 4):
            back += mm(y[r, j * share : (j + 1) * share], w[j, c, :], NT)
        up_delta[r, c] = (back * active[r, c]).astype(BF16)
        gate_delta[r, c] = (back * slope[r, c]).astype(BF16)
        return 0

    lax.fori_loop(0, 2 * (hidden // tn), step, 0)


def grad_blocks(place, x, wanted):
    share = x.shape[1] // 4
    tm = share // 2
    for k, targets in wanted:

        def step(i, _, k=k, targets=targets):
            cols = pl.ds(pl.multiple_of((place[0] ^ k) * share + i * tm, tm), tm)
            turned = jnp.transpose(x[:, cols])
            part = pl.ds(pl.multiple_of(i * tm, tm), tm)
            for delta, dst, slot in targets:
                value = mm(turned, delta[...], NN).astype(BF16)
                if slot is None:
                    dst[part, :] = value
                else:
                    dst[slot, part, :] = value
            return 0

        lax.fori_loop(0, 2, step, 0)


def grad_send_body(place, x, gd, ud, gate_send, up_send):
    grad_blocks(
        place, x, ((1, [(gd, gate_send, 0)]), (3, [(gd, gate_send, 1), (ud, up_send, 1)]), (2, [(ud, up_send, 0)]))
    )


def grad_keep_body(place, x, gd, ud, g0, g1, u0, u1):
    grad_blocks(place, x, ((2, [(gd, g1, None)]), (1, [(ud, u1, None)]), (0, [(gd, g0, None), (ud, u0, None)])))


def pair_body(gate_delta, up_delta, wg, wu, send, keep):
    tn = 256
    part = keep.shape[0] // 4

    def step(i, _):
        c = pl.ds(pl.multiple_of(i * tn, tn), tn)
        total = (mm(gate_delta[...], wg[c, :], NT) + mm(up_delta[...], wu[c, :], NT)).astype(BF16)
        keep[: 3 * part, c] = total[: 3 * part]
        send[: 3 * part, c] = total[3 * part : 6 * part]
        keep[3 * part :, c] = total[6 * part : 7 * part]
        send[3 * part :, c] = total[7 * part :]
        return 0

    lax.fori_loop(0, wg.shape[0] // tn, step, 0)


def add(*terms):
    total = terms[0].astype(F32)
    for term in terms[1:]:
        total = total + term.astype(F32)
    return total.astype(BF16)


def dense(tokens, out_grad, routes, gate_values, w_gate, w_up, w_down):
    tok, width = tokens.shape
    experts = lax.axis_size("expert")
    chips = experts // 2
    hidden = w_gate.shape[2]
    share = width // 4
    half = hidden // 2
    rows = experts * tok
    expert = lax.axis_index("expert")
    chip = expert // 2
    place = jnp.stack([lax.axis_index("dp"), chip, expert]).astype(jnp.int32)

    def to_x(block):
        return lax.ppermute(block, "dp", [(i, i ^ 1) for i in range(4)])

    def to_y(block):
        return lax.ppermute(block, "dp", [(i, i ^ 2) for i in range(4)])

    def hop(block, moves):
        return lax.ppermute(block, "expert", [(2 * a + c, 2 * b + c) for a, b in moves for c in (0, 1)])

    def swap(block, at=range(chips)):
        return lax.ppermute(block, "expert", [(2 * z + c, 2 * z + 1 - c) for z in at for c in (0, 1)])

    def line(own):
        two = hop(own, TWO)
        outer = hop(own, OUTER)
        inner = hop(own, INNER)
        far = hop(two, ((2, 3), (1, 0)))
        early = [own, two, outer, swap(own), swap(two), swap(outer)]
        late = [inner, far, swap(inner, (1, 2)), swap(far, (0, 3))]
        return early, late

    x_early, x_late = line(tokens)
    (y_own,) = call(
        functools.partial(prep_body, experts),
        [((tok, width + LANES), BF16, VMEM)],
        [(routes.T, VMEM), (gate_values.T, VMEM), (out_grad, VMEM)],
        [],
        1000,
        4 * tok * width,
    )
    y_early, y_late = line(y_own)

    wg0, wu0, wd0 = w_gate[0], w_up[0], w_down[0]
    wg1, wu2 = to_x(wg0), to_y(wu0)
    wg2, wu1 = to_y(wg0), to_x(wu0)
    wg3, wu3 = to_y(wg1), to_x(wu2)
    da0, db0 = wd0[:half], wd0[half:]
    da1, db2 = to_x(da0), to_y(db0)
    da2, db1 = to_y(da0), to_x(db0)
    da3, db3 = to_y(da1), to_x(db2)

    def dma(n):
        return pltpu.SemaphoreType.DMA((n,))

    def anys(arrays):
        return [(a, ANY) for a in arrays]

    x_out = ((rows, width), BF16, VMEM)
    weight = ((width, hidden), BF16, VMEM)
    flat = ((rows, hidden), BF16, VMEM)
    wide = ((rows, hidden), F32, VMEM)
    x, wg, wu = call(
        own_body,
        [x_out, weight, weight],
        [(place, SMEM)] + anys((tokens, wg0, wu0)),
        [dma(3)],
        1000,
        width * (2 * tok + hidden),
    )
    x, wg, wu = call(
        near_body,
        [x_out, weight, weight],
        [(place, SMEM)] + anys(x_early[1:]) + anys((wg1, wu1, wg2, wu2)) + [(x, VMEM), (wg, VMEM), (wu, VMEM)],
        [dma(9)],
        1000,
        width * (10 * tok + 2 * hidden),
        {10: 0, 11: 1, 12: 2},
    )
    parts = call(
        pre_part_body,
        [wide, wide],
        [(place, SMEM), (x, VMEM), (wg, VMEM), (wu, VMEM)],
        [],
        9 * rows * width * hidden // 4,
        3 * rows * width + 6 * width * hidden + 6 * rows * hidden,
    )
    *pre, wg, wu = call(
        pre_early_body,
        [flat, wide, wide, weight, weight],
        [(place, SMEM)] + anys((wg3, wu3)) + [(a, VMEM) for a in (x, *parts, wg, wu)],
        [dma(2)],
        3 * rows * width * hidden // 4,
        rows * width + 2 * width * hidden + 16 * rows * hidden,
        {4: 1, 5: 2, 6: 3, 7: 4},
    )
    act, active, slope, x = call(
        pre_late_body,
        [flat, wide, wide, x_out],
        [(place, SMEM)] + anys(x_late) + [(a, VMEM) for a in (wg, wu, *pre, x)],
        [dma(2)],
        rows * width * hidden,
        rows * width + 4 * width * hidden + 3 * rows * hidden,
        {7 + i: i for i in range(4)},
    )
    y_rows = ((rows, width), BF16, VMEM)
    (y,) = call(
        functools.partial(scale_early_body, experts),
        [y_rows],
        [(place, SMEM)] + anys((y_early[0], y_early[1], y_early[3], y_early[4])),
        [pltpu.VMEM((4 * tok, width + LANES), BF16), dma(4)],
        rows * width,
        3 * rows * width,
    )
    piece = (2, half, share)
    part, y = call(
        functools.partial(down_early_body, experts),
        [((4, half, share), F32, VMEM), y_rows],
        [(place, SMEM)] + anys((y_early[2], y_early[5])) + [(act, VMEM), (y, VMEM)],
        [pltpu.VMEM((2 * tok, width + LANES), BF16), dma(2)],
        3 * rows * width * hidden // 4,
        2 * (rows * width + rows * hidden + width * hidden),
        {4: 1},
    )
    send_a, send_b, y = call(
        functools.partial(down_send_body, experts),
        [(piece, BF16, VMEM)] * 2 + [((rows, width), BF16, VMEM)],
        [(place, SMEM)] + anys(y_late) + [(act, VMEM), (part, VMEM), (y, VMEM)],
        [pltpu.VMEM((2 * tok, width + LANES), BF16), dma(2)],
        rows * width * hidden // 4,
        2 * (rows * width + rows * hidden // 4 + width * hidden),
        {7: 2},
    )
    got_a, got_b = to_x(send_a), to_y(send_b)
    gate_delta, up_delta = call(
        back_body,
        [((rows, hidden), BF16, VMEM)] * 2,
        [(place, SMEM), (y, VMEM), (active, VMEM), (slope, VMEM)] + anys((wd0, da1, db1, da2, db2, da3, db3)),
        [pltpu.VMEM((4, hidden, share), BF16), dma(7)],
        2 * rows * width * hidden,
        2 * (rows * width + width * hidden) + 12 * rows * hidden,
    )
    gate_send, up_send = call(
        grad_send_body,
        [((2, share, hidden), BF16, VMEM)] * 2,
        [(place, SMEM), (x, VMEM), (gate_delta, VMEM), (up_delta, VMEM)],
        [],
        2 * rows * width * hidden,
        2 * (rows * width + 2 * rows * hidden + width * hidden),
    )
    gate_got, up_got = to_x(gate_send), to_y(up_send)
    pair_send, pair_keep = call(
        pair_body,
        [((rows // 2, width), BF16, VMEM)] * 2,
        [(gate_delta, VMEM), (up_delta, VMEM), (wg, VMEM), (wu, VMEM)],
        [],
        4 * rows * width * hidden,
        2 * (rows * width + 2 * rows * hidden + 2 * width * hidden),
    )
    total = add(pair_keep, swap(pair_send)).reshape(chips, tok, width)
    keep_a0, keep_a1, keep_b0, keep_b1 = call(
        down_keep_body,
        [((half, share), BF16, VMEM)] * 4,
        [(place, SMEM), (act, VMEM), (y, VMEM)],
        [],
        rows * width * hidden,
        2 * (rows * width + rows * hidden + width * hidden // 2),
    )
    gate0, gate1, up0, up1 = call(
        grad_keep_body,
        [((share, hidden), BF16, VMEM)] * 4,
        [(place, SMEM), (x, VMEM), (gate_delta, VMEM), (up_delta, VMEM)],
        [],
        2 * rows * width * hidden,
        2 * (rows * width + 2 * rows * hidden + width * hidden),
    )
    down_a, down_b = to_y(add(keep_a1, got_a[1])), to_x(add(keep_b1, got_b[1]))
    gate1, up1 = add(gate1, gate_got[1]), add(up1, up_got[1])
    sums = add(gate0, gate_got[0]), add(up0, up_got[0])
    gate_last, up_last = to_y(gate1), to_x(up1)
    gate_sum, up_sum = lax.optimization_barrier(sums)
    down_grad = jnp.concatenate([add(keep_a0, got_a[0], down_a), add(keep_b0, got_b[0], down_b)], axis=0)
    result = (1, share, hidden)
    gate_grad, up_grad = call(
        last_body,
        [(result, BF16, ANY)] * 2,
        [(a, VMEM) for a in (gate_sum, gate_last, up_sum, up_last)],
        [pltpu.VMEM(result, BF16)] * 2 + [dma(4)],
        share * hidden,
        12 * share * hidden,
    )

    far = hop(total[3], ((0, 1), (3, 2)))
    inner = hop(total[3], INNER)
    outer = hop(total[2], OUTER)
    two = hop(add(total[1], far), TWO)
    input_grad = add(total[0], inner, outer, two)
    return input_grad, gate_grad, up_grad, down_grad[None]


def routed(tokens, out_grad, routes, gate_values, w_gate, w_up, w_down):
    tok_rows, model_width = tokens.shape
    top_count = routes.shape[1]
    group_count = lax.axis_size("expert")
    local_count = w_gate.shape[0]
    expert_count = group_count * local_count
    hidden_units = w_gate.shape[2]
    capacity = slots_of(tok_rows, top_count, expert_count)
    pair_count = tok_rows * top_count
    slot_count = group_count * capacity
    expert_of = routes.reshape(-1)
    onehot = (expert_of[:, None] == jnp.arange(expert_count, dtype=jnp.int32)[None, :]).astype(
        jnp.int32
    )
    before = jnp.cumsum(onehot, axis=0) - onehot
    placed = jnp.sum(before * onehot, axis=1)
    slot_of = expert_of * capacity + placed
    slot_table = jnp.full((expert_count * capacity,), pair_count, jnp.int32)
    slot_table = slot_table.at[slot_of].set(jnp.arange(pair_count, dtype=jnp.int32))
    filled = slot_table < pair_count
    source = jnp.where(filled, slot_table, 0)
    owner_row = source // top_count
    send_x = jnp.where(filled[:, None], tokens[owner_row], jnp.zeros((), jnp.bfloat16))
    scaled = gate_values.reshape(-1)[source][:, None] * out_grad[owner_row].astype(jnp.float32)
    send_dy = jnp.where(filled[:, None], scaled, 0.0).astype(jnp.bfloat16)
    send_x = send_x.reshape(expert_count, capacity, model_width)
    send_dy = send_dy.reshape(expert_count, capacity, model_width)
    recv_x, recv_dy = (
        lax.all_to_all(send_x, "expert", split_axis=0, concat_axis=0, tiled=True),
        lax.all_to_all(send_dy, "expert", split_axis=0, concat_axis=0, tiled=True),
    )

    def to_local(stacked):
        shaped = stacked.reshape(group_count, local_count, capacity, model_width)
        return shaped.transpose(1, 0, 2, 3).reshape(local_count, slot_count, model_width)

    slot_x = to_local(recv_x)
    slot_dy = to_local(recv_dy)
    part_x = slot_x
    gate_term = jnp.einsum(
        "asd,adf->asf",
        part_x,
        lax.all_gather(w_gate, "dp", axis=1, tiled=True),
        preferred_element_type=jnp.float32,
    )
    up_term = jnp.einsum(
        "asd,adf->asf",
        part_x,
        lax.all_gather(w_up, "dp", axis=1, tiled=True),
        preferred_element_type=jnp.float32,
    )
    full_gate, full_up, full_down = (
        lax.all_gather(w_gate, "dp", axis=1, tiled=True),
        lax.all_gather(w_up, "dp", axis=1, tiled=True),
        lax.all_gather(w_down, "dp", axis=2, tiled=True),
    )
    sigma = jax.nn.sigmoid(gate_term)
    active = gate_term * sigma
    activated = (active * up_term).astype(jnp.bfloat16)
    back_hidden = jnp.einsum("asd,afd->asf", slot_dy, full_down, preferred_element_type=jnp.float32)
    up_delta = (back_hidden * active).astype(jnp.bfloat16)
    gate_delta = (back_hidden * up_term * sigma * (1.0 + gate_term * (1.0 - sigma))).astype(
        jnp.bfloat16
    )
    pair_grad = (
        jnp.einsum("asf,adf->asd", gate_delta, full_gate, preferred_element_type=jnp.float32)
        + jnp.einsum("asf,adf->asd", up_delta, full_up, preferred_element_type=jnp.float32)
    ).astype(jnp.bfloat16)
    send_back = pair_grad.reshape(local_count, group_count, capacity, model_width).transpose(
        1, 0, 2, 3
    )
    send_back = send_back.reshape(expert_count, capacity, model_width)
    returned = lax.all_to_all(send_back, "expert", split_axis=0, concat_axis=0, tiled=True)
    per_pair = returned.reshape(expert_count * capacity, model_width)[slot_of].astype(jnp.float32)
    input_grad = jnp.sum(per_pair.reshape(tok_rows, top_count, model_width), axis=1).astype(
        jnp.bfloat16
    )
    block_width = local_count * hidden_units
    share_width = model_width // lax.axis_size("dp")
    part_x = slot_x
    term_gate = jnp.einsum("asd,asf->daf", part_x, gate_delta, preferred_element_type=jnp.float32)
    term_up = jnp.einsum("asd,asf->daf", part_x, up_delta, preferred_element_type=jnp.float32)
    term_down = jnp.einsum("asd,asf->daf", slot_dy, activated, preferred_element_type=jnp.float32)
    shares = lax.psum_scatter(
        jnp.concatenate(
            [
                term_gate.reshape(lax.axis_size("dp") * share_width, block_width),
                term_up.reshape(lax.axis_size("dp") * share_width, block_width),
                term_down.reshape(lax.axis_size("dp") * share_width, block_width),
            ],
            axis=1,
        ).astype(jnp.bfloat16),
        "dp",
        scatter_dimension=0,
        tiled=True,
    ).astype(jnp.float32)
    share_rows = shares.shape[0]

    def unpack(which):
        return shares[:, which * block_width : (which + 1) * block_width].reshape(
            share_rows, local_count, hidden_units
        )

    gate_grad = unpack(0).transpose(1, 0, 2).astype(jnp.bfloat16)
    up_grad = unpack(1).transpose(1, 0, 2).astype(jnp.bfloat16)
    down_grad = unpack(2).transpose(1, 2, 0).astype(jnp.bfloat16)
    return (input_grad, gate_grad, up_grad, down_grad)


def lined(dp, expert):
    return dp == 4 and expert == 8


def local(tokens, out_grad, routes, gate_values, w_gate, w_up, w_down):
    experts = lax.axis_size("expert") * w_gate.shape[0]
    capacity = slots_of(tokens.shape[0], routes.shape[1], experts)
    fits = w_gate.shape[0] == 1 and tokens.shape[0] <= 2 * capacity
    if not (fits and lined(lax.axis_size("dp"), lax.axis_size("expert"))):
        return routed(tokens, out_grad, routes, gate_values, w_gate, w_up, w_down)
    return dense(tokens, out_grad, routes, gate_values, w_gate, w_up, w_down)


def solution(mesh):
    return jax.shard_map(
        local,
        mesh=mesh,
        in_specs=(
            P(("dp", "expert"), None),
            P(("dp", "expert"), None),
            P(("dp", "expert"), None),
            P(("dp", "expert"), None),
            P("expert", "dp", None),
            P("expert", "dp", None),
            P("expert", None, "dp"),
        ),
        out_specs=(
            P(("dp", "expert"), None),
            P("expert", "dp", None),
            P("expert", "dp", None),
            P("expert", None, "dp"),
        ),
        check_vma=False,
    )
```

```python
import jax
import jax.numpy as jnp
from jax import lax
from jax.experimental import pallas as pl
from jax.experimental.pallas import tpu as pltpu
from jax.sharding import PartitionSpec as P


F32 = jnp.float32
BF16 = jnp.bfloat16
ANY = pl.BlockSpec(memory_space=pl.ANY)
VMEM = pl.BlockSpec(memory_space=pltpu.VMEM)
SMEM = pl.BlockSpec(memory_space=pltpu.SMEM)
LIMIT = 12 * 1024 * 1024
NN = (((1,), (0,)), ((), ()))
NT = (((1,), (1,)), ((), ()))


def mm(a, b, dims):
    return lax.dot_general(a, b, dims, preferred_element_type=F32)


def slots_of(tok_rows, top_count, expert_count):
    return min(tok_rows, max(2, 9 * tok_rows * top_count // (8 * expert_count)))


def call(body, outs, ins, scratch, flops, moved, aliases=None):
    return pl.pallas_call(
        body,
        input_output_aliases=aliases or {},
        out_shape=[jax.ShapeDtypeStruct(s, d) for s, d, _ in outs],
        in_specs=[s for _, s in ins],
        out_specs=[s for _, _, s in outs],
        scratch_shapes=scratch,
        compiler_params=pltpu.CompilerParams(vmem_limit_bytes=LIMIT),
        cost_estimate=pl.CostEstimate(flops=flops, bytes_accessed=moved, transcendentals=0),
    )(*[a for a, _ in ins])


TWO = ((0, 2), (1, 3), (2, 0), (3, 1))
OUTER = ((0, 1), (1, 0), (2, 3), (3, 2))
INNER = ((1, 2), (2, 1))


def prep_body(place, routes, gates, *outs):
    for k, out in enumerate(outs):
        value = jnp.zeros(out.shape, F32)
        for i in range(routes.shape[0]):
            value += jnp.where(routes[i : i + 1, :] == (place[2] ^ k), gates[i : i + 1, :], 0.0)
        out[...] = value


class Copies:
    def __init__(self, sems):
        self.sems, self.used = sems, 0

    def start(self, src, dst):
        copy = pltpu.make_async_copy(src, dst, self.sems.at[self.used])
        self.used += 1
        copy.start()
        return copy

    def pick(self, first, src, other, dst):
        sem = self.sems.at[self.used]
        self.used += 1

        @pl.when(first)
        def _():
            pltpu.make_async_copy(src, dst, sem).start()

        @pl.when(jnp.logical_not(first))
        def _():
            pltpu.make_async_copy(other, dst, sem).start()

        return pltpu.make_async_copy(other, dst, sem)


def load_early(copies, pieces, dst, first=0):
    tok = pieces[0].shape[0]
    return [copies.start(src, dst.at[pl.ds((first + i) * tok, tok)]) for i, src in enumerate(pieces)]


def load_weights(copies, place, which, pieces, wg, wu):
    share = pieces[0].shape[0]
    started = []
    for i, k in enumerate(which):
        at = pl.ds((place[0] ^ k) * share, share)
        started += [copies.start(pieces[2 * i], wg.at[at]), copies.start(pieces[2 * i + 1], wu.at[at])]
    return started


def own_body(place, tokens, w_gate, w_up, x, wg, wu, sems):
    copies = Copies(sems)
    started = load_early(copies, (tokens,), x) + load_weights(copies, place, (0,), (w_gate, w_up), wg, wu)
    for c in started:
        c.wait()


def near_body(place, *refs):
    pieces, weights = refs[:5], refs[5:9]
    x, wg, wu, sems = refs[12:]
    copies = Copies(sems)
    for c in load_early(copies, pieces, x, 1) + load_weights(copies, place, (1, 2), weights, wg, wu):
        c.wait()


def load_late(copies, chip, pieces, dst):
    tok = pieces[0].shape[0]
    middle = jnp.logical_or(chip == 1, chip == 2)
    return [
        copies.pick(middle, pieces[2 * core], pieces[2 * core + 1], dst.at[pl.ds(core * tok, tok)]) for core in (0, 1)
    ]


def pre_blocks(x, first, count, wg, wu, act, active_out, slope_out):
    tn = 256

    def step(i, _):
        r = slice(first, first + count)
        c = pl.ds(pl.multiple_of(i * tn, tn), tn)
        lhs = x[r, :]
        gate = mm(lhs, wg[:, c], NN)
        up = mm(lhs, wu[:, c], NN)
        activate(gate, up, r, c, act, active_out, slope_out)
        return 0

    lax.fori_loop(0, wg.shape[1] // tn, step, 0)


def activate(gate, up, r, c, act, active_out, slope_out):
    sigma = jax.nn.sigmoid(gate)
    active = gate * sigma
    act[r, c] = (active * up).astype(BF16)
    active_out[r, c] = active
    slope_out[r, c] = up * sigma * (1.0 + gate * (1.0 - sigma))


def pre_part_body(place, x, wg, wu, gate_part, up_part):
    tn, share = 256, wg.shape[0] // 4
    r = slice(0, x.shape[0] // 4 * 3)

    def step(i, _):
        c = pl.ds(pl.multiple_of(i * tn, tn), tn)
        gate = up = None
        for k in range(3):
            block = pl.ds(pl.multiple_of((place[0] ^ k) * share, share), share)
            lhs = x[r, block]
            more = mm(lhs, wg[block, c], NN), mm(lhs, wu[block, c], NN)
            gate, up = more if gate is None else (gate + more[0], up + more[1])
        gate_part[r, c] = gate
        up_part[r, c] = up
        return 0

    lax.fori_loop(0, wg.shape[1] // tn, step, 0)


def pre_early_body(place, *refs):
    x, gate_part, up_part = refs[2:5]
    act, active, slope, wg, wu, sems = refs[7:]
    for c in load_weights(Copies(sems), place, (3,), refs[:2], wg, wu):
        c.wait()
    tn, share = 256, wg.shape[0] // 4
    r = slice(0, x.shape[0] // 4 * 3)
    block = pl.ds(pl.multiple_of((place[0] ^ 3) * share, share), share)

    def step(i, _):
        c = pl.ds(pl.multiple_of(i * tn, tn), tn)
        lhs = x[r, block]
        gate = gate_part[r, c] + mm(lhs, wg[block, c], NN)
        up = up_part[r, c] + mm(lhs, wu[block, c], NN)
        activate(gate, up, r, c, act, active, slope)
        return 0

    lax.fori_loop(0, wg.shape[1] // tn, step, 0)


def pre_late_body(place, *refs):
    pieces, wg, wu = refs[:4], refs[4], refs[5]
    act, active, slope, x, sems = refs[10:]
    count = x.shape[0] // 4
    for c in load_late(Copies(sems), place[1], pieces, x.at[pl.ds(3 * count, count)]):
        c.wait()
    pre_blocks(x, 3 * count, count, wg, wu, act, active, slope)


def scale(gate, raw, y, row):
    tok = raw.shape[0]
    column = jnp.transpose(jnp.broadcast_to(gate[...], (tok, tok)))[:, :1]
    y[row : row + tok, :] = (raw[...].astype(F32) * column).astype(BF16)


def load_scaled(copies, pieces, gates, raw, y, blocks):
    tok = pieces[0].shape[0]
    at = [raw.at[pl.ds(i * tok, tok)] for i in range(len(pieces))]
    started = [copies.start(src, dst) for src, dst in zip(pieces, at)]
    for copy, gate, dst, block in zip(started, gates, at, blocks):
        copy.wait()
        scale(gate, dst, y, block * tok)


def scale_early_body(*refs):
    y, raw, sems = refs[8:]
    load_scaled(Copies(sems), refs[:4], refs[4:8], raw, y, (0, 1, 3, 4))


def down_blocks(place, act, y, first, count, wanted, put):
    share = y.shape[1] // 4
    half = act.shape[1] // 2
    rows = slice(first, first + count)
    for h in (0, 1):
        turned = jnp.transpose(act[rows, h * half : (h + 1) * half])
        for which, k, target in wanted:
            if which == h:
                cols = pl.ds(pl.multiple_of((place[0] ^ k) * share, share), share)
                put(target, mm(turned, y[rows, cols], NN))


def down_early_body(place, *refs):
    pieces, gates, act = refs[:2], refs[2:4], refs[4]
    part, y, raw, sems = refs[6:]
    load_scaled(Copies(sems), pieces, gates, raw, y, (2, 5))

    def put(target, value):
        part[target] = value

    early = y.shape[0] // 4 * 3
    down_blocks(place, act, y, 0, early, ((0, 1, 0), (0, 3, 1), (1, 2, 2), (1, 3, 3)), put)


def down_send_body(place, *refs):
    pieces, gates, act, part = refs[:4], refs[4:6], refs[6], refs[7]
    send_a, send_b, y, raw, sems = refs[9:]
    for c in load_late(Copies(sems), place[1], pieces, raw):
        c.wait()
    count = raw.shape[0]
    first = y.shape[0] - count
    for core in (0, 1):
        tok = count // 2
        scale(gates[core], raw.at[pl.ds(core * tok, tok)], y, first + core * tok)

    def put(target, value):
        dst = (send_a, send_b)[target // 2]
        dst[target % 2] = (part[target] + value).astype(BF16)

    down_blocks(place, act, y, first, count, ((0, 1, 0), (0, 3, 1), (1, 2, 2), (1, 3, 3)), put)


def down_keep_body(place, act, y, a0, a1, b0, b1):
    def put(target, value):
        target[...] = value.astype(BF16)

    down_blocks(place, act, y, 0, y.shape[0], ((0, 0, a0), (0, 2, a1), (1, 0, b0), (1, 1, b1)), put)


def last_body(gate_sum, gate_last, up_sum, up_last, gate_out, up_out, gate, up, sems):
    copies = Copies(sems)
    part = gate.shape[1] // 2
    started = []
    for total, last, held, out in ((gate_sum, gate_last, gate, gate_out), (up_sum, up_last, up, up_out)):
        for i in (0, 1):
            r = slice(i * part, (i + 1) * part)
            held[0, r, :] = (total[r, :].astype(F32) + last[r, :].astype(F32)).astype(BF16)
            at = pl.ds(i * part, part)
            started.append(copies.start(held.at[0, at], out.at[0, at]))
    for c in started:
        c.wait()


def back_body(place, y, active, slope, *refs):
    own, halves = refs[0], refs[1:7]
    gate_delta, up_delta, w, sems = refs[7:]
    me = place[0]
    copies = Copies(sems)
    hidden, share = own.shape
    half = hidden // 2
    started = [copies.start(own, w.at[me])]
    for i, src in enumerate(halves):
        started.append(copies.start(src, w.at[me ^ (1 + i // 2), pl.ds(i % 2 * half, half)]))
    for c in started:
        c.wait()
    rows = y.shape[0]
    tm, tn = rows // 2, 256

    def step(i, _):
        r = pl.ds(pl.multiple_of(i // (hidden // tn) * tm, tm), tm)
        c = pl.ds(pl.multiple_of(i % (hidden // tn) * tn, tn), tn)
        back = mm(y[r, 0:share], w[0, c, :], NT)
        for j in range(1, 4):
            back += mm(y[r, j * share : (j + 1) * share], w[j, c, :], NT)
        up_delta[r, c] = (back * active[r, c]).astype(BF16)
        gate_delta[r, c] = (back * slope[r, c]).astype(BF16)
        return 0

    lax.fori_loop(0, 2 * (hidden // tn), step, 0)


def grad_blocks(place, x, wanted):
    share = x.shape[1] // 4
    tm = share // 2
    for k, targets in wanted:

        def step(i, _, k=k, targets=targets):
            cols = pl.ds(pl.multiple_of((place[0] ^ k) * share + i * tm, tm), tm)
            turned = jnp.transpose(x[:, cols])
            part = pl.ds(pl.multiple_of(i * tm, tm), tm)
            for delta, dst, slot in targets:
                value = mm(turned, delta[...], NN).astype(BF16)
                if slot is None:
                    dst[part, :] = value
                else:
                    dst[slot, part, :] = value
            return 0

        lax.fori_loop(0, 2, step, 0)


def grad_send_body(place, x, gd, ud, gate_send, up_send):
    grad_blocks(
        place, x, ((1, [(gd, gate_send, 0)]), (3, [(gd, gate_send, 1), (ud, up_send, 1)]), (2, [(ud, up_send, 0)]))
    )


def grad_keep_body(place, x, gd, ud, g0, g1, u0, u1):
    grad_blocks(place, x, ((2, [(gd, g1, None)]), (1, [(ud, u1, None)]), (0, [(gd, g0, None), (ud, u0, None)])))


def pair_body(gate_delta, up_delta, wg, wu, send, keep):
    tn = 256
    part = keep.shape[0] // 4

    def step(i, _):
        c = pl.ds(pl.multiple_of(i * tn, tn), tn)
        total = (mm(gate_delta[...], wg[c, :], NT) + mm(up_delta[...], wu[c, :], NT)).astype(BF16)
        keep[: 3 * part, c] = total[: 3 * part]
        send[: 3 * part, c] = total[3 * part : 6 * part]
        keep[3 * part :, c] = total[6 * part : 7 * part]
        send[3 * part :, c] = total[7 * part :]
        return 0

    lax.fori_loop(0, wg.shape[0] // tn, step, 0)


def add(*terms):
    total = terms[0].astype(F32)
    for term in terms[1:]:
        total = total + term.astype(F32)
    return total.astype(BF16)


def dense(tokens, out_grad, routes, gate_values, w_gate, w_up, w_down):
    tok, width = tokens.shape
    experts = lax.axis_size("expert")
    chips = experts // 2
    hidden = w_gate.shape[2]
    share = width // 4
    half = hidden // 2
    rows = experts * tok
    expert = lax.axis_index("expert")
    chip = expert // 2
    place = jnp.stack([lax.axis_index("dp"), chip, expert]).astype(jnp.int32)

    def to_x(block):
        return lax.ppermute(block, "dp", [(i, i ^ 1) for i in range(4)])

    def to_y(block):
        return lax.ppermute(block, "dp", [(i, i ^ 2) for i in range(4)])

    def hop(block, moves):
        return lax.ppermute(block, "expert", [(2 * a + c, 2 * b + c) for a, b in moves for c in (0, 1)])

    def swap(block, at=range(chips)):
        return lax.ppermute(block, "expert", [(2 * z + c, 2 * z + 1 - c) for z in at for c in (0, 1)])

    def line(own):
        two = hop(own, TWO)
        outer = hop(own, OUTER)
        inner = hop(own, INNER)
        far = hop(two, ((2, 3), (1, 0)))
        early = [own, two, outer, swap(own), swap(two), swap(outer)]
        late = [inner, far, swap(inner, (1, 2)), swap(far, (0, 3))]
        return early, late

    x_early, x_late = line(tokens)
    gates = list(call(
        prep_body,
        [((1, tok), F32, VMEM)] * experts,
        [(place, SMEM), (routes.T, VMEM), (gate_values.T, VMEM)],
        [],
        1000,
        1000,
    ))
    for k in range(1, experts):
        gates[k] = lax.ppermute(gates[k], "expert", [(e, e ^ k) for e in range(experts)])

    def gates_of(*distances):
        return [(gates[k], VMEM) for k in distances]

    y_early, y_late = line(out_grad)

    wg0, wu0, wd0 = w_gate[0], w_up[0], w_down[0]
    wg1, wu2 = to_x(wg0), to_y(wu0)
    wg2, wu1 = to_y(wg0), to_x(wu0)
    wg3, wu3 = to_y(wg1), to_x(wu2)
    da0, db0 = wd0[:half], wd0[half:]
    da1, db2 = to_x(da0), to_y(db0)
    da2, db1 = to_y(da0), to_x(db0)
    da3, db3 = to_y(da1), to_x(db2)

    def dma(n):
        return pltpu.SemaphoreType.DMA((n,))

    def anys(arrays):
        return [(a, ANY) for a in arrays]

    x_out = ((rows, width), BF16, VMEM)
    weight = ((width, hidden), BF16, VMEM)
    flat = ((rows, hidden), BF16, VMEM)
    wide = ((rows, hidden), F32, VMEM)
    x, wg, wu = call(
        own_body,
        [x_out, weight, weight],
        [(place, SMEM)] + anys((tokens, wg0, wu0)),
        [dma(3)],
        1000,
        width * (2 * tok + hidden),
    )
    x, wg, wu = call(
        near_body,
        [x_out, weight, weight],
        [(place, SMEM)] + anys(x_early[1:]) + anys((wg1, wu1, wg2, wu2)) + [(x, VMEM), (wg, VMEM), (wu, VMEM)],
        [dma(9)],
        1000,
        width * (10 * tok + 2 * hidden),
        {10: 0, 11: 1, 12: 2},
    )
    parts = call(
        pre_part_body,
        [wide, wide],
        [(place, SMEM), (x, VMEM), (wg, VMEM), (wu, VMEM)],
        [],
        9 * rows * width * hidden // 4,
        3 * rows * width + 6 * width * hidden + 6 * rows * hidden,
    )
    *pre, wg, wu = call(
        pre_early_body,
        [flat, wide, wide, weight, weight],
        [(place, SMEM)] + anys((wg3, wu3)) + [(a, VMEM) for a in (x, *parts, wg, wu)],
        [dma(2)],
        3 * rows * width * hidden // 4,
        rows * width + 2 * width * hidden + 16 * rows * hidden,
        {4: 1, 5: 2, 6: 3, 7: 4},
    )
    y_rows = ((rows, width), BF16, VMEM)
    (y,) = call(
        scale_early_body,
        [y_rows],
        anys((y_early[0], y_early[1], y_early[3], y_early[4])) + gates_of(0, 4, 1, 5),
        [pltpu.VMEM((4 * tok, width), BF16), dma(4)],
        rows * width,
        3 * rows * width,
    )
    part, y = call(
        down_early_body,
        [((4, half, share), F32, VMEM), y_rows],
        [(place, SMEM)] + anys((y_early[2], y_early[5])) + gates_of(2, 3) + [(pre[0], VMEM), (y, VMEM)],
        [pltpu.VMEM((2 * tok, width), BF16), dma(2)],
        3 * rows * width * hidden // 4,
        2 * (rows * width + rows * hidden + width * hidden),
        {6: 1},
    )
    act, active, slope, x = call(
        pre_late_body,
        [flat, wide, wide, x_out],
        [(place, SMEM)] + anys(x_late) + [(a, VMEM) for a in (wg, wu, *pre, x)],
        [dma(2)],
        rows * width * hidden,
        rows * width + 4 * width * hidden + 3 * rows * hidden,
        {7 + i: i for i in range(4)},
    )
    piece = (2, half, share)
    send_a, send_b, y = call(
        down_send_body,
        [(piece, BF16, VMEM)] * 2 + [((rows, width), BF16, VMEM)],
        [(place, SMEM)] + anys(y_late) + gates_of(6, 7) + [(act, VMEM), (part, VMEM), (y, VMEM)],
        [pltpu.VMEM((2 * tok, width), BF16), dma(2)],
        rows * width * hidden // 4,
        2 * (rows * width + rows * hidden // 4 + width * hidden),
        {9: 2},
    )
    got_a, got_b = to_x(send_a), to_y(send_b)
    gate_delta, up_delta = call(
        back_body,
        [((rows, hidden), BF16, VMEM)] * 2,
        [(place, SMEM), (y, VMEM), (active, VMEM), (slope, VMEM)] + anys((wd0, da1, db1, da2, db2, da3, db3)),
        [pltpu.VMEM((4, hidden, share), BF16), dma(7)],
        2 * rows * width * hidden,
        2 * (rows * width + width * hidden) + 12 * rows * hidden,
    )
    gate_send, up_send = call(
        grad_send_body,
        [((2, share, hidden), BF16, VMEM)] * 2,
        [(place, SMEM), (x, VMEM), (gate_delta, VMEM), (up_delta, VMEM)],
        [],
        2 * rows * width * hidden,
        2 * (rows * width + 2 * rows * hidden + width * hidden),
    )
    gate_got, up_got = to_x(gate_send), to_y(up_send)
    pair_send, pair_keep = call(
        pair_body,
        [((rows // 2, width), BF16, VMEM)] * 2,
        [(gate_delta, VMEM), (up_delta, VMEM), (wg, VMEM), (wu, VMEM)],
        [],
        4 * rows * width * hidden,
        2 * (rows * width + 2 * rows * hidden + 2 * width * hidden),
    )
    total = add(pair_keep, swap(pair_send)).reshape(chips, tok, width)
    keep_a0, keep_a1, keep_b0, keep_b1 = call(
        down_keep_body,
        [((half, share), BF16, VMEM)] * 4,
        [(place, SMEM), (act, VMEM), (y, VMEM)],
        [],
        rows * width * hidden,
        2 * (rows * width + rows * hidden + width * hidden // 2),
    )
    gate0, gate1, up0, up1 = call(
        grad_keep_body,
        [((share, hidden), BF16, VMEM)] * 4,
        [(place, SMEM), (x, VMEM), (gate_delta, VMEM), (up_delta, VMEM)],
        [],
        2 * rows * width * hidden,
        2 * (rows * width + 2 * rows * hidden + width * hidden),
    )
    down_a, down_b = to_y(add(keep_a1, got_a[1])), to_x(add(keep_b1, got_b[1]))
    gate1, up1 = add(gate1, gate_got[1]), add(up1, up_got[1])
    sums = add(gate0, gate_got[0]), add(up0, up_got[0])
    gate_last, up_last = to_y(gate1), to_x(up1)
    gate_sum, up_sum = lax.optimization_barrier(sums)
    down_grad = jnp.concatenate([add(keep_a0, got_a[0], down_a), add(keep_b0, got_b[0], down_b)], axis=0)
    result = (1, share, hidden)
    gate_grad, up_grad = call(
        last_body,
        [(result, BF16, ANY)] * 2,
        [(a, VMEM) for a in (gate_sum, gate_last, up_sum, up_last)],
        [pltpu.VMEM(result, BF16)] * 2 + [dma(4)],
        share * hidden,
        12 * share * hidden,
    )

    far = hop(total[3], ((0, 1), (3, 2)))
    inner = hop(total[3], INNER)
    outer = hop(total[2], OUTER)
    two = hop(add(total[1], far), TWO)
    input_grad = add(total[0], inner, outer, two)
    return input_grad, gate_grad, up_grad, down_grad[None]


def routed(tokens, out_grad, routes, gate_values, w_gate, w_up, w_down):
    tok_rows, model_width = tokens.shape
    top_count = routes.shape[1]
    group_count = lax.axis_size("expert")
    local_count = w_gate.shape[0]
    expert_count = group_count * local_count
    hidden_units = w_gate.shape[2]
    capacity = slots_of(tok_rows, top_count, expert_count)
    pair_count = tok_rows * top_count
    slot_count = group_count * capacity
    expert_of = routes.reshape(-1)
    onehot = (expert_of[:, None] == jnp.arange(expert_count, dtype=jnp.int32)[None, :]).astype(
        jnp.int32
    )
    before = jnp.cumsum(onehot, axis=0) - onehot
    placed = jnp.sum(before * onehot, axis=1)
    slot_of = expert_of * capacity + placed
    slot_table = jnp.full((expert_count * capacity,), pair_count, jnp.int32)
    slot_table = slot_table.at[slot_of].set(jnp.arange(pair_count, dtype=jnp.int32))
    filled = slot_table < pair_count
    source = jnp.where(filled, slot_table, 0)
    owner_row = source // top_count
    send_x = jnp.where(filled[:, None], tokens[owner_row], jnp.zeros((), jnp.bfloat16))
    scaled = gate_values.reshape(-1)[source][:, None] * out_grad[owner_row].astype(jnp.float32)
    send_dy = jnp.where(filled[:, None], scaled, 0.0).astype(jnp.bfloat16)
    send_x = send_x.reshape(expert_count, capacity, model_width)
    send_dy = send_dy.reshape(expert_count, capacity, model_width)
    recv_x, recv_dy = (
        lax.all_to_all(send_x, "expert", split_axis=0, concat_axis=0, tiled=True),
        lax.all_to_all(send_dy, "expert", split_axis=0, concat_axis=0, tiled=True),
    )

    def to_local(stacked):
        shaped = stacked.reshape(group_count, local_count, capacity, model_width)
        return shaped.transpose(1, 0, 2, 3).reshape(local_count, slot_count, model_width)

    slot_x = to_local(recv_x)
    slot_dy = to_local(recv_dy)
    part_x = slot_x
    gate_term = jnp.einsum(
        "asd,adf->asf",
        part_x,
        lax.all_gather(w_gate, "dp", axis=1, tiled=True),
        preferred_element_type=jnp.float32,
    )
    up_term = jnp.einsum(
        "asd,adf->asf",
        part_x,
        lax.all_gather(w_up, "dp", axis=1, tiled=True),
        preferred_element_type=jnp.float32,
    )
    full_gate, full_up, full_down = (
        lax.all_gather(w_gate, "dp", axis=1, tiled=True),
        lax.all_gather(w_up, "dp", axis=1, tiled=True),
        lax.all_gather(w_down, "dp", axis=2, tiled=True),
    )
    sigma = jax.nn.sigmoid(gate_term)
    active = gate_term * sigma
    activated = (active * up_term).astype(jnp.bfloat16)
    back_hidden = jnp.einsum("asd,afd->asf", slot_dy, full_down, preferred_element_type=jnp.float32)
    up_delta = (back_hidden * active).astype(jnp.bfloat16)
    gate_delta = (back_hidden * up_term * sigma * (1.0 + gate_term * (1.0 - sigma))).astype(
        jnp.bfloat16
    )
    pair_grad = (
        jnp.einsum("asf,adf->asd", gate_delta, full_gate, preferred_element_type=jnp.float32)
        + jnp.einsum("asf,adf->asd", up_delta, full_up, preferred_element_type=jnp.float32)
    ).astype(jnp.bfloat16)
    send_back = pair_grad.reshape(local_count, group_count, capacity, model_width).transpose(
        1, 0, 2, 3
    )
    send_back = send_back.reshape(expert_count, capacity, model_width)
    returned = lax.all_to_all(send_back, "expert", split_axis=0, concat_axis=0, tiled=True)
    per_pair = returned.reshape(expert_count * capacity, model_width)[slot_of].astype(jnp.float32)
    input_grad = jnp.sum(per_pair.reshape(tok_rows, top_count, model_width), axis=1).astype(
        jnp.bfloat16
    )
    block_width = local_count * hidden_units
    share_width = model_width // lax.axis_size("dp")
    part_x = slot_x
    term_gate = jnp.einsum("asd,asf->daf", part_x, gate_delta, preferred_element_type=jnp.float32)
    term_up = jnp.einsum("asd,asf->daf", part_x, up_delta, preferred_element_type=jnp.float32)
    term_down = jnp.einsum("asd,asf->daf", slot_dy, activated, preferred_element_type=jnp.float32)
    shares = lax.psum_scatter(
        jnp.concatenate(
            [
                term_gate.reshape(lax.axis_size("dp") * share_width, block_width),
                term_up.reshape(lax.axis_size("dp") * share_width, block_width),
                term_down.reshape(lax.axis_size("dp") * share_width, block_width),
            ],
            axis=1,
        ).astype(jnp.bfloat16),
        "dp",
        scatter_dimension=0,
        tiled=True,
    ).astype(jnp.float32)
    share_rows = shares.shape[0]

    def unpack(which):
        return shares[:, which * block_width : (which + 1) * block_width].reshape(
            share_rows, local_count, hidden_units
        )

    gate_grad = unpack(0).transpose(1, 0, 2).astype(jnp.bfloat16)
    up_grad = unpack(1).transpose(1, 0, 2).astype(jnp.bfloat16)
    down_grad = unpack(2).transpose(1, 2, 0).astype(jnp.bfloat16)
    return (input_grad, gate_grad, up_grad, down_grad)


def lined(dp, expert):
    return dp == 4 and expert == 8


def local(tokens, out_grad, routes, gate_values, w_gate, w_up, w_down):
    experts = lax.axis_size("expert") * w_gate.shape[0]
    capacity = slots_of(tokens.shape[0], routes.shape[1], experts)
    fits = w_gate.shape[0] == 1 and tokens.shape[0] <= 2 * capacity
    if not (fits and lined(lax.axis_size("dp"), lax.axis_size("expert"))):
        return routed(tokens, out_grad, routes, gate_values, w_gate, w_up, w_down)
    return dense(tokens, out_grad, routes, gate_values, w_gate, w_up, w_down)


def solution(mesh):
    return jax.shard_map(
        local,
        mesh=mesh,
        in_specs=(
            P(("dp", "expert"), None),
            P(("dp", "expert"), None),
            P(("dp", "expert"), None),
            P(("dp", "expert"), None),
            P("expert", "dp", None),
            P("expert", "dp", None),
            P("expert", None, "dp"),
        ),
        out_specs=(
            P(("dp", "expert"), None),
            P("expert", "dp", None),
            P("expert", "dp", None),
            P("expert", None, "dp"),
        ),
        check_vma=False,
    )
```

```python
import jax
import jax.numpy as jnp
from jax import lax
from jax.experimental import pallas as pl
from jax.experimental.pallas import tpu as pltpu
from jax.sharding import PartitionSpec as P


F32 = jnp.float32
BF16 = jnp.bfloat16
ANY = pl.BlockSpec(memory_space=pl.ANY)
VMEM = pl.BlockSpec(memory_space=pltpu.VMEM)
SMEM = pl.BlockSpec(memory_space=pltpu.SMEM)
LIMIT = 12 * 1024 * 1024
NN = (((1,), (0,)), ((), ()))
NT = (((1,), (1,)), ((), ()))


def mm(a, b, dims):
    return lax.dot_general(a, b, dims, preferred_element_type=F32)


def slots_of(tok_rows, top_count, expert_count):
    return min(tok_rows, max(2, 9 * tok_rows * top_count // (8 * expert_count)))


def call(body, outs, ins, scratch, flops, moved, aliases=None):
    return pl.pallas_call(
        body,
        input_output_aliases=aliases or {},
        out_shape=[jax.ShapeDtypeStruct(s, d) for s, d, _ in outs],
        in_specs=[s for _, s in ins],
        out_specs=[s for _, _, s in outs],
        scratch_shapes=scratch,
        compiler_params=pltpu.CompilerParams(vmem_limit_bytes=LIMIT),
        cost_estimate=pl.CostEstimate(flops=flops, bytes_accessed=moved, transcendentals=0),
    )(*[a for a, _ in ins])


TWO = ((0, 2), (1, 3), (2, 0), (3, 1))
OUTER = ((0, 1), (1, 0), (2, 3), (3, 2))
INNER = ((1, 2), (2, 1))


def prep_body(place, routes, gates, *outs):
    for k, out in enumerate(outs):
        value = jnp.zeros(out.shape, F32)
        for i in range(routes.shape[0]):
            value += jnp.where(routes[i : i + 1, :] == (place[2] ^ k), gates[i : i + 1, :], 0.0)
        out[...] = value


class Copies:
    def __init__(self, sems):
        self.sems, self.used = sems, 0

    def start(self, src, dst):
        copy = pltpu.make_async_copy(src, dst, self.sems.at[self.used])
        self.used += 1
        copy.start()
        return copy

    def pick(self, first, src, other, dst):
        sem = self.sems.at[self.used]
        self.used += 1

        @pl.when(first)
        def _():
            pltpu.make_async_copy(src, dst, sem).start()

        @pl.when(jnp.logical_not(first))
        def _():
            pltpu.make_async_copy(other, dst, sem).start()

        return pltpu.make_async_copy(other, dst, sem)


def load_early(copies, pieces, dst, first=0):
    tok = pieces[0].shape[0]
    return [copies.start(src, dst.at[pl.ds((first + i) * tok, tok)]) for i, src in enumerate(pieces)]


def load_weights(copies, place, which, pieces, wg, wu):
    share = pieces[0].shape[0]
    started = []
    for i, k in enumerate(which):
        at = pl.ds((place[0] ^ k) * share, share)
        started += [copies.start(pieces[2 * i], wg.at[at]), copies.start(pieces[2 * i + 1], wu.at[at])]
    return started


def own_body(place, tokens, w_gate, w_up, x, wg, wu, sems):
    copies = Copies(sems)
    started = load_early(copies, (tokens,), x) + load_weights(copies, place, (0,), (w_gate, w_up), wg, wu)
    for c in started:
        c.wait()


def near_body(place, *refs):
    pieces, weights = refs[:5], refs[5:9]
    x, wg, wu, sems = refs[12:]
    copies = Copies(sems)
    for c in load_early(copies, pieces, x, 1) + load_weights(copies, place, (1, 2), weights, wg, wu):
        c.wait()


def load_late(copies, chip, pieces, dst):
    tok = pieces[0].shape[0]
    middle = jnp.logical_or(chip == 1, chip == 2)
    return [
        copies.pick(middle, pieces[2 * core], pieces[2 * core + 1], dst.at[pl.ds(core * tok, tok)]) for core in (0, 1)
    ]


def pre_blocks(x, first, count, wg, wu, act, active_out, slope_out):
    tn = 256

    def step(i, _):
        r = slice(first, first + count)
        c = pl.ds(pl.multiple_of(i * tn, tn), tn)
        lhs = x[r, :]
        gate = mm(lhs, wg[:, c], NN)
        up = mm(lhs, wu[:, c], NN)
        activate(gate, up, r, c, act, active_out, slope_out)
        return 0

    lax.fori_loop(0, wg.shape[1] // tn, step, 0)


def activate(gate, up, r, c, act, active_out, slope_out):
    sigma = jax.nn.sigmoid(gate)
    active = gate * sigma
    act[r, c] = (active * up).astype(BF16)
    active_out[r, c] = active
    slope_out[r, c] = up * sigma * (1.0 + gate * (1.0 - sigma))


def pre_part_body(place, x, wg, wu, gate_part, up_part):
    tn, share = 256, wg.shape[0] // 4
    r = slice(0, x.shape[0] // 4 * 3)

    def step(i, _):
        c = pl.ds(pl.multiple_of(i * tn, tn), tn)
        gate = up = None
        for k in range(3):
            block = pl.ds(pl.multiple_of((place[0] ^ k) * share, share), share)
            lhs = x[r, block]
            more = mm(lhs, wg[block, c], NN), mm(lhs, wu[block, c], NN)
            gate, up = more if gate is None else (gate + more[0], up + more[1])
        gate_part[r, c] = gate
        up_part[r, c] = up
        return 0

    lax.fori_loop(0, wg.shape[1] // tn, step, 0)


def pre_early_body(place, *refs):
    x, gate_part, up_part = refs[2:5]
    act, active, slope, wg, wu, sems = refs[7:]
    for c in load_weights(Copies(sems), place, (3,), refs[:2], wg, wu):
        c.wait()
    tn, share = 256, wg.shape[0] // 4
    r = slice(0, x.shape[0] // 4 * 3)
    block = pl.ds(pl.multiple_of((place[0] ^ 3) * share, share), share)

    def step(i, _):
        c = pl.ds(pl.multiple_of(i * tn, tn), tn)
        lhs = x[r, block]
        gate = gate_part[r, c] + mm(lhs, wg[block, c], NN)
        up = up_part[r, c] + mm(lhs, wu[block, c], NN)
        activate(gate, up, r, c, act, active, slope)
        return 0

    lax.fori_loop(0, wg.shape[1] // tn, step, 0)


def pre_late_body(place, *refs):
    pieces, wg, wu = refs[:4], refs[4], refs[5]
    act, active, slope, x, sems = refs[10:]
    count = x.shape[0] // 4
    for c in load_late(Copies(sems), place[1], pieces, x.at[pl.ds(3 * count, count)]):
        c.wait()
    pre_blocks(x, 3 * count, count, wg, wu, act, active, slope)


def scale(gate, raw, y, row):
    tok = raw.shape[0]
    column = jnp.transpose(jnp.broadcast_to(gate[...], (tok, tok)))[:, :1]
    y[row : row + tok, :] = (raw[...].astype(F32) * column).astype(BF16)


def load_scaled(copies, pieces, gates, raw, y, blocks):
    tok = pieces[0].shape[0]
    at = [raw.at[pl.ds(i * tok, tok)] for i in range(len(pieces))]
    started = [copies.start(src, dst) for src, dst in zip(pieces, at)]
    for copy, gate, dst, block in zip(started, gates, at, blocks):
        copy.wait()
        scale(gate, dst, y, block * tok)


def scale_early_body(*refs):
    y, raw, sems = refs[8:]
    load_scaled(Copies(sems), refs[:4], refs[4:8], raw, y, (0, 1, 3, 4))


def down_blocks(place, act, y, first, count, wanted, put):
    share = y.shape[1] // 4
    half = act.shape[1] // 2
    rows = slice(first, first + count)
    for h in (0, 1):
        turned = jnp.transpose(act[rows, h * half : (h + 1) * half])
        for which, k, target in wanted:
            if which == h:
                cols = pl.ds(pl.multiple_of((place[0] ^ k) * share, share), share)
                put(target, mm(turned, y[rows, cols], NN))


def down_early_body(place, *refs):
    pieces, gates, act = refs[:2], refs[2:4], refs[4]
    part, y, raw, sems = refs[6:]
    load_scaled(Copies(sems), pieces, gates, raw, y, (2, 5))

    def put(target, value):
        part[target] = value

    early = y.shape[0] // 4 * 3
    down_blocks(place, act, y, 0, early, ((0, 1, 0), (0, 3, 1), (1, 2, 2), (1, 3, 3)), put)


def down_send_body(place, *refs):
    pieces, gates, act, part = refs[:4], refs[4:6], refs[6], refs[7]
    send_a, send_b, y, raw, sems = refs[9:]
    for c in load_late(Copies(sems), place[1], pieces, raw):
        c.wait()
    count = raw.shape[0]
    first = y.shape[0] - count
    for core in (0, 1):
        tok = count // 2
        scale(gates[core], raw.at[pl.ds(core * tok, tok)], y, first + core * tok)

    def put(target, value):
        dst = (send_a, send_b)[target // 2]
        dst[target % 2] = (part[target] + value).astype(BF16)

    down_blocks(place, act, y, first, count, ((0, 1, 0), (0, 3, 1), (1, 2, 2), (1, 3, 3)), put)


def down_keep_body(place, act, y, a0, a1, b0, b1):
    def put(target, value):
        target[...] = value.astype(BF16)

    down_blocks(place, act, y, 0, y.shape[0], ((0, 0, a0), (0, 2, a1), (1, 0, b0), (1, 1, b1)), put)


def last_body(gate_sum, gate_last, up_sum, up_last, gate_out, up_out, gate, up, sems):
    copies = Copies(sems)
    part = gate.shape[1] // 8
    started = []
    for total, last, held, out in ((gate_sum, gate_last, gate, gate_out), (up_sum, up_last, up, up_out)):
        for i in range(8):
            r = slice(i * part, (i + 1) * part)
            held[0, r, :] = (total[r, :].astype(F32) + last[r, :].astype(F32)).astype(BF16)
            at = pl.ds(i * part, part)
            started.append(copies.start(held.at[0, at], out.at[0, at]))
    for c in started:
        c.wait()


def back_body(place, y, active, slope, *refs):
    own, halves = refs[0], refs[1:7]
    gate_delta, up_delta, w, sems = refs[7:]
    me = place[0]
    copies = Copies(sems)
    hidden, share = own.shape
    half = hidden // 2
    started = [copies.start(own, w.at[me])]
    for i, src in enumerate(halves):
        started.append(copies.start(src, w.at[me ^ (1 + i // 2), pl.ds(i % 2 * half, half)]))
    for c in started:
        c.wait()
    rows = y.shape[0]
    tm, tn = rows // 2, 256

    def step(i, _):
        r = pl.ds(pl.multiple_of(i // (hidden // tn) * tm, tm), tm)
        c = pl.ds(pl.multiple_of(i % (hidden // tn) * tn, tn), tn)
        back = mm(y[r, 0:share], w[0, c, :], NT)
        for j in range(1, 4):
            back += mm(y[r, j * share : (j + 1) * share], w[j, c, :], NT)
        up_delta[r, c] = (back * active[r, c]).astype(BF16)
        gate_delta[r, c] = (back * slope[r, c]).astype(BF16)
        return 0

    lax.fori_loop(0, 2 * (hidden // tn), step, 0)


def grad_blocks(place, x, wanted):
    share = x.shape[1] // 4
    tm = share // 2
    for k, targets in wanted:

        def step(i, _, k=k, targets=targets):
            cols = pl.ds(pl.multiple_of((place[0] ^ k) * share + i * tm, tm), tm)
            turned = jnp.transpose(x[:, cols])
            part = pl.ds(pl.multiple_of(i * tm, tm), tm)
            for delta, dst, slot in targets:
                value = mm(turned, delta[...], NN).astype(BF16)
                if slot is None:
                    dst[part, :] = value
                else:
                    dst[slot, part, :] = value
            return 0

        lax.fori_loop(0, 2, step, 0)


def grad_send_body(place, x, gd, ud, gate_send, up_send):
    grad_blocks(
        place, x, ((1, [(gd, gate_send, 0)]), (3, [(gd, gate_send, 1), (ud, up_send, 1)]), (2, [(ud, up_send, 0)]))
    )


def grad_keep_body(place, x, gd, ud, g0, g1, u0, u1):
    grad_blocks(place, x, ((2, [(gd, g1, None)]), (1, [(ud, u1, None)]), (0, [(gd, g0, None), (ud, u0, None)])))


def pair_body(gate_delta, up_delta, wg, wu, send, keep):
    tn = 256
    part = keep.shape[0] // 4

    def step(i, _):
        c = pl.ds(pl.multiple_of(i * tn, tn), tn)
        total = (mm(gate_delta[...], wg[c, :], NT) + mm(up_delta[...], wu[c, :], NT)).astype(BF16)
        keep[: 3 * part, c] = total[: 3 * part]
        send[: 3 * part, c] = total[3 * part : 6 * part]
        keep[3 * part :, c] = total[6 * part : 7 * part]
        send[3 * part :, c] = total[7 * part :]
        return 0

    lax.fori_loop(0, wg.shape[0] // tn, step, 0)


def add(*terms):
    total = terms[0].astype(F32)
    for term in terms[1:]:
        total = total + term.astype(F32)
    return total.astype(BF16)


def dense(tokens, out_grad, routes, gate_values, w_gate, w_up, w_down):
    tok, width = tokens.shape
    experts = lax.axis_size("expert")
    chips = experts // 2
    hidden = w_gate.shape[2]
    share = width // 4
    half = hidden // 2
    rows = experts * tok
    expert = lax.axis_index("expert")
    chip = expert // 2
    place = jnp.stack([lax.axis_index("dp"), chip, expert]).astype(jnp.int32)

    def to_x(block):
        return lax.ppermute(block, "dp", [(i, i ^ 1) for i in range(4)])

    def to_y(block):
        return lax.ppermute(block, "dp", [(i, i ^ 2) for i in range(4)])

    def hop(block, moves):
        return lax.ppermute(block, "expert", [(2 * a + c, 2 * b + c) for a, b in moves for c in (0, 1)])

    def swap(block, at=range(chips)):
        return lax.ppermute(block, "expert", [(2 * z + c, 2 * z + 1 - c) for z in at for c in (0, 1)])

    def line(own):
        two = hop(own, TWO)
        outer = hop(own, OUTER)
        inner = hop(own, INNER)
        far = hop(two, ((2, 3), (1, 0)))
        early = [own, two, outer, swap(own), swap(two), swap(outer)]
        late = [inner, far, swap(inner, (1, 2)), swap(far, (0, 3))]
        return early, late

    x_early, x_late = line(tokens)
    gates = list(call(
        prep_body,
        [((1, tok), F32, VMEM)] * experts,
        [(place, SMEM), (routes.T, VMEM), (gate_values.T, VMEM)],
        [],
        1000,
        1000,
    ))
    for k in range(1, experts):
        gates[k] = lax.ppermute(gates[k], "expert", [(e, e ^ k) for e in range(experts)])

    def gates_of(*distances):
        return [(gates[k], VMEM) for k in distances]

    y_early, y_late = line(out_grad)

    wg0, wu0, wd0 = w_gate[0], w_up[0], w_down[0]
    wg1, wu2 = to_x(wg0), to_y(wu0)
    wg2, wu1 = to_y(wg0), to_x(wu0)
    wg3, wu3 = to_y(wg1), to_x(wu2)
    da0, db0 = wd0[:half], wd0[half:]
    da1, db2 = to_x(da0), to_y(db0)
    da2, db1 = to_y(da0), to_x(db0)
    da3, db3 = to_y(da1), to_x(db2)

    def dma(n):
        return pltpu.SemaphoreType.DMA((n,))

    def anys(arrays):
        return [(a, ANY) for a in arrays]

    x_out = ((rows, width), BF16, VMEM)
    weight = ((width, hidden), BF16, VMEM)
    flat = ((rows, hidden), BF16, VMEM)
    wide = ((rows, hidden), F32, VMEM)
    x, wg, wu = call(
        own_body,
        [x_out, weight, weight],
        [(place, SMEM)] + anys((tokens, wg0, wu0)),
        [dma(3)],
        1000,
        width * (2 * tok + hidden),
    )
    x, wg, wu = call(
        near_body,
        [x_out, weight, weight],
        [(place, SMEM)] + anys(x_early[1:]) + anys((wg1, wu1, wg2, wu2)) + [(x, VMEM), (wg, VMEM), (wu, VMEM)],
        [dma(9)],
        1000,
        width * (10 * tok + 2 * hidden),
        {10: 0, 11: 1, 12: 2},
    )
    parts = call(
        pre_part_body,
        [wide, wide],
        [(place, SMEM), (x, VMEM), (wg, VMEM), (wu, VMEM)],
        [],
        9 * rows * width * hidden // 4,
        3 * rows * width + 6 * width * hidden + 6 * rows * hidden,
    )
    *pre, wg, wu = call(
        pre_early_body,
        [flat, wide, wide, weight, weight],
        [(place, SMEM)] + anys((wg3, wu3)) + [(a, VMEM) for a in (x, *parts, wg, wu)],
        [dma(2)],
        3 * rows * width * hidden // 4,
        rows * width + 2 * width * hidden + 16 * rows * hidden,
        {4: 1, 5: 2, 6: 3, 7: 4},
    )
    y_rows = ((rows, width), BF16, VMEM)
    (y,) = call(
        scale_early_body,
        [y_rows],
        anys((y_early[0], y_early[1], y_early[3], y_early[4])) + gates_of(0, 4, 1, 5),
        [pltpu.VMEM((4 * tok, width), BF16), dma(4)],
        rows * width,
        3 * rows * width,
    )
    part, y = call(
        down_early_body,
        [((4, half, share), F32, VMEM), y_rows],
        [(place, SMEM)] + anys((y_early[2], y_early[5])) + gates_of(2, 3) + [(pre[0], VMEM), (y, VMEM)],
        [pltpu.VMEM((2 * tok, width), BF16), dma(2)],
        3 * rows * width * hidden // 4,
        2 * (rows * width + rows * hidden + width * hidden),
        {6: 1},
    )
    act, active, slope, x = call(
        pre_late_body,
        [flat, wide, wide, x_out],
        [(place, SMEM)] + anys(x_late) + [(a, VMEM) for a in (wg, wu, *pre, x)],
        [dma(2)],
        rows * width * hidden,
        rows * width + 4 * width * hidden + 3 * rows * hidden,
        {7 + i: i for i in range(4)},
    )
    piece = (2, half, share)
    send_a, send_b, y = call(
        down_send_body,
        [(piece, BF16, VMEM)] * 2 + [((rows, width), BF16, VMEM)],
        [(place, SMEM)] + anys(y_late) + gates_of(6, 7) + [(act, VMEM), (part, VMEM), (y, VMEM)],
        [pltpu.VMEM((2 * tok, width), BF16), dma(2)],
        rows * width * hidden // 4,
        2 * (rows * width + rows * hidden // 4 + width * hidden),
        {9: 2},
    )
    got_a, got_b = to_x(send_a), to_y(send_b)
    gate_delta, up_delta = call(
        back_body,
        [((rows, hidden), BF16, VMEM)] * 2,
        [(place, SMEM), (y, VMEM), (active, VMEM), (slope, VMEM)] + anys((wd0, da1, db1, da2, db2, da3, db3)),
        [pltpu.VMEM((4, hidden, share), BF16), dma(7)],
        2 * rows * width * hidden,
        2 * (rows * width + width * hidden) + 12 * rows * hidden,
    )
    gate_send, up_send = call(
        grad_send_body,
        [((2, share, hidden), BF16, VMEM)] * 2,
        [(place, SMEM), (x, VMEM), (gate_delta, VMEM), (up_delta, VMEM)],
        [],
        2 * rows * width * hidden,
        2 * (rows * width + 2 * rows * hidden + width * hidden),
    )
    gate_got, up_got = to_x(gate_send), to_y(up_send)
    pair_send, pair_keep = call(
        pair_body,
        [((rows // 2, width), BF16, VMEM)] * 2,
        [(gate_delta, VMEM), (up_delta, VMEM), (wg, VMEM), (wu, VMEM)],
        [],
        4 * rows * width * hidden,
        2 * (rows * width + 2 * rows * hidden + 2 * width * hidden),
    )
    total = add(pair_keep, swap(pair_send)).reshape(chips, tok, width)
    keep_a0, keep_a1, keep_b0, keep_b1 = call(
        down_keep_body,
        [((half, share), BF16, VMEM)] * 4,
        [(place, SMEM), (act, VMEM), (y, VMEM)],
        [],
        rows * width * hidden,
        2 * (rows * width + rows * hidden + width * hidden // 2),
    )
    gate0, gate1, up0, up1 = call(
        grad_keep_body,
        [((share, hidden), BF16, VMEM)] * 4,
        [(place, SMEM), (x, VMEM), (gate_delta, VMEM), (up_delta, VMEM)],
        [],
        2 * rows * width * hidden,
        2 * (rows * width + 2 * rows * hidden + width * hidden),
    )
    down_a, down_b = to_y(add(keep_a1, got_a[1])), to_x(add(keep_b1, got_b[1]))
    gate1, up1 = add(gate1, gate_got[1]), add(up1, up_got[1])
    sums = add(gate0, gate_got[0]), add(up0, up_got[0])
    gate_last, up_last = to_y(gate1), to_x(up1)
    gate_sum, up_sum = lax.optimization_barrier(sums)
    down_grad = jnp.concatenate([add(keep_a0, got_a[0], down_a), add(keep_b0, got_b[0], down_b)], axis=0)
    result = (1, share, hidden)
    gate_grad, up_grad = call(
        last_body,
        [(result, BF16, ANY)] * 2,
        [(a, VMEM) for a in (gate_sum, gate_last, up_sum, up_last)],
        [pltpu.VMEM(result, BF16)] * 2 + [dma(16)],
        share * hidden,
        12 * share * hidden,
    )

    far = hop(total[3], ((0, 1), (3, 2)))
    inner = hop(total[3], INNER)
    outer = hop(total[2], OUTER)
    two = hop(add(total[1], far), TWO)
    input_grad = add(total[0], inner, outer, two)
    return input_grad, gate_grad, up_grad, down_grad[None]


def routed(tokens, out_grad, routes, gate_values, w_gate, w_up, w_down):
    tok_rows, model_width = tokens.shape
    top_count = routes.shape[1]
    group_count = lax.axis_size("expert")
    local_count = w_gate.shape[0]
    expert_count = group_count * local_count
    hidden_units = w_gate.shape[2]
    capacity = slots_of(tok_rows, top_count, expert_count)
    pair_count = tok_rows * top_count
    slot_count = group_count * capacity
    expert_of = routes.reshape(-1)
    onehot = (expert_of[:, None] == jnp.arange(expert_count, dtype=jnp.int32)[None, :]).astype(
        jnp.int32
    )
    before = jnp.cumsum(onehot, axis=0) - onehot
    placed = jnp.sum(before * onehot, axis=1)
    slot_of = expert_of * capacity + placed
    slot_table = jnp.full((expert_count * capacity,), pair_count, jnp.int32)
    slot_table = slot_table.at[slot_of].set(jnp.arange(pair_count, dtype=jnp.int32))
    filled = slot_table < pair_count
    source = jnp.where(filled, slot_table, 0)
    owner_row = source // top_count
    send_x = jnp.where(filled[:, None], tokens[owner_row], jnp.zeros((), jnp.bfloat16))
    scaled = gate_values.reshape(-1)[source][:, None] * out_grad[owner_row].astype(jnp.float32)
    send_dy = jnp.where(filled[:, None], scaled, 0.0).astype(jnp.bfloat16)
    send_x = send_x.reshape(expert_count, capacity, model_width)
    send_dy = send_dy.reshape(expert_count, capacity, model_width)
    recv_x, recv_dy = (
        lax.all_to_all(send_x, "expert", split_axis=0, concat_axis=0, tiled=True),
        lax.all_to_all(send_dy, "expert", split_axis=0, concat_axis=0, tiled=True),
    )

    def to_local(stacked):
        shaped = stacked.reshape(group_count, local_count, capacity, model_width)
        return shaped.transpose(1, 0, 2, 3).reshape(local_count, slot_count, model_width)

    slot_x = to_local(recv_x)
    slot_dy = to_local(recv_dy)
    part_x = slot_x
    gate_term = jnp.einsum(
        "asd,adf->asf",
        part_x,
        lax.all_gather(w_gate, "dp", axis=1, tiled=True),
        preferred_element_type=jnp.float32,
    )
    up_term = jnp.einsum(
        "asd,adf->asf",
        part_x,
        lax.all_gather(w_up, "dp", axis=1, tiled=True),
        preferred_element_type=jnp.float32,
    )
    full_gate, full_up, full_down = (
        lax.all_gather(w_gate, "dp", axis=1, tiled=True),
        lax.all_gather(w_up, "dp", axis=1, tiled=True),
        lax.all_gather(w_down, "dp", axis=2, tiled=True),
    )
    sigma = jax.nn.sigmoid(gate_term)
    active = gate_term * sigma
    activated = (active * up_term).astype(jnp.bfloat16)
    back_hidden = jnp.einsum("asd,afd->asf", slot_dy, full_down, preferred_element_type=jnp.float32)
    up_delta = (back_hidden * active).astype(jnp.bfloat16)
    gate_delta = (back_hidden * up_term * sigma * (1.0 + gate_term * (1.0 - sigma))).astype(
        jnp.bfloat16
    )
    pair_grad = (
        jnp.einsum("asf,adf->asd", gate_delta, full_gate, preferred_element_type=jnp.float32)
        + jnp.einsum("asf,adf->asd", up_delta, full_up, preferred_element_type=jnp.float32)
    ).astype(jnp.bfloat16)
    send_back = pair_grad.reshape(local_count, group_count, capacity, model_width).transpose(
        1, 0, 2, 3
    )
    send_back = send_back.reshape(expert_count, capacity, model_width)
    returned = lax.all_to_all(send_back, "expert", split_axis=0, concat_axis=0, tiled=True)
    per_pair = returned.reshape(expert_count * capacity, model_width)[slot_of].astype(jnp.float32)
    input_grad = jnp.sum(per_pair.reshape(tok_rows, top_count, model_width), axis=1).astype(
        jnp.bfloat16
    )
    block_width = local_count * hidden_units
    share_width = model_width // lax.axis_size("dp")
    part_x = slot_x
    term_gate = jnp.einsum("asd,asf->daf", part_x, gate_delta, preferred_element_type=jnp.float32)
    term_up = jnp.einsum("asd,asf->daf", part_x, up_delta, preferred_element_type=jnp.float32)
    term_down = jnp.einsum("asd,asf->daf", slot_dy, activated, preferred_element_type=jnp.float32)
    shares = lax.psum_scatter(
        jnp.concatenate(
            [
                term_gate.reshape(lax.axis_size("dp") * share_width, block_width),
                term_up.reshape(lax.axis_size("dp") * share_width, block_width),
                term_down.reshape(lax.axis_size("dp") * share_width, block_width),
            ],
            axis=1,
        ).astype(jnp.bfloat16),
        "dp",
        scatter_dimension=0,
        tiled=True,
    ).astype(jnp.float32)
    share_rows = shares.shape[0]

    def unpack(which):
        return shares[:, which * block_width : (which + 1) * block_width].reshape(
            share_rows, local_count, hidden_units
        )

    gate_grad = unpack(0).transpose(1, 0, 2).astype(jnp.bfloat16)
    up_grad = unpack(1).transpose(1, 0, 2).astype(jnp.bfloat16)
    down_grad = unpack(2).transpose(1, 2, 0).astype(jnp.bfloat16)
    return (input_grad, gate_grad, up_grad, down_grad)


def lined(dp, expert):
    return dp == 4 and expert == 8


def local(tokens, out_grad, routes, gate_values, w_gate, w_up, w_down):
    experts = lax.axis_size("expert") * w_gate.shape[0]
    capacity = slots_of(tokens.shape[0], routes.shape[1], experts)
    fits = w_gate.shape[0] == 1 and tokens.shape[0] <= 2 * capacity
    if not (fits and lined(lax.axis_size("dp"), lax.axis_size("expert"))):
        return routed(tokens, out_grad, routes, gate_values, w_gate, w_up, w_down)
    return dense(tokens, out_grad, routes, gate_values, w_gate, w_up, w_down)


def solution(mesh):
    return jax.shard_map(
        local,
        mesh=mesh,
        in_specs=(
            P(("dp", "expert"), None),
            P(("dp", "expert"), None),
            P(("dp", "expert"), None),
            P(("dp", "expert"), None),
            P("expert", "dp", None),
            P("expert", "dp", None),
            P("expert", None, "dp"),
        ),
        out_specs=(
            P(("dp", "expert"), None),
            P("expert", "dp", None),
            P("expert", "dp", None),
            P("expert", None, "dp"),
        ),
        check_vma=False,
    )
```
